128 devices in a mesh: grp: 8 (over x, y_lo), blk: 16 (over z, y_hi, core).
Axes of the slice: x: 4, y: 4 (y_hi: 2, y_lo: 2; y = y_hi * 2 + y_lo), z: 4, core: 2. Of those that a mesh axis runs over, the one named last changes fastest.
Arguments:
- source_emb: bfloat16 [24576, 768], P('blk'), may hold values from -32 to 32
- target_emb: bfloat16 [24576, 768], P(('grp', 'blk')), may hold values from -16 to 16
- hard_pool: bfloat16 [24576, 768], P(('grp', 'blk')), may hold values from -16 to 16
- hard_index: int32 [24576], P('blk'), may hold values from 0 to 24575, as said below
- language: int32 [24576], P('blk'), may hold values from 0 to 108
- margin: float32 [109], replicated, may hold values from 0.5 to 3
Outputs:
- row_loss: float32 [24576], P('blk')
- source_grad: float32 [24576, 768], P('blk')
- target_grad: float32 [24576, 768], P(('grp', 'blk'))
- pool_grad: float32 [24576, 768], P(('grp', 'blk'))
The draws below stay inside these ranges and needn't reach their ends.
Inputs may be any that keep to these rules, and one draw needn't show every extreme that they name: `hard_index`: each entry is a row of hard_pool; an entry's owner is its value // 192. Within each aligned block of 192 entries no owner is named more than 3 times, and one owner, the same for all blocks, is named exactly 3 times in every block.
All inputs are finite; a program needn't handle non-finite values.
Results may differ from the reference program's by a relative error of at most 0.0025.
Values may be sent and summed in bfloat16 or wider, within the bound.
No kernel may reach another device: no remote copies, remote signals or barrier semaphores. Data moves between devices by JAX's collectives and lax.ppermute only.
A program may use at most 64 MiB of HBM per device.

```python
import math
import jax
import jax.numpy as jnp
import numpy as np
from jax import lax

D = 768
LANGS = 109
TGT_DEV = 192
OWNERS = 128
HN_CAP = 3
SRC_DEV = 1536
N = 24576


def clipped_normal(key, shape):
    return jnp.clip(jax.random.normal(key, shape, jnp.float32), -6.0, 6.0)


def entries(key, shape):
    return clipped_normal(key, shape)


def spread(key, low, high):
    return jnp.exp(jax.random.uniform(key, (N, 1), jnp.float32, math.log(low), math.log(high)))


def target_values(key):
    base = entries(jax.random.fold_in(key, 11), (N, D))
    scale_t = spread(jax.random.fold_in(key, 13), 0.5, 2.0)
    values = base * scale_t
    return values


def pool_values(key):
    base = entries(jax.random.fold_in(key, 31), (N, D))
    return base * spread(jax.random.fold_in(key, 33), 0.5, 2.0)


def hard_ids(key):
    special = jax.random.randint(jax.random.fold_in(key, 52), (), 1, OWNERS - 1, jnp.int32)
    slot_total = OWNERS * HN_CAP
    slot_ids = jnp.arange(slot_total, dtype=jnp.int32)
    slot_owner = slot_ids // HN_CAP

    def one_block(block_key, block_at):
        order_key, place_key, row_key = jax.random.split(block_key, 3)
        priority = jax.random.permutation(order_key, slot_total).astype(jnp.int32)
        priority = jnp.where(slot_owner == special, priority + slot_total, priority)
        first = block_at == 0
        priority = jnp.where(first & (slot_ids == 0), -2, priority)
        priority = jnp.where(first & (slot_ids == (OWNERS - 1) * HN_CAP), -1, priority)
        taken = jnp.argsort(priority, stable=True)[:TGT_DEV - HN_CAP]
        owners = jnp.concatenate([jnp.full((HN_CAP,), special, jnp.int32), slot_owner[taken]])
        places = jax.random.permutation(place_key, TGT_DEV).astype(jnp.int32)
        owner_of = owners[places]
        row_of = jax.random.randint(row_key, (TGT_DEV,), 0, TGT_DEV, jnp.int32)
        row_of = jnp.where(first & (owner_of == 0), 0, jnp.where(first & (owner_of == OWNERS - 1), TGT_DEV - 1, row_of))
        return (owner_of * TGT_DEV + row_of).astype(jnp.int32)
    block_keys = jax.random.split(jax.random.fold_in(key, 51), OWNERS)
    return jax.vmap(one_block)(block_keys, jnp.arange(OWNERS, dtype=jnp.int32)).reshape(N)


def draw_target_emb(key, part):
    return target_values(key).astype(jnp.bfloat16)


def draw_hard_pool(key, part):
    return pool_values(key).astype(jnp.bfloat16)


def draw_hard_index(key, part):
    return hard_ids(key)


def draw_source_emb(key, part):
    targets = target_values(key)
    pooled = pool_values(key)
    chosen = hard_ids(key)
    noise = entries(jax.random.fold_in(key, 41), (N, D))
    row_scale = spread(jax.random.fold_in(key, 42), 0.3, 3.0)
    values = row_scale * (6.0 / D) * (targets + pooled[chosen] + noise)
    return values.astype(jnp.bfloat16)


def with_ends(drawn, own_key, low, top_value):
    place = [jax.random.randint(jax.random.fold_in(own_key, axis), (), 0, length) for axis, length in enumerate(drawn.shape)]
    longest = drawn.shape.index(max(drawn.shape))
    neighbour = place[:longest] + [(place[longest] + 1) % drawn.shape[longest]] + place[longest + 1:]
    return drawn.at[tuple(place)].set(low).at[tuple(neighbour)].set(top_value)


def rank_bounds(number_of, skew):
    weights = [(1 << 20) // math.isqrt(grade ** skew) + 1 for grade in range(1, number_of + 1)]
    scale = 1 + sum(weights) // (1 << 30)
    return np.cumsum(np.array([max(1, weight // scale) for weight in weights]))


def skewed_ids(stream_key, dims, number_of, skew):
    grid = rank_bounds(number_of, skew)
    ticket = jax.random.randint(jax.random.fold_in(stream_key, 1), dims, 0, int(grid[number_of - 1]))
    grade = jnp.searchsorted(jnp.asarray(grid, jnp.int32), ticket, side="right")
    return jax.random.permutation(jax.random.fold_in(stream_key, 2), number_of)[grade].astype(jnp.int32)


def setup_inputs(seed: int = 0) -> dict:
    seeds = jax.random.split(jax.random.key(seed), 7)
    return {
        "source_emb": draw_source_emb(jax.random.fold_in(seeds[6], 71), 0),
        "target_emb": draw_target_emb(jax.random.fold_in(seeds[6], 71), 0),
        "hard_pool": draw_hard_pool(jax.random.fold_in(seeds[6], 71), 0),
        "hard_index": draw_hard_index(jax.random.fold_in(seeds[6], 71), 0),
        "language": with_ends(skewed_ids(seeds[4], (N,), LANGS, 2), jax.random.fold_in(seeds[4], 3), 0, LANGS - 1).astype(jnp.int32),
        "margin": jnp.clip(jax.random.uniform(seeds[5], (LANGS,), jnp.float32, 0.5, 3.0), 0.5, 3.0),
    }


def reference(source_emb, target_emb, hard_pool, hard_index, language, margin):
    total_rows = source_emb.shape[0]
    width = source_emb.shape[1]
    margin_row = margin[language]
    hard_rows = hard_pool[hard_index]
    hard_score = jnp.sum(source_emb.astype(jnp.float32) * hard_rows.astype(jnp.float32), axis=1)
    block_rows = SRC_DEV
    block_count = total_rows // block_rows
    columns = jnp.arange(total_rows, dtype=jnp.int32)

    def one_block(grad_sum, block_at):
        start = (block_at * block_rows).astype(jnp.int32)
        sources = lax.dynamic_slice_in_dim(source_emb, start, block_rows, 0)
        margins = lax.dynamic_slice_in_dim(margin_row, start, block_rows, 0)
        hard_part = lax.dynamic_slice_in_dim(hard_score, start, block_rows, 0)
        hard_block = lax.dynamic_slice_in_dim(hard_rows, start, block_rows, 0)
        row_ids = start + jnp.arange(block_rows, dtype=jnp.int32)
        scores = jnp.dot(sources, target_emb.T, preferred_element_type=jnp.float32)
        positive = row_ids[:, None] == columns[None, :]
        adjusted = scores - jnp.where(positive, margins[:, None], jnp.float32(0.0))
        row_top = jnp.maximum(jnp.max(adjusted, axis=1), hard_part)
        row_total = jnp.sum(jnp.exp(adjusted - row_top[:, None]), axis=1) + jnp.exp(hard_part - row_top)
        log_total = row_top + jnp.log(row_total)
        row_loss = log_total - jnp.sum(jnp.where(positive, adjusted, jnp.float32(0.0)), axis=1)
        prob_tile = (jnp.exp(adjusted - log_total[:, None]) - positive.astype(jnp.float32)).astype(jnp.bfloat16)
        hard_prob = jnp.exp(hard_part - log_total)
        source_grad = jnp.dot(prob_tile, target_emb, preferred_element_type=jnp.float32)
        source_grad = source_grad + hard_prob[:, None] * hard_block.astype(jnp.float32)
        grad_sum = grad_sum + jnp.dot(prob_tile.T, sources, preferred_element_type=jnp.float32)
        return grad_sum, (row_loss, source_grad, hard_prob)

    start_grad = jnp.zeros((total_rows, width), jnp.float32)
    grad_sum, outputs = lax.scan(one_block, start_grad, jnp.arange(block_count, dtype=jnp.int32))
    row_loss = outputs[0].reshape(total_rows)
    source_grad = outputs[1].reshape(total_rows, width)
    hard_prob = outputs[2].reshape(total_rows)
    contribution = hard_prob[:, None] * source_emb.astype(jnp.float32)
    pool_grad = jnp.zeros((total_rows, width), jnp.float32).at[hard_index].add(contribution)
    return (row_loss, source_grad, grad_sum, pool_grad)
```

```python
import jax
import jax.numpy as jnp
from jax import lax
from jax.experimental import pallas as pl
from jax.experimental.pallas import tpu as pltpu
from jax.sharding import PartitionSpec as P

BF, F32 = jnp.bfloat16, jnp.float32
NEG = -1e30
LOW = -3e38
TILE = 384
CHUNKS = (((0, 0), (0, 1)), ((1, 0), (3, 0)), ((2, 0), (1, 1)), ((3, 1), (2, 1)))


def hop_blk(value, dz, dy, dc):
    route = []
    for i in range(16):
        z, y, c = i // 4, (i // 2) % 2, i % 2
        route.append((i, ((z + dz) % 4) * 4 + (y ^ dy) * 2 + (c ^ dc)))
    return lax.ppermute(value, "blk", route)


def hop_grp(value, dx, dy):
    return lax.ppermute(value, "grp", [(i, ((i // 2 + dx) % 4) * 2 + ((i % 2) ^ dy)) for i in range(8)])


def dot_f32(a, b, dims):
    return lax.dot_general(a, b, (dims, ((), ())), preferred_element_type=F32)


def columns_of(rows):
    pad = jnp.zeros((120, rows.shape[1]), F32)
    return jnp.transpose(jnp.concatenate([rows, pad], axis=0))


def score_kernel(place, src, t0, t1, t2, t3, e_out, stat_out, tgt_out, s_ref, d_ref, a_ref):
    rows = t0.shape[0]
    step = pl.program_id(0)

    @pl.when(step == 0)
    def _():
        top = jnp.zeros((1, 1), F32)
        for q, t in enumerate((t0, t1, t2, t3)):
            block = t[...]
            tgt_out[pl.ds(q * rows, rows), :] = block
            top = jnp.maximum(top, jnp.max(jnp.abs(block.astype(F32)), keepdims=True))
        a_ref[...] = jnp.broadcast_to(top, a_ref.shape)

    tgt = tgt_out[...]
    lane = lax.broadcasted_iota(jnp.int32, (rows, 128), 1)
    for sub in range(2):
        here = pl.ds(sub * rows, rows)
        s_ref[sub] = dot_f32(src[here, :], tgt, ((1,), (1,)))
        d_ref[sub] = jnp.zeros((rows, 1), F32)
        for q in range(4):

            @pl.when(place[q] == step * 2 + sub)
            def _():
                s = s_ref[sub]
                ahead = lax.broadcasted_iota(jnp.int32, s.shape, 1) - lax.broadcasted_iota(jnp.int32, s.shape, 0)
                mask = ahead == q * rows
                d_ref[sub] = jnp.sum(jnp.where(mask, s, 0.0), axis=1, keepdims=True)
                s_ref[sub] = jnp.where(mask, NEG, s)

    parts = []
    for sub in range(2):
        s = s_ref[sub]
        top = jnp.max(s, axis=1, keepdims=True)
        e = jnp.exp(s - top)
        total = jnp.sum(e, axis=1, keepdims=True)
        e_out[pl.ds(sub * rows, rows), :] = e.astype(BF)
        part = jnp.where(lane == 0, top, jnp.where(lane == 1, total, jnp.where(lane == 2, d_ref[sub], a_ref[0:1, :])))
        parts.append(part)
    stat_out[...] = jnp.transpose(jnp.concatenate(parts, axis=0))[0:8, :]


def score_call(place, src, blocks):
    rows, width = blocks[0].shape
    total = src.shape[0]
    cols = 4 * rows
    whole = pl.BlockSpec((rows, width), lambda i, p: (0, 0))
    return pl.pallas_call(
        score_kernel,
        out_shape=(
            jax.ShapeDtypeStruct((total, cols), BF),
            jax.ShapeDtypeStruct((8, total), F32),
            jax.ShapeDtypeStruct((cols, width), BF),
        ),
        grid_spec=pltpu.PrefetchScalarGridSpec(
            num_scalar_prefetch=1,
            grid=(total // TILE,),
            in_specs=[pl.BlockSpec((TILE, width), lambda i, p: (i, 0))] + [whole] * 4,
            out_specs=(
                pl.BlockSpec((TILE, cols), lambda i, p: (i, 0)),
                pl.BlockSpec((8, TILE), lambda i, p: (0, i)),
                pl.BlockSpec((cols, width), lambda i, p: (0, 0)),
            ),
            scratch_shapes=[
                pltpu.VMEM((2, rows, cols), F32),
                pltpu.VMEM((2, rows, 1), F32),
                pltpu.VMEM((8, 128), F32),
            ],
        ),
        compiler_params=pltpu.CompilerParams(vmem_limit_bytes=40 << 20),
        cost_estimate=pl.CostEstimate(
            flops=2 * total * cols * width, bytes_accessed=total * (width + cols) * 2, transcendentals=total * cols
        ),
        name="scores",
    )(place, src, *blocks)


def source_kernel(place, w_ref, *refs):
    es, tgts, out, acc = refs[0:4], refs[4:8], refs[8], refs[9]
    step = pl.program_id(0)
    rows = acc.shape[1]
    weights = columns_of(w_ref[...])
    for sub in range(2):
        here = slice(sub * rows, (sub + 1) * rows)
        total = None
        for c in range(4):
            part = dot_f32(es[c][here, :], tgts[c][...], ((1,), (0,))) * weights[here, c : c + 1]
            total = part if total is None else total + part
        acc[sub] = total
        at = place[step * 2 + sub]
        for c in range(4):

            @pl.when(at // 4 == c)
            def _():
                mine = tgts[c][pl.ds(pl.multiple_of((at % 4) * rows, rows), rows), :]
                acc[sub] = acc[sub] + weights[here, 4:5] * mine.astype(F32)

        out[here, :] = acc[sub].astype(BF)


def source_call(place, weights, es, tgts, rows):
    total, cols = es[0].shape
    width = tgts[0].shape[1]
    return pl.pallas_call(
        source_kernel,
        out_shape=jax.ShapeDtypeStruct((total, width), BF),
        grid_spec=pltpu.PrefetchScalarGridSpec(
            num_scalar_prefetch=1,
            grid=(total // TILE,),
            in_specs=[pl.BlockSpec((8, TILE), lambda i, p: (0, i))]
            + [pl.BlockSpec((TILE, cols), lambda i, p: (i, 0))] * 4
            + [pl.BlockSpec((cols, width), lambda i, p: (0, 0))] * 4,
            out_specs=pl.BlockSpec((TILE, width), lambda i, p: (i, 0)),
            scratch_shapes=[pltpu.VMEM((2, rows, width), F32)],
        ),
        compiler_params=pltpu.CompilerParams(vmem_limit_bytes=40 << 20),
        cost_estimate=pl.CostEstimate(
            flops=8 * total * cols * width, bytes_accessed=total * (4 * cols + width) * 2, transcendentals=0
        ),
        name="source_terms",
    )(place, weights, *es, *tgts)


def target_kernel(place, w_ref, e_ref, src_ref, keep, give, acc, scaled, *, chunk):
    step, steps = pl.program_id(0), pl.num_programs(0)
    rows = src_ref.shape[0] // 2
    weights = columns_of(w_ref[...])
    scaled[...] = (src_ref[...].astype(F32) * weights[:, chunk : chunk + 1]).astype(BF)
    part = dot_f32(e_ref[...], scaled[...], ((0,), (0,)))

    @pl.when(step == 0)
    def _():
        acc[...] = part

    @pl.when(step > 0)
    def _():
        acc[...] = acc[...] + part

    for sub in range(2):
        here = slice(sub * rows, (sub + 1) * rows)
        for q in range(4):

            @pl.when(place[q] == step * 2 + sub)
            def _():
                there = pl.ds(q * rows, rows)
                acc[there, :] = acc[there, :] + weights[here, 4:5] * src_ref[here, :].astype(F32)

    @pl.when(step == steps - 1)
    def _():
        keep[...] = acc[0 : 2 * rows, :]
        give[...] = acc[2 * rows : 4 * rows, :]


def target_call(place, weights, e, src, chunk):
    total, cols = e.shape
    width = src.shape[1]
    half = jax.ShapeDtypeStruct((cols // 2, width), F32)
    half_spec = pl.BlockSpec((cols // 2, width), lambda i, p: (0, 0))

    def kernel(*refs):
        target_kernel(*refs, chunk=chunk)

    return pl.pallas_call(
        kernel,
        out_shape=(half, half),
        grid_spec=pltpu.PrefetchScalarGridSpec(
            num_scalar_prefetch=1,
            grid=(total // TILE,),
            in_specs=[
                pl.BlockSpec((8, TILE), lambda i, p: (0, i)),
                pl.BlockSpec((TILE, cols), lambda i, p: (i, 0)),
                pl.BlockSpec((TILE, width), lambda i, p: (i, 0)),
            ],
            out_specs=(half_spec, half_spec),
            scratch_shapes=[pltpu.VMEM((cols, width), F32), pltpu.VMEM((TILE, width), BF)],
        ),
        compiler_params=pltpu.CompilerParams(vmem_limit_bytes=40 << 20),
        cost_estimate=pl.CostEstimate(
            flops=2 * total * cols * width, bytes_accessed=total * (width + cols) * 2 + cols * width * 4, transcendentals=0
        ),
        name="target_terms",
    )(place, weights, e, src)


def shards(source_emb, target_emb, hard_pool, hard_index, language, margin):
    total, width = source_emb.shape
    rows = target_emb.shape[0]
    blk, grp = lax.axis_index("blk"), lax.axis_index("grp")
    owners = 128
    cap = max(2, (2 * rows + owners - 1) // owners)
    slots = owners * cap
    z, y, c = blk // 4, (blk // 2) % 2, blk % 2

    start = grp * rows
    own_index = lax.dynamic_slice_in_dim(hard_index, start, rows, 0)
    own_source = lax.dynamic_slice_in_dim(source_emb, start, rows, 0)
    owner, pool_row = own_index // rows, own_index % rows
    position = jnp.arange(rows, dtype=jnp.int32)
    same = (owner[:, None] == owner[None, :]) & (position[None, :] < position[:, None])
    slot = owner * cap + jnp.sum(same.astype(jnp.int32), axis=1)
    at_slot = slot[:, None] == jnp.arange(slots, dtype=jnp.int32)[None, :]
    requests = jnp.sum(jnp.where(at_slot, pool_row[:, None] + 1, 0), axis=0) - 1
    wanted = lax.all_to_all(requests.reshape(owners, cap), ("grp", "blk"), 0, 0, tiled=True).reshape(slots)
    serve = (wanted[:, None] == position[None, :]).astype(BF)
    served = dot_f32(serve, hard_pool, ((1,), (0,))).astype(BF).reshape(owners, cap, width)
    fetched = lax.all_to_all(served, ("grp", "blk"), 0, 0, tiled=True).reshape(slots, width)
    pick = at_slot.astype(BF)
    hard_rows = dot_f32(pick, fetched, ((1,), (0,)))
    hard_score = jnp.sum(own_source.astype(F32) * hard_rows, axis=1)

    lang_match = language[:, None] == jnp.arange(margin.shape[0], dtype=jnp.int32)[None, :]
    margin_row = jnp.sum(jnp.where(lang_match, margin[None, :], 0.0), axis=1)

    have = {(0, 0, 0): target_emb}
    have[0, 1, 0] = hop_blk(target_emb, 0, 1, 0)
    for dz in (1, 3, 2):
        have[dz, 0, 0] = hop_blk(target_emb, -dz, 0, 0)
    for dz in (1, 3, 2):
        have[dz, 1, 0] = hop_blk(have[0, 1, 0], -dz, 0, 0)
    for dz, dy in [pair for chunk in CHUNKS for pair in chunk]:
        have[dz, dy, 1] = hop_blk(have[dz, dy, 0], 0, 0, 1)

    holds = grp == blk // 2
    place = {}
    for dz in range(4):
        for dy in range(2):
            for dc in range(2):
                zz = (z + dz) % 4
                k = (zz % 2) * 4 + (y ^ dy) * 2 + (c ^ dc)
                place[dz, dy, dc] = jnp.where(holds & (zz // 2 == c), k, -1)
    order = [[(dz, dy, dc) for dc in (0, 1) for dz, dy in chunk] for chunk in CHUNKS]
    places = [jnp.stack([place[key] for key in chunk]) for chunk in order]
    flat = jnp.concatenate(places)
    found = flat[None, :] == jnp.arange(8, dtype=jnp.int32)[:, None]
    where_is = jnp.sum(jnp.where(found, jnp.arange(16, dtype=jnp.int32)[None, :] + 1, 0), axis=1) - 1
    where_is = jnp.where(where_is < 0, -4, where_is)

    es, stats, tgts = [], [], []
    for chunk, at in zip(order, places):
        e, stat, tgt = score_call(at, source_emb, [have[key] for key in chunk])
        es.append(e)
        stats.append(stat)
        tgts.append(tgt)

    tops = jnp.stack([stat[0] for stat in stats])
    sums = jnp.stack([stat[1] for stat in stats])
    diag = sum(stat[2] for stat in stats)
    reach = jnp.maximum(jnp.max(jnp.stack([stat[3] for stat in stats]), axis=0), jnp.max(jnp.abs(hard_rows)))
    pos = jnp.where(holds, diag - margin_row, 0.0)
    hard_all = lax.dynamic_update_slice_in_dim(jnp.full((total,), LOW, F32), hard_score, start, 0)
    top = jnp.maximum(jnp.max(tops, axis=0), hard_all)
    off = jnp.sum(sums * jnp.exp(tops - top), axis=0) + jnp.exp(hard_all - top)
    mine = jnp.stack([top, off, pos, reach])
    everyone = lax.all_to_all(jnp.broadcast_to(mine[None], (8, 4, total)), "grp", 0, 0, tiled=True)
    pos = jnp.sum(everyone[:, 2], axis=0)
    reach = jnp.max(everyone[:, 3], axis=0)
    top = jnp.maximum(jnp.max(everyone[:, 0], axis=0), pos)
    off = jnp.sum(everyone[:, 1] * jnp.exp(everyone[:, 0] - top), axis=0)
    log_total = top + jnp.log(off + jnp.exp(pos - top))
    row_loss = log_total - pos
    less = jnp.exp(pos - log_total) - 1.0
    weights = jnp.exp(tops - log_total)
    diag_weight = jnp.where(holds, less, 0.0)
    weights = jnp.concatenate([weights, diag_weight[None], jnp.zeros((3, total), F32)])

    source_part = source_call(where_is, weights, es, tgts, rows)
    source_parts = lax.all_to_all(source_part.reshape(8, rows, width), "grp", 0, 0, tiled=True)
    own_total = lax.dynamic_slice_in_dim(log_total, start, rows, 0)
    hard_prob = jnp.exp(hard_score - own_total)
    own_grad = jnp.sum(source_parts.astype(F32), axis=0) + hard_prob[:, None] * hard_rows
    mass = jnp.abs(less) + off * jnp.exp(top - log_total)
    bound = jnp.maximum(1.01 * reach * mass, 1e-30)
    own_bound = lax.dynamic_slice_in_dim(bound, start, rows, 0)
    coded = jnp.round(jnp.clip(own_grad * (32767.0 / own_bound)[:, None], -32767.0, 32767.0)).astype(jnp.int16)
    pair = jnp.stack([coded, hop_grp(coded, 0, 1)])
    pairs = [pair] + [hop_grp(pair, -dx, 0) for dx in (1, 2, 3)]
    x_at, y_at = grp // 2, grp % 2
    source_grad = jnp.zeros((total, width), F32)
    for dx in range(4):
        for dy in range(2):
            at = (((x_at + dx) % 4) * 2 + (y_at ^ dy)) * rows
            scale = lax.dynamic_slice_in_dim(bound, at, rows, 0) * (1.0 / 32767.0)
            source_grad = lax.dynamic_update_slice_in_dim(
                source_grad, pairs[dx][dy].astype(F32) * scale[:, None], at, 0
            )

    part = {}
    for n, chunk in enumerate(CHUNKS):
        keep, give = target_call(places[n], weights, es[n], source_emb, n)
        both = keep + hop_blk(give, 0, 0, 1)
        part[chunk[0]], part[chunk[1]] = both[:rows], both[rows:]
    lines = [part[0, 0], part[0, 1]]
    for dz in (1, 3, 2):
        moved = [hop_blk(part[dz, dy].astype(BF), dz, 0, 0).astype(F32) for dy in range(2)]
        lines = [lines[0] + moved[0], lines[1] + moved[1]]
    target_grad = lines[0] + hop_blk(lines[1], 0, 1, 0)

    contribution = (hard_prob[:, None] * own_source.astype(F32)).astype(BF)
    outgoing = dot_f32(pick, contribution, ((0,), (0,))).astype(BF).reshape(owners, cap, width)
    incoming = lax.all_to_all(outgoing, ("grp", "blk"), 0, 0, tiled=True).reshape(slots, width)
    pool_grad = dot_f32(serve, incoming, ((0,), (0,)))
    return (row_loss, source_grad, target_grad, pool_grad)


def solution(mesh):
    in_specs = (P("blk", None), P(("grp", "blk"), None), P(("grp", "blk"), None), P("blk"), P("blk"), P())
    out_specs = (P("blk"), P("blk", None), P(("grp", "blk"), None), P(("grp", "blk"), None))
    return jax.shard_map(shards, mesh=mesh, in_specs=in_specs, out_specs=out_specs, check_vma=False)
```

```python
import jax
import jax.numpy as jnp
from jax import lax
from jax.experimental import pallas as pl
from jax.experimental.pallas import tpu as pltpu
from jax.sharding import PartitionSpec as P

BF, F32 = jnp.bfloat16, jnp.float32
NEG = -1e30
LOW = -3e38
TILE = 768
PART = 384
CHUNKS = (((0, 0), (0, 1)), ((1, 0), (3, 0)), ((2, 0), (1, 1)), ((3, 1), (2, 1)))


def hop_blk(value, dz, dy, dc):
    route = []
    for i in range(16):
        z, y, c = i // 4, (i // 2) % 2, i % 2
        route.append((i, ((z + dz) % 4) * 4 + (y ^ dy) * 2 + (c ^ dc)))
    return lax.ppermute(value, "blk", route)


def hop_grp(value, dx, dy):
    return lax.ppermute(value, "grp", [(i, ((i // 2 + dx) % 4) * 2 + ((i % 2) ^ dy)) for i in range(8)])


def dot_f32(a, b, dims):
    return lax.dot_general(a, b, (dims, ((), ())), preferred_element_type=F32)


def columns_of(rows):
    pad = jnp.zeros((120, rows.shape[1]), F32)
    return jnp.transpose(jnp.concatenate([rows, pad], axis=0))


def score_kernel(place, src, t0, t1, t2, t3, e_out, stat_out, tgt_out, d_ref, a_ref):
    rows = t0.shape[0]
    step = pl.program_id(0)
    blocks = (t0, t1, t2, t3)
    per = src.shape[0] // rows

    @pl.when(step == 0)
    def _():
        top = jnp.zeros((1, 1), F32)
        for q, t in enumerate(blocks):
            block = t[...]
            tgt_out[pl.ds(q * rows, rows), :] = block
            top = jnp.maximum(top, jnp.max(jnp.abs(block.astype(F32)), keepdims=True))
        a_ref[...] = jnp.broadcast_to(top, a_ref.shape)

    d_ref[...] = jnp.zeros_like(d_ref)
    for sub in range(per):
        for q, t in enumerate(blocks):

            @pl.when(place[q] == step * per + sub)
            def _():
                here = pl.ds(sub * rows, rows)
                d_ref[here, :] = jnp.sum(src[here, :].astype(F32) * t[...].astype(F32), axis=1, keepdims=True)

    tgt = tgt_out[...]
    lane = lax.broadcasted_iota(jnp.int32, (PART, 128), 1)
    column = lax.broadcasted_iota(jnp.int32, (PART, 4 * rows), 1)
    line = lax.broadcasted_iota(jnp.int32, (PART, 1), 0)
    parts = []
    for first in range(0, src.shape[0], PART):
        hole = jnp.full((PART, 1), -1, jnp.int32)
        for sub in range(PART // rows):
            for q in range(4):
                k = step * per + first // rows + sub
                at = jnp.where(place[q] == k, (q - sub) * rows, jnp.int32(-(1 << 20)))
                inside = (line >= sub * rows) & (line < (sub + 1) * rows) & (at > -(1 << 19))
                hole = jnp.where(inside, line + at, hole)
        here = pl.ds(first, PART)
        s = dot_f32(src[here, :], tgt, ((1,), (1,)))
        s = jnp.where(column == hole, NEG, s)
        top = jnp.max(s, axis=1, keepdims=True)
        e = jnp.exp(s - top)
        total = jnp.sum(e, axis=1, keepdims=True)
        e_out[here, :] = e.astype(BF)
        part = jnp.where(lane == 1, total, jnp.where(lane == 2, d_ref[here, :], a_ref[0:1, :]))
        parts.append(jnp.where(lane == 0, top, part))
    stat_out[...] = jnp.transpose(jnp.concatenate(parts, axis=0))[0:8, :]


def score_call(place, src, blocks):
    rows, width = blocks[0].shape
    total = src.shape[0]
    cols = 4 * rows
    whole = pl.BlockSpec((rows, width), lambda i, p: (0, 0))
    return pl.pallas_call(
        score_kernel,
        out_shape=(
            pltpu.HBM((total, cols), BF),
            jax.ShapeDtypeStruct((8, total), F32),
            pltpu.HBM((cols, width), BF),
        ),
        grid_spec=pltpu.PrefetchScalarGridSpec(
            num_scalar_prefetch=1,
            grid=(total // TILE,),
            in_specs=[pl.BlockSpec((TILE, width), lambda i, p: (i, 0))] + [whole] * 4,
            out_specs=(
                pl.BlockSpec((TILE, cols), lambda i, p: (i, 0)),
                pl.BlockSpec((8, TILE), lambda i, p: (0, i)),
                pl.BlockSpec((cols, width), lambda i, p: (0, 0)),
            ),
            scratch_shapes=[pltpu.VMEM((TILE, 1), F32), pltpu.VMEM((8, 128), F32)],
        ),
        compiler_params=pltpu.CompilerParams(vmem_limit_bytes=20 << 20),
        cost_estimate=pl.CostEstimate(
            flops=2 * total * cols * width, bytes_accessed=total * (width + cols) * 2, transcendentals=total * cols
        ),
        name="scores",
    )(place, src, *blocks)


def source_kernel(place, w_ref, *refs):
    es, tgts, out, base = refs[0:4], refs[4:8], refs[8], refs[9]
    step = pl.program_id(0)
    per = place.shape[0] // pl.num_programs(0)
    rows = base.shape[0] // per
    weights = columns_of(w_ref[...])

    @pl.when(step == 0)
    def _():
        base[...] = jnp.zeros_like(base)

    for sub in range(per):
        at = place[step * per + sub]
        here = slice(sub * rows, (sub + 1) * rows)
        for c in range(4):

            @pl.when(at // 4 == c)
            def _():
                mine = tgts[c][pl.ds(pl.multiple_of((at % 4) * rows, rows), rows), :]
                base[here, :] = weights[here, 4:5] * mine.astype(F32)

    for first in range(0, base.shape[0], PART):
        here = slice(first, first + PART)
        total = base[here, :]
        for c in range(4):
            total = total + dot_f32(es[c][here, :], tgts[c][...], ((1,), (0,))) * weights[here, c : c + 1]
        out[here, :] = total.astype(BF)


def source_call(place, weights, es, tgts):
    total, cols = es[0].shape
    width = tgts[0].shape[1]
    return pl.pallas_call(
        source_kernel,
        out_shape=jax.ShapeDtypeStruct((total, width), BF),
        grid_spec=pltpu.PrefetchScalarGridSpec(
            num_scalar_prefetch=1,
            grid=(total // TILE,),
            in_specs=[pl.BlockSpec((8, TILE), lambda i, p: (0, i))]
            + [pl.BlockSpec((TILE, cols), lambda i, p: (i, 0))] * 4
            + [pl.BlockSpec((cols, width), lambda i, p: (0, 0))] * 4,
            out_specs=pl.BlockSpec((TILE, width), lambda i, p: (i, 0)),
            scratch_shapes=[pltpu.VMEM((TILE, width), F32)],
        ),
        compiler_params=pltpu.CompilerParams(vmem_limit_bytes=32 << 20),
        cost_estimate=pl.CostEstimate(
            flops=8 * total * cols * width, bytes_accessed=total * (4 * cols + width) * 2, transcendentals=0
        ),
        name="source_terms",
    )(place, weights, *es, *tgts)


def target_kernel(place, w_ref, e_ref, src_ref, _, keep, give, acc, scaled, column, *, chunk):
    rows = acc.shape[0] // 4
    total = src_ref.shape[0]
    for first in range(0, total, PART):
        here = slice(first, first + PART)
        weights = columns_of(w_ref[:, here])
        column[here, :] = weights
        scaled[here, :] = (src_ref[here, :].astype(F32) * weights[:, chunk : chunk + 1]).astype(BF)
    acc[...] = dot_f32(e_ref[...], scaled[...], ((0,), (0,)))
    for q in range(4):

        @pl.when(place[q] >= 0)
        def _():
            there = slice(q * rows, (q + 1) * rows)
            here = pl.ds(pl.multiple_of(place[q] * rows, rows), rows)
            acc[there, :] = acc[there, :] + column[here, 4:5] * src_ref[here, :].astype(F32)

    keep[...] = acc[0 : 2 * rows, :]
    give[...] = acc[2 * rows : 4 * rows, :].astype(BF)


def target_call(place, weights, e, src, after, chunk):
    total, cols = e.shape
    width = src.shape[1]

    def kernel(*refs):
        target_kernel(*refs, chunk=chunk)

    vmem = pl.BlockSpec(memory_space=pltpu.VMEM)
    return pl.pallas_call(
        kernel,
        out_shape=(jax.ShapeDtypeStruct((cols // 2, width), F32), jax.ShapeDtypeStruct((cols // 2, width), BF)),
        in_specs=[pl.BlockSpec(memory_space=pltpu.SMEM), vmem, vmem, vmem, pl.BlockSpec(memory_space=pl.ANY)],
        out_specs=(vmem, vmem),
        scratch_shapes=[pltpu.VMEM((cols, width), F32), pltpu.VMEM((total, width), BF), pltpu.VMEM((total, 128), F32)],
        compiler_params=pltpu.CompilerParams(vmem_limit_bytes=24 << 20),
        cost_estimate=pl.CostEstimate(
            flops=2 * total * cols * width, bytes_accessed=total * (width + cols) * 2 + cols * width * 3, transcendentals=0
        ),
        name="target_terms",
    )(place, weights, e, src, after)


def code_kernel(parts, hard, col, out):
    total = hard[...] * col[:, 0:1]
    for g in range(parts.shape[0]):
        total = total + parts[g].astype(F32)
    scaled = jnp.clip(total * col[:, 1:2], -32767.0, 32767.0)
    out[...] = jnp.round(scaled).astype(jnp.int32).astype(jnp.int16)


def decode_kernel(order, scale, own, side, far, pairs1, pairs2, pairs3, far_side, out):
    step = pl.program_id(0)
    half = own.shape[0] // 2
    pairs = (None, pairs1, pairs2, pairs3)
    for dx in range(4):
        for dy in range(2):

            @pl.when(step == dx * 2 + dy)
            def _():
                if dx == 0:
                    whole = (own if dy == 0 else side)[...]
                    out[...] = whole.astype(jnp.int32).astype(F32) * scale[...]
                else:
                    low = pairs[dx][dy]
                    high = (far if dy == 0 else far_side)[dx - 1]
                    out[0:half, :] = low.astype(jnp.int32).astype(F32) * scale[0:half, :]
                    out[half:, :] = high.astype(jnp.int32).astype(F32) * scale[half:, :]


def decode_call(order, scale, pieces):
    rows, width = pieces[0].shape
    total = scale.shape[0]
    return pl.pallas_call(
        decode_kernel,
        out_shape=jax.ShapeDtypeStruct((total, width), F32),
        grid_spec=pltpu.PrefetchScalarGridSpec(
            num_scalar_prefetch=1,
            grid=(total // rows,),
            in_specs=[pl.BlockSpec((rows, 1), lambda i, p: (p[i], 0))]
            + [pl.BlockSpec(x.shape, lambda i, p, n=x.ndim: (0,) * n) for x in pieces],
            out_specs=pl.BlockSpec((rows, width), lambda i, p: (p[i], 0)),
        ),
        compiler_params=pltpu.CompilerParams(vmem_limit_bytes=24 << 20),
        cost_estimate=pl.CostEstimate(flops=total * width, bytes_accessed=total * width * 6, transcendentals=0),
        name="decode",
    )(order, scale, *pieces)


def shards(source_emb, target_emb, hard_pool, hard_index, language, margin):
    total, width = source_emb.shape
    rows = target_emb.shape[0]
    blk, grp = lax.axis_index("blk"), lax.axis_index("grp")
    owners = 128
    cap = max(2, (2 * rows + owners - 1) // owners)
    slots = owners * cap
    z, y, c = blk // 4, (blk // 2) % 2, blk % 2

    start = grp * rows
    own_index = lax.dynamic_slice_in_dim(hard_index, start, rows, 0)
    own_source = lax.dynamic_slice_in_dim(source_emb, start, rows, 0)
    owner, pool_row = own_index // rows, own_index % rows
    position = jnp.arange(rows, dtype=jnp.int32)
    same = (owner[:, None] == owner[None, :]) & (position[None, :] < position[:, None])
    slot = owner * cap + jnp.sum(same.astype(jnp.int32), axis=1)
    at_slot = slot[:, None] == jnp.arange(slots, dtype=jnp.int32)[None, :]
    requests = jnp.sum(jnp.where(at_slot, pool_row[:, None] + 1, 0), axis=0) - 1
    wanted = lax.all_to_all(requests.reshape(owners, cap), ("grp", "blk"), 0, 0, tiled=True)
    lang_match = language[:, None] == jnp.arange(margin.shape[0], dtype=jnp.int32)[None, :]
    margin_row = jnp.sum(jnp.where(lang_match, margin[None, :], 0.0), axis=1)

    have = {(0, 0, 0): target_emb}
    have[0, 1, 0] = hop_blk(target_emb, 0, 1, 0)
    for dz in (1, 3, 2):
        have[dz, 0, 0] = hop_blk(target_emb, -dz, 0, 0)
    for dz in (1, 3, 2):
        have[dz, 1, 0] = hop_blk(have[0, 1, 0], -dz, 0, 0)
    for dz, dy in [pair for chunk in CHUNKS for pair in chunk]:
        have[dz, dy, 1] = hop_blk(have[dz, dy, 0], 0, 0, 1)

    holds = grp == blk // 2
    place = {}
    for dz in range(4):
        for dy in range(2):
            for dc in range(2):
                zz = (z + dz) % 4
                k = (zz % 2) * 4 + (y ^ dy) * 2 + (c ^ dc)
                place[dz, dy, dc] = jnp.where(holds & (zz // 2 == c), k, -1)
    order = [[(dz, dy, dc) for dc in (0, 1) for dz, dy in chunk] for chunk in CHUNKS]
    places = [jnp.stack([place[key] for key in chunk]) for chunk in order]
    flat = jnp.concatenate(places)
    found = flat[None, :] == jnp.arange(8, dtype=jnp.int32)[:, None]
    where_is = jnp.sum(jnp.where(found, jnp.arange(16, dtype=jnp.int32)[None, :] + 1, 0), axis=1) - 1
    where_is = jnp.where(where_is < 0, -4, where_is)

    es, stats, tgts = [], [], []

    def add_chunk(n):
        e, stat, tgt = score_call(places[n], source_emb, [have[key] for key in order[n]])
        es.append(e)
        stats.append(stat)
        tgts.append(tgt)

    add_chunk(0)
    wanted, stats[0] = lax.optimization_barrier((wanted, stats[0]))
    serve = (wanted.reshape(slots)[:, None] == position[None, :]).astype(BF)
    served = dot_f32(serve, hard_pool, ((1,), (0,))).astype(BF).reshape(owners, cap, width)
    served, places[1] = lax.optimization_barrier((served, places[1]))
    fetched = lax.all_to_all(served, ("grp", "blk"), 0, 0, tiled=True).reshape(slots, width)
    add_chunk(1)
    add_chunk(2)
    fetched, stats[2] = lax.optimization_barrier((fetched, stats[2]))
    pick = at_slot.astype(BF)
    hard_rows = dot_f32(pick, fetched, ((1,), (0,)))
    hard_score = jnp.sum(own_source.astype(F32) * hard_rows, axis=1)
    add_chunk(3)

    tops = jnp.stack([stat[0] for stat in stats])
    sums = jnp.stack([stat[1] for stat in stats])
    diag = sum(stat[2] for stat in stats)
    reach = jnp.maximum(jnp.max(jnp.stack([stat[3] for stat in stats]), axis=0), jnp.max(jnp.abs(hard_rows)))
    pos = jnp.where(holds, diag - margin_row, 0.0)
    hard_all = lax.dynamic_update_slice_in_dim(jnp.full((total,), LOW, F32), hard_score, start, 0)
    top = jnp.maximum(jnp.max(tops, axis=0), hard_all)
    off = jnp.sum(sums * jnp.exp(tops - top), axis=0) + jnp.exp(hard_all - top)
    mine = jnp.stack([top, off, pos, reach])
    everyone = lax.all_to_all(jnp.broadcast_to(mine[None], (8, 4, total)), "grp", 0, 0, tiled=True)
    pos = jnp.sum(everyone[:, 2], axis=0)
    reach = jnp.max(everyone[:, 3], axis=0)
    top = jnp.maximum(jnp.max(everyone[:, 0], axis=0), pos)
    off = jnp.sum(everyone[:, 1] * jnp.exp(everyone[:, 0] - top), axis=0)
    log_total = top + jnp.log(off + jnp.exp(pos - top))
    row_loss = log_total - pos
    less = jnp.exp(pos - log_total) - 1.0
    weights = jnp.exp(tops - log_total)
    diag_weight = jnp.where(holds, less, 0.0)
    weights = jnp.concatenate([weights, diag_weight[None], jnp.zeros((3, total), F32)])

    source_part = source_call(where_is, weights, es, tgts)
    token = hop_blk(source_part[:16, :128], 0, 0, 1)
    source_parts = lax.all_to_all(source_part.reshape(8, rows, width), "grp", 0, 0, tiled=True)
    own_total = lax.dynamic_slice_in_dim(log_total, start, rows, 0)
    hard_prob = jnp.exp(hard_score - own_total)
    mass = jnp.abs(less) + off * jnp.exp(top - log_total)
    bound = jnp.maximum(1.01 * reach * mass, 1e-30)
    own_bound = lax.dynamic_slice_in_dim(bound, start, rows, 0)
    col = jnp.stack([hard_prob, 32767.0 / own_bound], axis=1)
    coded = pl.pallas_call(
        code_kernel,
        out_shape=jax.ShapeDtypeStruct((rows, width), jnp.int16),
        cost_estimate=pl.CostEstimate(flops=10 * rows * width, bytes_accessed=22 * rows * width, transcendentals=0),
        name="code",
    )(source_parts, hard_rows, col)
    hard_prob, coded = lax.optimization_barrier((hard_prob, coded))
    half = rows // 2
    side = hop_grp(coded, 0, 1)
    far = [hop_grp(coded[half:], -dx, 0) for dx in (1, 2, 3)]
    near = jnp.stack([coded[:half], side[:half]])
    pairs = [hop_grp(near, -dx, 0) for dx in (1, 2, 3)]
    far = jnp.stack(far)
    far_side = hop_grp(far, 0, 1)
    x_at, y_at = grp // 2, grp % 2
    blocks = jnp.stack([((x_at + dx) % 4) * 2 + (y_at ^ dy) for dx in range(4) for dy in range(2)])
    source_grad = decode_call(
        blocks, (bound * (1.0 / 32767.0))[:, None], [coded, side, far, *pairs, far_side]
    )

    part = {}
    for n, chunk in enumerate(CHUNKS):
        keep, give = target_call(places[n], weights, es[n], source_emb, token, n)
        both = keep + hop_blk(give, 0, 0, 1).astype(F32)
        part[chunk[0]], part[chunk[1]] = both[:rows], both[rows:]
    lines = [part[0, 0], part[0, 1]]
    for dz in (1, 3, 2):
        moved = [hop_blk(part[dz, dy].astype(BF), dz, 0, 0).astype(F32) for dy in range(2)]
        lines = [lines[0] + moved[0], lines[1] + moved[1]]
    target_grad = lines[0] + hop_blk(lines[1].astype(BF), 0, 1, 0).astype(F32)

    contribution = (hard_prob[:, None] * own_source.astype(F32)).astype(BF)
    outgoing = dot_f32(pick, contribution, ((0,), (0,))).astype(BF).reshape(owners, cap, width)
    incoming = lax.all_to_all(outgoing, ("grp", "blk"), 0, 0, tiled=True).reshape(slots, width)
    pool_grad = dot_f32(serve, incoming, ((0,), (0,)))
    return (row_loss, source_grad, target_grad, pool_grad)


def solution(mesh):
    in_specs = (P("blk", None), P(("grp", "blk"), None), P(("grp", "blk"), None), P("blk"), P("blk"), P())
    out_specs = (P("blk"), P("blk", None), P(("grp", "blk"), None), P(("grp", "blk"), None))
    return jax.shard_map(shards, mesh=mesh, in_specs=in_specs, out_specs=out_specs, check_vma=False)
```

```python
import jax
import jax.numpy as jnp
from jax import lax
from jax.experimental import pallas as pl
from jax.experimental.pallas import tpu as pltpu
from jax.sharding import PartitionSpec as P

BF, F32 = jnp.bfloat16, jnp.float32
NEG = -1e30
LOW = -3e38
TILE = 768
PART = 384
CHUNKS = tuple(((dz, 0), (dz, 1)) for dz in (0, 1, 3, 2))


def hop_blk(value, dz, dy, dc):
    route = []
    for i in range(16):
        z, y, c = i // 4, (i // 2) % 2, i % 2
        route.append((i, ((z + dz) % 4) * 4 + (y ^ dy) * 2 + (c ^ dc)))
    return lax.ppermute(value, "blk", route)


def hop_grp(value, dx, dy):
    return lax.ppermute(value, "grp", [(i, ((i // 2 + dx) % 4) * 2 + ((i % 2) ^ dy)) for i in range(8)])


def dot_f32(a, b, dims):
    return lax.dot_general(a, b, (dims, ((), ())), preferred_element_type=F32)


def columns_of(rows):
    pad = jnp.zeros((120, rows.shape[1]), F32)
    return jnp.transpose(jnp.concatenate([rows, pad], axis=0))


def score_kernel(place, src, t0, t1, t2, t3, *refs):
    e_out, stat_out, tgt_out, d_ref, a_ref = refs[-5:]
    rows = t0.shape[0]
    step = pl.program_id(0)
    blocks = (t0, t1, t2, t3)
    per = src.shape[0] // rows

    @pl.when(step == 0)
    def _():
        top = jnp.zeros((1, 1), F32)
        for q, t in enumerate(blocks):
            block = t[...]
            tgt_out[0, pl.ds(q * rows, rows), :] = block
            top = jnp.maximum(top, jnp.max(jnp.abs(block.astype(F32)), keepdims=True))
        a_ref[...] = jnp.broadcast_to(top, a_ref.shape)
        d_ref[...] = jnp.zeros_like(d_ref)

    for sub in range(per):
        for q, t in enumerate(blocks):

            @pl.when(place[q] == step * per + sub)
            def _():
                here = pl.ds(sub * rows, rows)
                d_ref[step * per + sub] = jnp.sum(src[here, :].astype(F32) * t[...].astype(F32), axis=1, keepdims=True)

    tgt = tgt_out[0]
    lane = lax.broadcasted_iota(jnp.int32, (PART, 128), 1)
    column = lax.broadcasted_iota(jnp.int32, (PART, 4 * rows), 1)
    line = lax.broadcasted_iota(jnp.int32, (PART, 1), 0)
    none = jnp.int32(-(1 << 20))
    parts = []
    for first in range(0, src.shape[0], PART):
        ats, ds = [], []
        for sub in range(PART // rows):
            k = step * per + first // rows + sub
            at = none
            for q in range(4):
                at = jnp.where(place[q] == k, (q - sub) * rows, at)
            ats.append(at)
            ds.append(d_ref[k])
        hole = line + jnp.where(line < rows, ats[0], ats[1])
        here = pl.ds(first, PART)
        s = dot_f32(src[here, :], tgt, ((1,), (1,)))
        s = jnp.where(column == hole, NEG, s)
        top = jnp.max(s, axis=1, keepdims=True)
        e = jnp.exp(s - top)
        total = jnp.sum(e, axis=1, keepdims=True)
        e_out[0, here, :] = e.astype(BF)
        part = jnp.where(lane == 1, total, jnp.where(lane == 2, jnp.concatenate(ds, axis=0), a_ref[0:1, :]))
        parts.append(jnp.where(lane == 0, top, part))
    stat_out[...] = jnp.transpose(jnp.concatenate(parts, axis=0))[0:8, :]


def score_call(place, src, blocks, n, so_far):
    rows, width = blocks[0].shape
    total = src.shape[0]
    cols = 4 * rows
    whole = pl.BlockSpec((rows, width), lambda i, p: (0, 0))
    so_far = list(so_far)
    return pl.pallas_call(
        score_kernel,
        out_shape=(
            pltpu.HBM((4, total, cols), BF),
            jax.ShapeDtypeStruct((8, total), F32),
            pltpu.HBM((4, cols, width), BF),
        ),
        grid_spec=pltpu.PrefetchScalarGridSpec(
            num_scalar_prefetch=1,
            grid=(total // TILE,),
            in_specs=[pl.BlockSpec((TILE, width), lambda i, p: (i, 0))]
            + [whole] * 4
            + [pl.BlockSpec(memory_space=pl.ANY)] * len(so_far),
            out_specs=(
                pl.BlockSpec((1, TILE, cols), lambda i, p: (n, i, 0)),
                pl.BlockSpec((8, TILE), lambda i, p: (0, i)),
                pl.BlockSpec((1, cols, width), lambda i, p: (n, 0, 0)),
            ),
            scratch_shapes=[pltpu.VMEM((total // rows, rows, 1), F32), pltpu.VMEM((8, 128), F32)],
        ),
        input_output_aliases={6: 0, 7: 2} if so_far else {},
        cost_estimate=pl.CostEstimate(
            flops=2 * total * cols * width, bytes_accessed=total * (width + cols) * 2, transcendentals=total * cols
        ),
        name="scores",
    )(place, src, *blocks, *so_far)


def source_kernel(w_ref, e_ref, tgt_ref, out):
    weights = columns_of(w_ref[...])
    total = None
    for c in range(4):
        part = dot_f32(e_ref[c], tgt_ref[c], ((1,), (0,))) * weights[:, c : c + 1]
        total = part if total is None else total + part
    out[...] = total


def source_call(weights, e_all, tgt_all):
    _, total, cols = e_all.shape
    width = tgt_all.shape[2]
    return pl.pallas_call(
        source_kernel,
        out_shape=jax.ShapeDtypeStruct((total, width), F32),
        grid=(total // PART,),
        in_specs=[
            pl.BlockSpec((8, PART), lambda i: (0, i)),
            pl.BlockSpec((4, PART, cols), lambda i: (0, i, 0)),
            pl.BlockSpec((4, cols, width), lambda i: (0, 0, 0), pipeline_mode=pl.Buffered(1)),
        ],
        out_specs=pl.BlockSpec((PART, width), lambda i: (i, 0)),
        cost_estimate=pl.CostEstimate(
            flops=8 * total * cols * width, bytes_accessed=total * (8 * cols + 4 * width), transcendentals=0
        ),
        name="source_terms",
    )(weights, e_all, tgt_all)


def finish_kernel(place, w_ref, acc, t0, t1, out):
    rows = t0.shape[1]
    weights = columns_of(w_ref[...])
    for h, t in enumerate((t0, t1)):
        here = slice(h * rows, (h + 1) * rows)
        out[here, :] = (acc[here, :] * weights[here, 0:1] + weights[here, 1:2] * t[0].astype(F32)).astype(BF)


def finish_call(place, weights, acc, tgt_all):
    total, width = acc.shape
    rows = total // 8

    def diag_spec(h):
        def index(i, p):
            at = jnp.maximum(p[2 * i + h], 0)
            return (at // 4, at % 4, 0)

        return pl.BlockSpec((1, rows, width), index)

    return pl.pallas_call(
        finish_kernel,
        out_shape=jax.ShapeDtypeStruct((total, width), BF),
        grid_spec=pltpu.PrefetchScalarGridSpec(
            num_scalar_prefetch=1,
            grid=(4,),
            in_specs=[
                pl.BlockSpec((8, 2 * rows), lambda i, p: (0, i)),
                pl.BlockSpec((2 * rows, width), lambda i, p: (i, 0)),
                diag_spec(0),
                diag_spec(1),
            ],
            out_specs=pl.BlockSpec((2 * rows, width), lambda i, p: (i, 0)),
        ),
        cost_estimate=pl.CostEstimate(flops=4 * total * width, bytes_accessed=8 * total * width, transcendentals=0),
        name="finish",
    )(place, weights, acc, tgt_all, tgt_all)


def target_kernel(place, w_ref, e_ref, src_ref, _, keep, give, acc, scaled, column):
    rows = acc.shape[0] // 4
    total = src_ref.shape[0]
    chunk = pl.program_id(0)

    @pl.when(chunk == 0)
    def _():
        for first in range(0, total, PART):
            here = slice(first, first + PART)
            column[here, :] = columns_of(w_ref[:, here])

    lane = lax.broadcasted_iota(jnp.int32, (PART, 128), 1)
    for first in range(0, total, PART):
        here = slice(first, first + PART)
        weight = jnp.sum(jnp.where(lane == chunk, column[here, :], 0.0), axis=1, keepdims=True)
        scaled[here, :] = (src_ref[here, :].astype(F32) * weight).astype(BF)
    acc[...] = dot_f32(e_ref[0], scaled[...], ((0,), (0,)))
    for q in range(4):
        at = place[chunk * 4 + q]

        @pl.when(at >= 0)
        def _():
            there = slice(q * rows, (q + 1) * rows)
            here = pl.ds(pl.multiple_of(at * rows, rows), rows)
            acc[there, :] = acc[there, :] + column[here, 4:5] * src_ref[here, :].astype(F32)

    keep[0] = acc[0 : 2 * rows, :]
    give[0] = acc[2 * rows : 4 * rows, :].astype(BF)


def target_call(place, weights, e_all, src, after):
    _, total, cols = e_all.shape
    width = src.shape[1]
    half = (4, cols // 2, width)
    half_spec = pl.BlockSpec((1, cols // 2, width), lambda i, p: (i, 0, 0))
    return pl.pallas_call(
        target_kernel,
        out_shape=(jax.ShapeDtypeStruct(half, F32), jax.ShapeDtypeStruct(half, BF)),
        grid_spec=pltpu.PrefetchScalarGridSpec(
            num_scalar_prefetch=1,
            grid=(4,),
            in_specs=[
                pl.BlockSpec((8, total), lambda i, p: (0, 0)),
                pl.BlockSpec((1, total, cols), lambda i, p: (i, 0, 0)),
                pl.BlockSpec((total, width), lambda i, p: (0, 0)),
                pl.BlockSpec(memory_space=pl.ANY),
            ],
            out_specs=(half_spec, half_spec),
            scratch_shapes=[
                pltpu.VMEM((cols, width), F32),
                pltpu.VMEM((total, width), BF),
                pltpu.VMEM((total, 128), F32),
            ],
        ),
        cost_estimate=pl.CostEstimate(
            flops=8 * total * cols * width, bytes_accessed=total * (width + 4 * cols) * 2 + cols * width * 12, transcendentals=0
        ),
        name="target_terms",
    )(place, weights, e_all, src, after)


def code_kernel(parts, hard, col, out, high):
    total = hard[...] * col[:, 0:1]
    for g in range(parts.shape[0]):
        total = total + parts[g].astype(F32)
    scaled = jnp.clip(total * col[:, 1:2], -32767.0, 32767.0)
    coded = jnp.round(scaled).astype(jnp.int32).astype(jnp.int16)
    out[...] = coded
    high[...] = coded[high.shape[0] :, :]


def line_kernel(keep, got, m1, m2, m3, _, mine, other):
    rows = mine.shape[0]
    total = keep[0] + got[0].astype(F32)
    for part in (m1, m2, m3):
        total = total + part[...].astype(F32)
    mine[...] = total[:rows, :]
    other[...] = total[rows:, :].astype(BF)


def decode_kernel(order, scale, own, side, far1, far2, far3, pairs1, pairs2, pairs3, far_side, out):
    step = pl.program_id(0)
    half = own.shape[0] // 2
    far, pairs = (None, far1, far2, far3), (None, pairs1, pairs2, pairs3)
    for dx in range(4):
        for dy in range(2):

            @pl.when(step == dx * 2 + dy)
            def _():
                if dx == 0:
                    whole = (own if dy == 0 else side)[...]
                    out[...] = whole.astype(jnp.int32).astype(F32) * scale[...]
                else:
                    low = pairs[dx][dy]
                    high = far[dx][...] if dy == 0 else far_side[dx - 1]
                    out[0:half, :] = low.astype(jnp.int32).astype(F32) * scale[0:half, :]
                    out[half:, :] = high.astype(jnp.int32).astype(F32) * scale[half:, :]


def decode_call(order, scale, pieces):
    rows, width = pieces[0].shape
    total = scale.shape[0]
    return pl.pallas_call(
        decode_kernel,
        out_shape=jax.ShapeDtypeStruct((total, width), F32),
        grid_spec=pltpu.PrefetchScalarGridSpec(
            num_scalar_prefetch=1,
            grid=(total // rows,),
            in_specs=[pl.BlockSpec((rows, 1), lambda i, p: (p[i], 0))]
            + [pl.BlockSpec(x.shape, lambda i, p, n=x.ndim: (0,) * n) for x in pieces],
            out_specs=pl.BlockSpec((rows, width), lambda i, p: (p[i], 0)),
        ),
        cost_estimate=pl.CostEstimate(flops=total * width, bytes_accessed=total * width * 6, transcendentals=0),
        name="decode",
    )(order, scale, *pieces)


def shards(source_emb, target_emb, hard_pool, hard_index, language, margin):
    total, width = source_emb.shape
    rows = target_emb.shape[0]
    blk, grp = lax.axis_index("blk"), lax.axis_index("grp")
    owners = 128
    cap = max(2, (2 * rows + owners - 1) // owners)
    slots = owners * cap
    z, y, c = blk // 4, (blk // 2) % 2, blk % 2

    start = grp * rows
    own_index = lax.dynamic_slice_in_dim(hard_index, start, rows, 0)
    own_source = lax.dynamic_slice_in_dim(source_emb, start, rows, 0)
    owner, pool_row = own_index // rows, own_index % rows
    position = jnp.arange(rows, dtype=jnp.int32)
    same = (owner[:, None] == owner[None, :]) & (position[None, :] < position[:, None])
    slot = owner * cap + jnp.sum(same.astype(jnp.int32), axis=1)
    at_slot = slot[:, None] == jnp.arange(slots, dtype=jnp.int32)[None, :]
    requests = jnp.sum(jnp.where(at_slot, pool_row[:, None] + 1, 0), axis=0) - 1
    wanted = lax.all_to_all(requests.reshape(owners, cap), ("grp", "blk"), 0, 0, tiled=True)
    lang_match = language[:, None] == jnp.arange(margin.shape[0], dtype=jnp.int32)[None, :]
    margin_row = jnp.sum(jnp.where(lang_match, margin[None, :], 0.0), axis=1)

    have = {(0, 0, 0): target_emb}
    have[0, 1, 0] = hop_blk(target_emb, 0, 1, 0)
    for dz in (1, 3, 2):
        have[dz, 0, 0] = hop_blk(target_emb, -dz, 0, 0)
    for dz in (1, 3, 2):
        have[dz, 1, 0] = hop_blk(have[0, 1, 0], -dz, 0, 0)
    for dz, dy in [pair for chunk in CHUNKS for pair in chunk]:
        have[dz, dy, 1] = hop_blk(have[dz, dy, 0], 0, 0, 1)

    holds = grp == blk // 2
    place = {}
    for dz in range(4):
        for dy in range(2):
            for dc in range(2):
                zz = (z + dz) % 4
                k = (zz % 2) * 4 + (y ^ dy) * 2 + (c ^ dc)
                place[dz, dy, dc] = jnp.where(holds & (zz // 2 == c), k, -1)
    order = [[(dz, dy, dc) for dc in (0, 1) for dz, dy in chunk] for chunk in CHUNKS]
    places = [jnp.stack([place[key] for key in chunk]) for chunk in order]
    flat = jnp.concatenate(places)
    found = flat[None, :] == jnp.arange(8, dtype=jnp.int32)[:, None]
    where_is = jnp.sum(jnp.where(found, jnp.arange(16, dtype=jnp.int32)[None, :] + 1, 0), axis=1) - 1
    where_is = jnp.where(where_is < 0, -4, where_is)

    stats, so_far = [], ()

    def add_chunk(n):
        nonlocal so_far
        e, stat, tgt = score_call(places[n], source_emb, [have[key] for key in order[n]], n, so_far)
        so_far = (e, tgt)
        stats.append(stat)

    add_chunk(0)
    wanted, stats[0] = lax.optimization_barrier((wanted, stats[0]))
    serve = (wanted.reshape(slots)[:, None] == position[None, :]).astype(BF)
    served = dot_f32(serve, hard_pool, ((1,), (0,))).astype(BF).reshape(owners, cap, width)
    served, places[1] = lax.optimization_barrier((served, places[1]))
    fetched = lax.all_to_all(served, ("grp", "blk"), 0, 0, tiled=True).reshape(slots, width)
    add_chunk(1)
    add_chunk(2)
    fetched, stats[2] = lax.optimization_barrier((fetched, stats[2]))
    pick = at_slot.astype(BF)
    hard_rows = dot_f32(pick, fetched, ((1,), (0,)))
    hard_score = jnp.sum(own_source.astype(F32) * hard_rows, axis=1)
    add_chunk(3)

    tops = jnp.stack([stat[0] for stat in stats])
    sums = jnp.stack([stat[1] for stat in stats])
    diag = sum(stat[2] for stat in stats)
    reach = jnp.maximum(jnp.max(jnp.stack([stat[3] for stat in stats]), axis=0), jnp.max(jnp.abs(hard_rows)))
    pos = jnp.where(holds, diag - margin_row, 0.0)
    hard_all = lax.dynamic_update_slice_in_dim(jnp.full((total,), LOW, F32), hard_score, start, 0)
    soft_top = jnp.max(tops, axis=0)
    top = jnp.maximum(soft_top, hard_all)
    off = jnp.sum(sums * jnp.exp(tops - top), axis=0) + jnp.exp(hard_all - top)
    mine = jnp.stack([top, off, pos, reach])
    everyone = lax.all_to_all(jnp.broadcast_to(mine[None], (8, 4, total)), "grp", 0, 0, tiled=True)
    pad = jnp.zeros((4, total), F32)
    source_acc = source_call(jnp.concatenate([jnp.exp(tops - soft_top), pad]), *so_far)
    everyone, source_acc = lax.optimization_barrier((everyone, source_acc))
    pos = jnp.sum(everyone[:, 2], axis=0)
    reach = jnp.max(everyone[:, 3], axis=0)
    top = jnp.maximum(jnp.max(everyone[:, 0], axis=0), pos)
    off = jnp.sum(everyone[:, 1] * jnp.exp(everyone[:, 0] - top), axis=0)
    log_total = top + jnp.log(off + jnp.exp(pos - top))
    row_loss = log_total - pos
    less = jnp.exp(pos - log_total) - 1.0
    diag_weight = jnp.where(holds, less, 0.0)

    x_at, y_at = grp // 2, grp % 2
    finish_rows = jnp.stack([jnp.exp(soft_top - log_total), diag_weight] + [jnp.zeros((total,), F32)] * 6)
    source_part = finish_call(where_is, finish_rows, source_acc, so_far[1])
    token = hop_blk(source_part[:16, :128], 0, 0, 1)
    source_parts = lax.all_to_all(source_part.reshape(8, rows, width), "grp", 0, 0, tiled=True)
    own_total = lax.dynamic_slice_in_dim(log_total, start, rows, 0)
    hard_prob = jnp.exp(hard_score - own_total)
    mass = jnp.abs(less) + off * jnp.exp(top - log_total)
    bound = jnp.maximum(1.01 * reach * mass, 1e-30)
    own_bound = lax.dynamic_slice_in_dim(bound, start, rows, 0)
    col = jnp.stack([hard_prob, 32767.0 / own_bound], axis=1)
    half = rows // 2
    coded, coded_high = pl.pallas_call(
        code_kernel,
        out_shape=(jax.ShapeDtypeStruct((rows, width), jnp.int16), jax.ShapeDtypeStruct((half, width), jnp.int16)),
        cost_estimate=pl.CostEstimate(flops=10 * rows * width, bytes_accessed=22 * rows * width, transcendentals=0),
        name="code",
    )(source_parts, hard_rows, col)
    hard_gate = hard_prob + 0.0 * coded[0, 0].astype(F32)
    side = hop_grp(coded, 0, 1)
    far = [hop_grp(coded_high, -dx, 0) for dx in (1, 2, 3)]
    near = jnp.stack([coded[:half], side[:half]])
    pairs = [hop_grp(near, -dx, 0) for dx in (1, 2, 3)]
    far_side = hop_grp(jnp.stack(far), 0, 1)
    blocks = jnp.stack([((x_at + dx) % 4) * 2 + (y_at ^ dy) for dx in range(4) for dy in range(2)])
    source_grad = decode_call(
        blocks, (bound * (1.0 / 32767.0))[:, None], [coded, side, *far, *pairs, far_side]
    )

    weights = jnp.concatenate([jnp.exp(tops - log_total), diag_weight[None], jnp.zeros((3, total), F32)])
    keep, give = target_call(flat, weights, so_far[0], source_emb, token)
    got = hop_blk(give, 0, 0, 1)
    moved = []
    for n in (1, 2, 3):
        dz = CHUNKS[n][0][0]
        moved.append(hop_blk((keep[n] + got[n].astype(F32)).astype(BF), dz, 0, 0))
    whole = [pl.BlockSpec((1, 2 * rows, width), lambda i: (0, 0, 0))] * 2
    whole += [pl.BlockSpec((2 * rows, width), lambda i: (0, 0))] * 3 + [pl.BlockSpec(memory_space=pl.ANY)]
    mine, other = pl.pallas_call(
        line_kernel,
        out_shape=(jax.ShapeDtypeStruct((rows, width), F32), jax.ShapeDtypeStruct((rows, width), BF)),
        grid=(1,),
        in_specs=whole,
        out_specs=[pl.BlockSpec((rows, width), lambda i: (0, 0))] * 2,
        cost_estimate=pl.CostEstimate(flops=10 * rows * width, bytes_accessed=30 * rows * width, transcendentals=0),
        name="lines",
    )(keep, got, *moved, coded)
    target_grad = mine + hop_blk(other, 0, 1, 0).astype(F32)

    contribution = (hard_gate[:, None] * own_source.astype(F32)).astype(BF)
    outgoing = dot_f32(pick, contribution, ((0,), (0,))).astype(BF).reshape(owners, cap, width)
    incoming = lax.all_to_all(outgoing, ("grp", "blk"), 0, 0, tiled=True).reshape(slots, width)
    pool_grad = dot_f32(serve, incoming, ((0,), (0,)))
    return (row_loss, source_grad, target_grad, pool_grad)


def solution(mesh):
    in_specs = (P("blk", None), P(("grp", "blk"), None), P(("grp", "blk"), None), P("blk"), P("blk"), P())
    out_specs = (P("blk"), P("blk", None), P(("grp", "blk"), None), P(("grp", "blk"), None))
    return jax.shard_map(shards, mesh=mesh, in_specs=in_specs, out_specs=out_specs, check_vma=False)
```

```python
import jax
import jax.numpy as jnp
from jax import lax
from jax.experimental import pallas as pl
from jax.experimental.pallas import tpu as pltpu
from jax.sharding import PartitionSpec as P

BF, F32 = jnp.bfloat16, jnp.float32
NEG = -1e30
LOW = -3e38
TILE = 768
PART = 384
CHUNKS = tuple(((dz, 0), (dz, 1)) for dz in (0, 1, 3, 2))


def hop_blk(value, dz, dy, dc):
    route = []
    for i in range(16):
        z, y, c = i // 4, (i // 2) % 2, i % 2
        route.append((i, ((z + dz) % 4) * 4 + (y ^ dy) * 2 + (c ^ dc)))
    return lax.ppermute(value, "blk", route)


def hop_grp(value, dx, dy):
    return lax.ppermute(value, "grp", [(i, ((i // 2 + dx) % 4) * 2 + ((i % 2) ^ dy)) for i in range(8)])


def dot_f32(a, b, dims):
    return lax.dot_general(a, b, (dims, ((), ())), preferred_element_type=F32)


def columns_of(rows):
    pad = jnp.zeros((120, rows.shape[1]), F32)
    return jnp.transpose(jnp.concatenate([rows, pad], axis=0))


def score_kernel(place, src, near_pair, away_pair, *refs):
    e_out, stat_out, tgt_out, a_ref = refs[-4:]
    half = near_pair.shape[0]
    rows = half // 2
    step = pl.program_id(0)

    @pl.when(step == 0)
    def _():
        top = jnp.zeros((1, 1), F32)
        for q, pair in enumerate((near_pair, away_pair)):
            block = pair[...]
            tgt_out[0, q * half : (q + 1) * half, :] = block
            top = jnp.maximum(top, jnp.max(jnp.abs(block).astype(F32), keepdims=True))
        a_ref[...] = jnp.broadcast_to(top, a_ref.shape)

    tgt = tgt_out[0]
    lane = lax.broadcasted_iota(jnp.int32, (PART, 128), 1)
    column = lax.broadcasted_iota(jnp.int32, (PART, 2 * half), 1)
    line = lax.broadcasted_iota(jnp.int32, (PART, 1), 0)
    parts = []
    for first in range(0, src.shape[0], PART):
        ats = []
        for sub in range(2):
            k = step * (src.shape[0] // rows) + first // rows + sub
            at = jnp.int32(-(1 << 20))
            for q in range(4):
                at = jnp.where(place[q] == k, (q - sub) * rows, at)
            ats.append(at)
        hole = line + jnp.where(line < rows, ats[0], ats[1])
        here = pl.ds(first, PART)
        s = dot_f32(src[here, :], tgt, ((1,), (1,)))
        s = jnp.where(column == hole, NEG, s)
        top = jnp.max(s, axis=1, keepdims=True)
        e = jnp.exp(s - top)
        total = jnp.sum(e, axis=1, keepdims=True)
        e_out[0, here, :] = e.astype(BF)
        parts.append(jnp.where(lane == 0, top, jnp.where(lane == 1, total, a_ref[0:1, :])))
    stat_out[...] = jnp.transpose(jnp.concatenate(parts, axis=0))[0:8, :]


def score_call(place, src, near_pair, away_pair, n, so_far):
    half, width = near_pair.shape
    total = src.shape[0]
    cols = 2 * half
    so_far = list(so_far)
    vmem = pl.BlockSpec((half, width), lambda i, p: (0, 0))
    return pl.pallas_call(
        score_kernel,
        out_shape=(
            pltpu.HBM((4, total, cols), BF),
            jax.ShapeDtypeStruct((8, total), F32),
            pltpu.HBM((4, cols, width), BF),
        ),
        grid_spec=pltpu.PrefetchScalarGridSpec(
            num_scalar_prefetch=1,
            grid=(total // TILE,),
            in_specs=[pl.BlockSpec((TILE, width), lambda i, p: (i, 0)), vmem, vmem]
            + [pl.BlockSpec(memory_space=pl.ANY)] * len(so_far),
            out_specs=(
                pl.BlockSpec((1, TILE, cols), lambda i, p: (n, i, 0)),
                pl.BlockSpec((8, TILE), lambda i, p: (0, i)),
                pl.BlockSpec((1, cols, width), lambda i, p: (n, 0, 0)),
            ),
            scratch_shapes=[pltpu.VMEM((8, 128), F32)],
        ),
        input_output_aliases={4: 0, 5: 2} if so_far else {},
        compiler_params=pltpu.CompilerParams(vmem_limit_bytes=24 << 20),
        cost_estimate=pl.CostEstimate(
            flops=2 * total * cols * width, bytes_accessed=total * (width + cols) * 2, transcendentals=total * cols
        ),
        name="scores",
    )(place, src, near_pair, away_pair, *so_far)


def source_kernel(w_ref, e_ref, tgt_ref, out, acc):
    c, i = pl.program_id(0), pl.program_id(1)
    lane = lax.broadcasted_iota(jnp.int32, (PART, 128), 1)
    weight = jnp.sum(jnp.where(lane == c, columns_of(w_ref[...]), 0.0), axis=1, keepdims=True)
    part = dot_f32(e_ref[0], tgt_ref[0], ((1,), (0,))) * weight
    total = jnp.where(c == 0, 0.0, acc[i]) + part
    acc[i] = total
    out[...] = total.astype(BF)


def source_call(weights, e_all, tgt_all):
    _, total, cols = e_all.shape
    width = tgt_all.shape[2]
    return pl.pallas_call(
        source_kernel,
        out_shape=jax.ShapeDtypeStruct((total, width), BF),
        grid=(4, total // PART),
        in_specs=[
            pl.BlockSpec((8, PART), lambda c, i: (0, i)),
            pl.BlockSpec((1, PART, cols), lambda c, i: (c, i, 0)),
            pl.BlockSpec((1, cols, width), lambda c, i: (c, 0, 0)),
        ],
        out_specs=pl.BlockSpec((PART, width), lambda c, i: (jnp.where(c == 3, i, 0), 0)),
        scratch_shapes=[pltpu.VMEM((total // PART, PART, width), F32)],
        cost_estimate=pl.CostEstimate(
            flops=8 * total * cols * width, bytes_accessed=total * (8 * cols + 2 * width), transcendentals=0
        ),
        name="source_terms",
    )(weights, e_all, tgt_all)


def target_kernel(place, w_ref, e_ref, src_ref, _, keep, give, acc, scaled, column):
    rows = acc.shape[0] // 4
    total = src_ref.shape[0]
    chunk = pl.program_id(0)

    @pl.when(chunk == 0)
    def _():
        for first in range(0, total, PART):
            here = slice(first, first + PART)
            column[here, :] = columns_of(w_ref[:, here])

    lane = lax.broadcasted_iota(jnp.int32, (PART, 128), 1)
    for first in range(0, total, PART):
        here = slice(first, first + PART)
        weight = jnp.sum(jnp.where(lane == chunk, column[here, :], 0.0), axis=1, keepdims=True)
        scaled[here, :] = (src_ref[here, :].astype(F32) * weight).astype(BF)
    acc[...] = dot_f32(e_ref[0], scaled[...], ((0,), (0,)))
    for q in range(4):
        at = place[chunk * 4 + q]

        @pl.when(at >= 0)
        def _():
            there = slice(q * rows, (q + 1) * rows)
            here = pl.ds(pl.multiple_of(at * rows, rows), rows)
            acc[there, :] = acc[there, :] + column[here, 4:5] * src_ref[here, :].astype(F32)

    keep[0] = acc[0 : 2 * rows, :]
    give[0] = acc[2 * rows : 4 * rows, :].astype(BF)


def target_call(place, weights, e_all, src, after):
    _, total, cols = e_all.shape
    width = src.shape[1]
    half = (4, cols // 2, width)
    half_spec = pl.BlockSpec((1, cols // 2, width), lambda i, p: (i, 0, 0))
    return pl.pallas_call(
        target_kernel,
        out_shape=(jax.ShapeDtypeStruct(half, F32), jax.ShapeDtypeStruct(half, BF)),
        grid_spec=pltpu.PrefetchScalarGridSpec(
            num_scalar_prefetch=1,
            grid=(4,),
            in_specs=[
                pl.BlockSpec((8, total), lambda i, p: (0, 0)),
                pl.BlockSpec((1, total, cols), lambda i, p: (i, 0, 0)),
                pl.BlockSpec((total, width), lambda i, p: (0, 0)),
                pl.BlockSpec(memory_space=pl.ANY),
            ],
            out_specs=(half_spec, half_spec),
            scratch_shapes=[
                pltpu.VMEM((cols, width), F32),
                pltpu.VMEM((total, width), BF),
                pltpu.VMEM((total, 128), F32),
            ],
        ),
        cost_estimate=pl.CostEstimate(
            flops=8 * total * cols * width, bytes_accessed=total * (width + 4 * cols) * 2 + cols * width * 12, transcendentals=0
        ),
        name="target_terms",
    )(place, weights, e_all, src, after)


def code_kernel(parts, hard, tgt, col, _, out, high):
    total = hard[...] * col[:, 0:1] + tgt[...].astype(F32) * col[:, 1:2]
    for g in range(parts.shape[0]):
        total = total + parts[g].astype(F32) * col[:, 3 + g : 4 + g]
    scaled = jnp.clip(total * col[:, 2:3], -32767.0, 32767.0)
    coded = jnp.round(scaled).astype(jnp.int32).astype(jnp.int16)
    out[...] = coded
    high[...] = coded


def line_kernel(keep, got, m1, m2, m3, mine, other):
    rows = mine.shape[0]
    total = keep[0] + got[0].astype(F32)
    for part in (m1, m2, m3):
        total = total + part[...].astype(F32)
    mine[...] = total[:rows, :]
    other[...] = total[rows:, :].astype(BF)


def decode_kernel(order, scale, own, side, far1, far2, far3, pairs1, pairs2, pairs3, far_side, out):
    step = pl.program_id(0)
    half = own.shape[0] // 2
    far, pairs = (None, far1, far2, far3), (None, pairs1, pairs2, pairs3)
    for dx in range(4):
        for dy in range(2):

            @pl.when(step == dx * 2 + dy)
            def _():
                if dx == 0:
                    whole = (own if dy == 0 else side)[...]
                    out[...] = whole.astype(jnp.int32).astype(F32) * scale[...]
                else:
                    low = pairs[dx][dy]
                    high = far[dx][...] if dy == 0 else far_side[dx - 1]
                    out[0:half, :] = low.astype(jnp.int32).astype(F32) * scale[0:half, :]
                    out[half:, :] = high.astype(jnp.int32).astype(F32) * scale[half:, :]


def decode_call(order, scale, pieces):
    rows, width = pieces[0].shape
    total = scale.shape[0]
    return pl.pallas_call(
        decode_kernel,
        out_shape=jax.ShapeDtypeStruct((total, width), F32),
        grid_spec=pltpu.PrefetchScalarGridSpec(
            num_scalar_prefetch=1,
            grid=(total // rows,),
            in_specs=[pl.BlockSpec((rows, 1), lambda i, p: (p[i], 0))]
            + [pl.BlockSpec(x.shape, lambda i, p, n=x.ndim: (0,) * n) for x in pieces],
            out_specs=pl.BlockSpec((rows, width), lambda i, p: (p[i], 0)),
        ),
        cost_estimate=pl.CostEstimate(flops=total * width, bytes_accessed=total * width * 6, transcendentals=0),
        name="decode",
    )(order, scale, *pieces)


def shards(source_emb, target_emb, hard_pool, hard_index, language, margin):
    total, width = source_emb.shape
    rows = target_emb.shape[0]
    blk, grp = lax.axis_index("blk"), lax.axis_index("grp")
    owners = 128
    cap = max(2, (2 * rows + owners - 1) // owners)
    slots = owners * cap
    z, y, c = blk // 4, (blk // 2) % 2, blk % 2

    start = grp * rows
    own_index = lax.dynamic_slice_in_dim(hard_index, start, rows, 0)
    own_source = lax.dynamic_slice_in_dim(source_emb, start, rows, 0)
    owner, pool_row = own_index // rows, own_index % rows
    position = jnp.arange(rows, dtype=jnp.int32)
    same = (owner[:, None] == owner[None, :]) & (position[None, :] < position[:, None])
    slot = owner * cap + jnp.sum(same.astype(jnp.int32), axis=1)
    at_slot = slot[:, None] == jnp.arange(slots, dtype=jnp.int32)[None, :]
    requests = jnp.sum(jnp.where(at_slot, pool_row[:, None] + 1, 0), axis=0) - 1
    wanted = lax.all_to_all(requests.reshape(owners, cap), ("grp", "blk"), 0, 0, tiled=True)
    lang_match = language[:, None] == jnp.arange(margin.shape[0], dtype=jnp.int32)[None, :]
    margin_row = jnp.sum(jnp.where(lang_match, margin[None, :], 0.0), axis=1)

    across = hop_blk(target_emb, 0, 1, 0)
    line = {0: target_emb, **{dz: hop_blk(target_emb, -dz, 0, 0) for dz in (1, 3, 2)}}
    lines = {0: across, **{dz: hop_blk(across, -dz, 0, 0) for dz in (1, 3, 2)}}
    near = {dz: jnp.concatenate([line[dz], lines[dz]]) for dz in (0, 1, 3, 2)}
    away = {dz: hop_blk(near[dz], 0, 0, 1) for dz in (0, 1, 3, 2)}

    own_target = lax.ppermute(
        target_emb, ("grp", "blk"), [(16 * i + j, (j % 8) * 16 + 2 * i + j // 8) for i in range(8) for j in range(16)]
    )

    holds = grp == blk // 2
    place = {}
    for dz in range(4):
        for dy in range(2):
            for dc in range(2):
                zz = (z + dz) % 4
                k = (zz % 2) * 4 + (y ^ dy) * 2 + (c ^ dc)
                place[dz, dy, dc] = jnp.where(holds & (zz // 2 == c), k, -1)
    order = [[(dz, dy, dc) for dc in (0, 1) for dz, dy in chunk] for chunk in CHUNKS]
    places = [jnp.stack([place[key] for key in chunk]) for chunk in order]
    flat = jnp.concatenate(places)

    stats, so_far = [], ()

    def add_chunk(n):
        nonlocal so_far
        e, stat, tgt = score_call(places[n], source_emb, near[CHUNKS[n][0][0]], away[CHUNKS[n][0][0]], n, so_far)
        so_far = (e, tgt)
        stats.append(stat)

    add_chunk(0)
    wanted, stats[0] = lax.optimization_barrier((wanted, stats[0]))
    serve = (wanted.reshape(slots)[:, None] == position[None, :]).astype(BF)
    served = dot_f32(serve, hard_pool, ((1,), (0,))).astype(BF).reshape(owners, cap, width)
    served, places[1] = lax.optimization_barrier((served, places[1]))
    fetched = lax.all_to_all(served, ("grp", "blk"), 0, 0, tiled=True).reshape(slots, width)
    add_chunk(1)
    add_chunk(2)
    fetched, stats[2] = lax.optimization_barrier((fetched, stats[2]))
    pick = at_slot.astype(BF)
    hard_rows = dot_f32(pick, fetched, ((1,), (0,)))
    hard_score = jnp.sum(own_source.astype(F32) * hard_rows, axis=1)
    add_chunk(3)

    tops = jnp.stack([stat[0] for stat in stats])
    sums = jnp.stack([stat[1] for stat in stats])
    reach = jnp.maximum(jnp.max(jnp.stack([stat[2] for stat in stats]), axis=0), jnp.max(jnp.abs(hard_rows)))
    own_margin = lax.dynamic_slice_in_dim(margin_row, start, rows, 0)
    own_pos = jnp.sum(own_source.astype(F32) * own_target.astype(F32), axis=1) - own_margin
    pos = lax.dynamic_update_slice_in_dim(jnp.zeros((total,), F32), own_pos, start, 0)
    hard_all = lax.dynamic_update_slice_in_dim(jnp.full((total,), LOW, F32), hard_score, start, 0)
    soft_top = jnp.max(tops, axis=0)
    soft = jnp.sum(sums * jnp.exp(tops - soft_top), axis=0)
    mine = jnp.stack([soft_top, soft, pos, hard_all, reach] + [jnp.zeros((total,), F32)] * 3)
    everyone = lax.all_to_all(jnp.broadcast_to(mine[None], (8, 8, total)), "grp", 0, 0, tiled=True)
    source_part = source_call(jnp.concatenate([jnp.exp(tops - soft_top), jnp.zeros((4, total), F32)]), *so_far)
    everyone, source_part = lax.optimization_barrier((everyone, source_part))
    source_parts = lax.all_to_all(source_part.reshape(8, rows, width), "grp", 0, 0, tiled=True)
    token = hop_blk(source_part[:16, :128], 0, 0, 1)
    pos = jnp.sum(everyone[:, 2], axis=0)
    hard_all = jnp.max(everyone[:, 3], axis=0)
    reach = jnp.max(everyone[:, 4], axis=0)
    top = jnp.maximum(jnp.max(everyone[:, 0], axis=0), jnp.maximum(pos, hard_all))
    off = jnp.sum(everyone[:, 1] * jnp.exp(everyone[:, 0] - top), axis=0) + jnp.exp(hard_all - top)
    log_total = top + jnp.log(off + jnp.exp(pos - top))
    row_loss = log_total - pos
    less = jnp.exp(pos - log_total) - 1.0
    diag_weight = jnp.where(holds, less, 0.0)

    x_at, y_at = grp // 2, grp % 2
    mass = jnp.abs(less) + off * jnp.exp(top - log_total)
    bound = jnp.maximum(1.01 * reach * mass, 1e-30)
    col = jnp.concatenate(
        [jnp.stack([jnp.exp(hard_all - log_total), less, 32767.0 / bound]), jnp.exp(everyone[:, 0] - log_total[None])]
    )
    col = lax.dynamic_slice_in_dim(col, start, rows, 1)
    hard_prob = col[0]
    col = jnp.transpose(col)
    half = rows // 2

    weights = jnp.concatenate([jnp.exp(tops - log_total), diag_weight[None], jnp.zeros((3, total), F32)])
    keep, give = target_call(flat, weights, so_far[0], source_emb, token)
    got = hop_blk(give, 0, 0, 1)
    moved = []
    for n in (1, 2, 3):
        dz = CHUNKS[n][0][0]
        moved.append(hop_blk((keep[n] + got[n].astype(F32)).astype(BF), dz, 0, 0))
    whole = [pl.BlockSpec((1, 2 * rows, width), lambda i: (0, 0, 0))] * 2
    whole += [pl.BlockSpec((2 * rows, width), lambda i: (0, 0))] * 3
    mine, other = pl.pallas_call(
        line_kernel,
        out_shape=(jax.ShapeDtypeStruct((rows, width), F32), jax.ShapeDtypeStruct((rows, width), BF)),
        grid=(1,),
        in_specs=whole,
        out_specs=[pl.BlockSpec((rows, width), lambda i: (0, 0))] * 2,
        cost_estimate=pl.CostEstimate(flops=10 * rows * width, bytes_accessed=30 * rows * width, transcendentals=0),
        name="lines",
    )(keep, got, *moved)
    target_grad = mine + hop_blk(other, 0, 1, 0).astype(F32)

    coded, coded_high = pl.pallas_call(
        code_kernel,
        out_shape=(jax.ShapeDtypeStruct((rows, width), jnp.int16), jax.ShapeDtypeStruct((half, width), jnp.int16)),
        grid=(2,),
        in_specs=[
            pl.BlockSpec((8, half, width), lambda i: (0, i, 0)),
            pl.BlockSpec((half, width), lambda i: (i, 0)),
            pl.BlockSpec((half, width), lambda i: (i, 0)),
            pl.BlockSpec((half, col.shape[1]), lambda i: (i, 0)),
            pl.BlockSpec(memory_space=pl.ANY),
        ],
        out_specs=(pl.BlockSpec((half, width), lambda i: (i, 0)), pl.BlockSpec((half, width), lambda i: (0, 0))),
        cost_estimate=pl.CostEstimate(flops=10 * rows * width, bytes_accessed=22 * rows * width, transcendentals=0),
        name="code",
    )(source_parts, hard_rows, own_target, col, other)
    hard_gate = hard_prob + 0.0 * coded[0, 0].astype(F32)
    side = hop_grp(coded, 0, 1)
    far = [hop_grp(coded_high, -dx, 0) for dx in (1, 2, 3)]
    low = jnp.stack([coded[:half], side[:half]])
    pairs = [hop_grp(low, -dx, 0) for dx in (1, 2, 3)]
    far_side = hop_grp(jnp.stack(far), 0, 1)
    blocks = jnp.stack([((x_at + dx) % 4) * 2 + (y_at ^ dy) for dx in range(4) for dy in range(2)])
    source_grad = decode_call(
        blocks, (bound * (1.0 / 32767.0))[:, None], [coded, side, *far, *pairs, far_side]
    )

    contribution = (hard_gate[:, None] * own_source.astype(F32)).astype(BF)
    outgoing = dot_f32(pick, contribution, ((0,), (0,))).astype(BF).reshape(owners, cap, width)
    incoming = lax.all_to_all(outgoing, ("grp", "blk"), 0, 0, tiled=True).reshape(slots, width)
    pool_grad = dot_f32(serve, incoming, ((0,), (0,)))
    return (row_loss, source_grad, target_grad, pool_grad)


def solution(mesh):
    in_specs = (P("blk", None), P(("grp", "blk"), None), P(("grp", "blk"), None), P("blk"), P("blk"), P())
    out_specs = (P("blk"), P("blk", None), P(("grp", "blk"), None), P(("grp", "blk"), None))
    return jax.shard_map(shards, mesh=mesh, in_specs=in_specs, out_specs=out_specs, check_vma=False)
```

```python
import jax
import jax.numpy as jnp
from jax import lax
from jax.experimental import pallas as pl
from jax.experimental.pallas import tpu as pltpu
from jax.sharding import PartitionSpec as P

BF, F32 = jnp.bfloat16, jnp.float32
NEG = -1e30
LOW = -3e38
TILE = 768
PART = 384
CHUNKS = tuple(((dz, 0), (dz, 1)) for dz in (0, 1, 3, 2))


def hop_blk(value, dz, dy, dc):
    route = []
    for i in range(16):
        z, y, c = i // 4, (i // 2) % 2, i % 2
        route.append((i, ((z + dz) % 4) * 4 + (y ^ dy) * 2 + (c ^ dc)))
    return lax.ppermute(value, "blk", route)


def hop_grp(value, dx, dy):
    return lax.ppermute(value, "grp", [(i, ((i // 2 + dx) % 4) * 2 + ((i % 2) ^ dy)) for i in range(8)])


def dot_f32(a, b, dims):
    return lax.dot_general(a, b, (dims, ((), ())), preferred_element_type=F32)


def columns_of(rows):
    pad = jnp.zeros((120, rows.shape[1]), F32)
    return jnp.transpose(jnp.concatenate([rows, pad], axis=0))


def score_kernel(place, src, near_pair, away_pair, *refs):
    e_out, stat_out, tgt_out, a_ref = refs[-4:]
    half = near_pair.shape[0]
    rows = half // 2
    step = pl.program_id(0)

    @pl.when(step == 0)
    def _():
        top = jnp.zeros((1, 1), F32)
        for q, pair in enumerate((near_pair, away_pair)):
            block = pair[...]
            tgt_out[0, q * half : (q + 1) * half, :] = block
            top = jnp.maximum(top, jnp.max(jnp.abs(block).astype(F32), keepdims=True))
        a_ref[...] = jnp.broadcast_to(top, a_ref.shape)

    tgt = tgt_out[0]
    lane = lax.broadcasted_iota(jnp.int32, (PART, 128), 1)
    column = lax.broadcasted_iota(jnp.int32, (PART, 2 * half), 1)
    line = lax.broadcasted_iota(jnp.int32, (PART, 1), 0)
    parts = []
    for first in range(0, src.shape[0], PART):
        ats = []
        for sub in range(2):
            k = step * (src.shape[0] // rows) + first // rows + sub
            at = jnp.int32(-(1 << 20))
            for q in range(4):
                at = jnp.where(place[q] == k, (q - sub) * rows, at)
            ats.append(at)
        hole = line + jnp.where(line < rows, ats[0], ats[1])
        here = pl.ds(first, PART)
        s = dot_f32(src[here, :], tgt, ((1,), (1,)))
        s = jnp.where(column == hole, NEG, s)
        top = jnp.max(s, axis=1, keepdims=True)
        e = jnp.exp(s - top)
        total = jnp.sum(e, axis=1, keepdims=True)
        e_out[0, here, :] = e.astype(BF)
        parts.append(jnp.where(lane == 0, top, jnp.where(lane == 1, total, a_ref[0:1, :])))
    stat_out[...] = jnp.transpose(jnp.concatenate(parts, axis=0))[0:8, :]


def score_call(place, src, near_pair, away_pair, n, so_far):
    half, width = near_pair.shape
    total = src.shape[0]
    cols = 2 * half
    so_far = list(so_far)
    vmem = pl.BlockSpec((half, width), lambda i, p: (0, 0))
    return pl.pallas_call(
        score_kernel,
        out_shape=(
            pltpu.HBM((4, total, cols), BF),
            jax.ShapeDtypeStruct((8, total), F32),
            pltpu.HBM((4, cols, width), BF),
        ),
        grid_spec=pltpu.PrefetchScalarGridSpec(
            num_scalar_prefetch=1,
            grid=(total // TILE,),
            in_specs=[pl.BlockSpec((TILE, width), lambda i, p: (i, 0)), vmem, vmem]
            + [pl.BlockSpec(memory_space=pl.ANY)] * len(so_far),
            out_specs=(
                pl.BlockSpec((1, TILE, cols), lambda i, p: (n, i, 0)),
                pl.BlockSpec((8, TILE), lambda i, p: (0, i)),
                pl.BlockSpec((1, cols, width), lambda i, p: (n, 0, 0)),
            ),
            scratch_shapes=[pltpu.VMEM((8, 128), F32)],
        ),
        input_output_aliases={4: 0, 5: 2} if so_far else {},
        compiler_params=pltpu.CompilerParams(vmem_limit_bytes=24 << 20),
        cost_estimate=pl.CostEstimate(
            flops=2 * total * cols * width, bytes_accessed=total * (width + cols) * 2, transcendentals=total * cols
        ),
        name="scores",
    )(place, src, near_pair, away_pair, *so_far)


def source_kernel(w_ref, e_ref, tgt_ref, out):
    weights = columns_of(w_ref[...])
    total = None
    for c in range(4):
        part = dot_f32(e_ref[c], tgt_ref[c], ((1,), (0,))) * weights[:, c : c + 1]
        total = part if total is None else total + part
    out[...] = total.astype(BF)


def source_call(weights, e_all, tgt_all):
    _, total, cols = e_all.shape
    width = tgt_all.shape[2]
    return pl.pallas_call(
        source_kernel,
        out_shape=jax.ShapeDtypeStruct((total, width), BF),
        grid=(total // PART,),
        in_specs=[
            pl.BlockSpec((8, PART), lambda i: (0, i)),
            pl.BlockSpec((4, PART, cols), lambda i: (0, i, 0)),
            pl.BlockSpec((4, cols, width), lambda i: (0, 0, 0), pipeline_mode=pl.Buffered(1)),
        ],
        out_specs=pl.BlockSpec((PART, width), lambda i: (i, 0)),
        cost_estimate=pl.CostEstimate(
            flops=8 * total * cols * width, bytes_accessed=total * (8 * cols + 2 * width), transcendentals=0
        ),
        name="source_terms",
    )(weights, e_all, tgt_all)


def target_kernel(place, w_ref, e_ref, src_ref, _, keep, give, acc, scaled, column):
    rows = acc.shape[0] // 4
    total = src_ref.shape[0]
    chunk = pl.program_id(0)

    @pl.when(chunk == 0)
    def _():
        for first in range(0, total, PART):
            here = slice(first, first + PART)
            column[here, :] = columns_of(w_ref[:, here])

    lane = lax.broadcasted_iota(jnp.int32, (PART, 128), 1)
    for first in range(0, total, PART):
        here = slice(first, first + PART)
        weight = jnp.sum(jnp.where(lane == chunk, column[here, :], 0.0), axis=1, keepdims=True)
        scaled[here, :] = (src_ref[here, :].astype(F32) * weight).astype(BF)
    acc[...] = dot_f32(e_ref[0], scaled[...], ((0,), (0,)))
    for q in range(4):
        at = place[chunk * 4 + q]

        @pl.when(at >= 0)
        def _():
            there = slice(q * rows, (q + 1) * rows)
            here = pl.ds(pl.multiple_of(at * rows, rows), rows)
            acc[there, :] = acc[there, :] + column[here, 4:5] * src_ref[here, :].astype(F32)

    keep[0] = acc[0 : 2 * rows, :]
    give[0] = acc[2 * rows : 4 * rows, :].astype(BF)


def target_call(place, weights, e_all, src, after):
    _, total, cols = e_all.shape
    width = src.shape[1]
    half = (4, cols // 2, width)
    half_spec = pl.BlockSpec((1, cols // 2, width), lambda i, p: (i, 0, 0))
    return pl.pallas_call(
        target_kernel,
        out_shape=(jax.ShapeDtypeStruct(half, F32), jax.ShapeDtypeStruct(half, BF)),
        grid_spec=pltpu.PrefetchScalarGridSpec(
            num_scalar_prefetch=1,
            grid=(4,),
            in_specs=[
                pl.BlockSpec((8, total), lambda i, p: (0, 0)),
                pl.BlockSpec((1, total, cols), lambda i, p: (i, 0, 0)),
                pl.BlockSpec((total, width), lambda i, p: (0, 0)),
                pl.BlockSpec(memory_space=pl.ANY),
            ],
            out_specs=(half_spec, half_spec),
            scratch_shapes=[
                pltpu.VMEM((cols, width), F32),
                pltpu.VMEM((total, width), BF),
                pltpu.VMEM((total, 128), F32),
            ],
        ),
        cost_estimate=pl.CostEstimate(
            flops=8 * total * cols * width, bytes_accessed=total * (width + 4 * cols) * 2 + cols * width * 12, transcendentals=0
        ),
        name="target_terms",
    )(place, weights, e_all, src, after)


def code_kernel(parts, hard, tgt, col, *refs):
    out = refs[-1]
    total = hard[...] * col[:, 0:1] + tgt[...].astype(F32) * col[:, 1:2]
    for g in range(parts.shape[0]):
        total = total + parts[g].astype(F32) * col[:, 3 + g : 4 + g]
    scaled = jnp.clip(total * col[:, 2:3], -32767.0, 32767.0)
    coded = jnp.round(scaled).astype(jnp.int32).astype(jnp.int16)
    for g in range(parts.shape[0]):
        out[g] = coded


def code_call(parts, hard, tgt, col, after):
    groups, rows, width = parts.shape
    half = rows // 2
    return pl.pallas_call(
        code_kernel,
        out_shape=jax.ShapeDtypeStruct((groups, rows, width), jnp.int16),
        grid=(2,),
        in_specs=[
            pl.BlockSpec((groups, half, width), lambda i: (0, i, 0)),
            pl.BlockSpec((half, width), lambda i: (i, 0)),
            pl.BlockSpec((half, width), lambda i: (i, 0)),
            pl.BlockSpec((half, col.shape[1]), lambda i: (i, 0)),
        ]
        + [pl.BlockSpec(memory_space=pl.ANY)] * len(after),
        out_specs=pl.BlockSpec((groups, half, width), lambda i: (0, i, 0)),
        cost_estimate=pl.CostEstimate(flops=30 * rows * width, bytes_accessed=40 * rows * width, transcendentals=0),
        name="code",
    )(parts, hard, tgt, col, *after)


def line_kernel(keep, got, m1, m2, m3, _, mine, other):
    rows = mine.shape[0]
    total = keep[0] + got[0].astype(F32)
    for part in (m1, m2, m3):
        total = total + part[...].astype(F32)
    mine[...] = total[:rows, :]
    other[...] = total[rows:, :].astype(BF)


def shards(source_emb, target_emb, hard_pool, hard_index, language, margin):
    total, width = source_emb.shape
    rows = target_emb.shape[0]
    blk, grp = lax.axis_index("blk"), lax.axis_index("grp")
    owners = 128
    cap = max(2, (2 * rows + owners - 1) // owners)
    slots = owners * cap
    z, y, c = blk // 4, (blk // 2) % 2, blk % 2

    start = grp * rows
    own_index = lax.dynamic_slice_in_dim(hard_index, start, rows, 0)
    own_source = lax.dynamic_slice_in_dim(source_emb, start, rows, 0)
    owner, pool_row = own_index // rows, own_index % rows
    position = jnp.arange(rows, dtype=jnp.int32)
    same = (owner[:, None] == owner[None, :]) & (position[None, :] < position[:, None])
    slot = owner * cap + jnp.sum(same.astype(jnp.int32), axis=1)
    pick = (slot[:, None] == jnp.arange(slots, dtype=jnp.int32)[None, :]).astype(BF)
    lane = jnp.arange(128, dtype=jnp.int32)[None, :]
    note = jnp.where(lane == 0, pool_row[:, None] + 1, jnp.where(lane == 1, position[:, None], 0)).astype(BF)
    sent = dot_f32(pick, jnp.concatenate([own_source, note], axis=1), ((0,), (0,))).astype(BF)
    sent = sent.reshape(owners, cap, width + 128)

    lang_match = language[:, None] == jnp.arange(margin.shape[0], dtype=jnp.int32)[None, :]
    margin_row = jnp.sum(jnp.where(lang_match, margin[None, :], 0.0), axis=1)

    across = hop_blk(target_emb, 0, 1, 0)
    sent, across = lax.optimization_barrier((sent, across))
    asked = lax.all_to_all(sent, ("grp", "blk"), 0, 0, tiled=True)
    line = {0: target_emb, **{dz: hop_blk(target_emb, -dz, 0, 0) for dz in (1, 3, 2)}}
    lines = {0: across, **{dz: hop_blk(across, -dz, 0, 0) for dz in (1, 3, 2)}}
    holds = grp == blk // 2
    place = {}
    for dz in range(4):
        for dy in range(2):
            for dc in range(2):
                zz = (z + dz) % 4
                k = (zz % 2) * 4 + (y ^ dy) * 2 + (c ^ dc)
                place[dz, dy, dc] = jnp.where(holds & (zz // 2 == c), k, -1)
    order = [[(dz, dy, dc) for dc in (0, 1) for dz, dy in chunk] for chunk in CHUNKS]
    places = [jnp.stack([place[key] for key in chunk]) for chunk in order]
    flat = jnp.concatenate(places)

    stats, so_far = [], ()

    def pair_of(n):
        dz = CHUNKS[n][0][0]
        near = jnp.concatenate([line[dz], lines[dz]])
        return near, hop_blk(near, 0, 0, 1)

    def add_chunk(n, pair):
        nonlocal so_far
        e, stat, tgt = score_call(places[n], source_emb, *pair, n, so_far)
        so_far = (e, tgt)
        stats.append(stat)

    add_chunk(0, pair_of(0))
    asked, line[1], lines[1], line[3], lines[3], stats[0] = lax.optimization_barrier(
        (asked, line[1], lines[1], line[3], lines[3], stats[0])
    )
    asked = asked.reshape(slots, width + 128)
    asker_rows = asked[:, :width]
    pool_at = asked[:, width].astype(jnp.int32) - 1
    asker_at = asked[:, width + 1].astype(jnp.int32)
    serve = (pool_at[:, None] == position[None, :]).astype(BF)
    served = dot_f32(serve, hard_pool, ((1,), (0,))).astype(BF)
    first_pair = pair_of(1)
    second_pair = pair_of(2)
    served, places[1] = lax.optimization_barrier((served, places[1]))
    fetched = lax.all_to_all(served.reshape(owners, cap, width), ("grp", "blk"), 0, 0, tiled=True)
    asked_score = jnp.sum(asker_rows.astype(F32) * served.astype(F32), axis=1)
    add_chunk(1, first_pair)
    early_target, line[2], lines[2], stats[1] = lax.optimization_barrier((target_emb, line[2], lines[2], stats[1]))
    own_target = lax.ppermute(
        early_target, ("grp", "blk"), [(16 * i + j, (j % 8) * 16 + 2 * i + j // 8) for i in range(8) for j in range(16)]
    )
    last_pair = pair_of(2 + 1)
    add_chunk(2, second_pair)
    fetched, stats[2] = lax.optimization_barrier((fetched, stats[2]))
    hard_rows = dot_f32(pick, fetched.reshape(slots, width), ((1,), (0,)))
    hard_score = jnp.sum(own_source.astype(F32) * hard_rows, axis=1)
    add_chunk(3, last_pair)

    tops = jnp.stack([stat[0] for stat in stats])
    sums = jnp.stack([stat[1] for stat in stats])
    reach = jnp.maximum(jnp.max(jnp.stack([stat[2] for stat in stats]), axis=0), jnp.max(jnp.abs(hard_rows)))
    own_margin = lax.dynamic_slice_in_dim(margin_row, start, rows, 0)
    own_pos = jnp.sum(own_source.astype(F32) * own_target.astype(F32), axis=1) - own_margin
    pos = lax.dynamic_update_slice_in_dim(jnp.zeros((total,), F32), own_pos, start, 0)
    hard_all = lax.dynamic_update_slice_in_dim(jnp.full((total,), LOW, F32), hard_score, start, 0)
    soft_top = jnp.max(tops, axis=0)
    soft = jnp.sum(sums * jnp.exp(tops - soft_top), axis=0)
    mine = jnp.stack([soft_top, soft, pos, hard_all, reach] + [jnp.zeros((total,), F32)] * 3)
    everyone = lax.all_to_all(jnp.broadcast_to(mine[None], (8, 8, total)), "grp", 0, 0, tiled=True)
    source_part = source_call(jnp.concatenate([jnp.exp(tops - soft_top), jnp.zeros((4, total), F32)]), *so_far)
    everyone, source_part = lax.optimization_barrier((everyone, source_part))
    source_parts = lax.all_to_all(source_part.reshape(8, rows, width), "grp", 0, 0, tiled=True)
    pos = jnp.sum(everyone[:, 2], axis=0)
    hard_all = jnp.max(everyone[:, 3], axis=0)
    reach = jnp.max(everyone[:, 4], axis=0)
    top = jnp.maximum(jnp.max(everyone[:, 0], axis=0), jnp.maximum(pos, hard_all))
    off = jnp.sum(everyone[:, 1] * jnp.exp(everyone[:, 0] - top), axis=0) + jnp.exp(hard_all - top)
    log_total = top + jnp.log(off + jnp.exp(pos - top))
    row_loss = log_total - pos
    less = jnp.exp(pos - log_total) - 1.0
    diag_weight = jnp.where(holds, less, 0.0)

    mass = jnp.abs(less) + off * jnp.exp(top - log_total)
    bound = jnp.maximum(1.01 * reach * mass, 1e-30)
    col = jnp.concatenate(
        [jnp.stack([jnp.exp(hard_all - log_total), less, 32767.0 / bound]), jnp.exp(everyone[:, 0] - log_total[None])]
    )
    col = lax.dynamic_slice_in_dim(col, start, rows, 1)
    col = jnp.transpose(col)

    all_logs = jnp.concatenate([log_total[None], hop_blk(log_total[None], 0, 0, 1)])
    all_logs = jnp.concatenate([all_logs] + [hop_blk(all_logs, -dz, 0, 0) for dz in (1, 2, 3)])
    all_logs = jnp.concatenate([all_logs, hop_blk(all_logs, 0, 1, 0)])
    asker = jnp.arange(owners, dtype=jnp.int32)
    asker_blk = asker % 16
    log_at = ((asker_blk // 2 % 2) ^ y) * 8 + (asker_blk // 4 - z) % 4 * 2 + ((asker_blk % 2) ^ c)
    log_rows = jnp.take(all_logs, jnp.repeat(log_at, cap), axis=0, mode="clip")
    row_in_block = jnp.repeat(asker // 16 * rows, cap) + asker_at
    match = row_in_block[:, None] == jnp.arange(total, dtype=jnp.int32)[None, :]
    asked_log = jnp.sum(jnp.where(match, log_rows, 0.0), axis=1)
    asked_prob = jnp.where(pool_at >= 0, jnp.exp(jnp.where(pool_at >= 0, asked_score - asked_log, LOW)), 0.0)
    pool_terms = (asked_prob[:, None] * asker_rows.astype(F32)).astype(BF)
    pool_grad = dot_f32(serve, pool_terms, ((0,), (0,)))

    weights = jnp.concatenate([jnp.exp(tops - log_total), diag_weight[None], jnp.zeros((3, total), F32)])
    keep, give = target_call(flat, weights, so_far[0], source_emb, all_logs)
    got = hop_blk(give, 0, 0, 1)
    leave = [(keep[n] + got[n].astype(F32)).astype(BF) for n in (1, 2, 3)]
    coded = code_call(source_parts, hard_rows, own_target, col, [])
    source_codes = lax.all_to_all(coded, "grp", 0, 0, tiled=True).reshape(total, width)
    source_grad = source_codes.astype(F32) * (bound * (1.0 / 32767.0))[:, None]
    moved = [hop_blk(leave[n - 1], CHUNKS[n][0][0], 0, 0) for n in (1, 2, 3)]
    whole = [pl.BlockSpec((1, 2 * rows, width), lambda i: (0, 0, 0))] * 2
    whole += [pl.BlockSpec((2 * rows, width), lambda i: (0, 0))] * 3 + [pl.BlockSpec(memory_space=pl.ANY)]
    mine, other = pl.pallas_call(
        line_kernel,
        out_shape=(jax.ShapeDtypeStruct((rows, width), F32), jax.ShapeDtypeStruct((rows, width), BF)),
        grid=(1,),
        in_specs=whole,
        out_specs=[pl.BlockSpec((rows, width), lambda i: (0, 0))] * 2,
        cost_estimate=pl.CostEstimate(flops=10 * rows * width, bytes_accessed=30 * rows * width, transcendentals=0),
        name="lines",
    )(keep, got, *moved, coded)
    target_grad = mine + hop_blk(other, 0, 1, 0).astype(F32)
    return (row_loss, source_grad, target_grad, pool_grad)


def solution(mesh):
    in_specs = (P("blk", None), P(("grp", "blk"), None), P(("grp", "blk"), None), P("blk"), P("blk"), P())
    out_specs = (P("blk"), P("blk", None), P(("grp", "blk"), None), P(("grp", "blk"), None))
    return jax.shard_map(shards, mesh=mesh, in_specs=in_specs, out_specs=out_specs, check_vma=False)
```

```python
import jax
import jax.numpy as jnp
from jax import lax
from jax.experimental import pallas as pl
from jax.experimental.pallas import tpu as pltpu
from jax.sharding import PartitionSpec as P

BF, F32 = jnp.bfloat16, jnp.float32
NEG = -1e30
LOW = -3e38
TILE = 768
PART = 384
CHUNKS = (((0, 0), (0, 1)), ((1, 0), (3, 0)), ((2, 0), (1, 1)), ((3, 1), (2, 1)))


def hop_blk(value, dz, dy, dc):
    route = []
    for i in range(16):
        z, y, c = i // 4, (i // 2) % 2, i % 2
        route.append((i, ((z + dz) % 4) * 4 + (y ^ dy) * 2 + (c ^ dc)))
    return lax.ppermute(value, "blk", route)


def hop_grp(value, dx, dy):
    return lax.ppermute(value, "grp", [(i, ((i // 2 + dx) % 4) * 2 + ((i % 2) ^ dy)) for i in range(8)])


def dot_f32(a, b, dims):
    return lax.dot_general(a, b, (dims, ((), ())), preferred_element_type=F32)


def columns_of(rows):
    pad = jnp.zeros((120, rows.shape[1]), F32)
    return jnp.transpose(jnp.concatenate([rows, pad], axis=0))


def score_kernel(place, src, t0, t1, t2, t3, *refs):
    e_out, stat_out, tgt_out, a_ref = refs[-4:]
    rows = t0.shape[0]
    half = 2 * rows
    step = pl.program_id(0)

    @pl.when(step == 0)
    def _():
        top = jnp.zeros((1, 1), F32)
        for q, t in enumerate((t0, t1, t2, t3)):
            block = t[...]
            tgt_out[0, q * rows : (q + 1) * rows, :] = block
            top = jnp.maximum(top, jnp.max(jnp.abs(block).astype(F32), keepdims=True))
        a_ref[...] = jnp.broadcast_to(top, a_ref.shape)

    tgt = tgt_out[0]
    lane = lax.broadcasted_iota(jnp.int32, (PART, 128), 1)
    column = lax.broadcasted_iota(jnp.int32, (PART, 2 * half), 1)
    line = lax.broadcasted_iota(jnp.int32, (PART, 1), 0)
    parts = []
    for first in range(0, src.shape[0], PART):
        ats = []
        for sub in range(2):
            k = step * (src.shape[0] // rows) + first // rows + sub
            at = jnp.int32(-(1 << 20))
            for q in range(4):
                at = jnp.where(place[q] == k, (q - sub) * rows, at)
            ats.append(at)
        hole = line + jnp.where(line < rows, ats[0], ats[1])
        here = pl.ds(first, PART)
        s = dot_f32(src[here, :], tgt, ((1,), (1,)))
        s = jnp.where(column == hole, NEG, s)
        top = jnp.max(s, axis=1, keepdims=True)
        e = jnp.exp(s - top)
        total = jnp.sum(e, axis=1, keepdims=True)
        e_out[0, here, :] = e.astype(BF)
        parts.append(jnp.where(lane == 0, top, jnp.where(lane == 1, total, a_ref[0:1, :])))
    stat_out[...] = jnp.transpose(jnp.concatenate(parts, axis=0))[0:8, :]


def score_call(place, src, blocks, n, so_far):
    rows, width = blocks[0].shape
    total = src.shape[0]
    cols = 4 * rows
    so_far = list(so_far)
    whole = pl.BlockSpec((rows, width), lambda i, p: (0, 0))
    return pl.pallas_call(
        score_kernel,
        out_shape=(
            pltpu.HBM((4, total, cols), BF),
            jax.ShapeDtypeStruct((8, total), F32),
            pltpu.HBM((4, cols, width), BF),
        ),
        grid_spec=pltpu.PrefetchScalarGridSpec(
            num_scalar_prefetch=1,
            grid=(total // TILE,),
            in_specs=[pl.BlockSpec((TILE, width), lambda i, p: (i, 0))]
            + [whole] * 4
            + [pl.BlockSpec(memory_space=pl.ANY)] * len(so_far),
            out_specs=(
                pl.BlockSpec((1, TILE, cols), lambda i, p: (n, i, 0)),
                pl.BlockSpec((8, TILE), lambda i, p: (0, i)),
                pl.BlockSpec((1, cols, width), lambda i, p: (n, 0, 0)),
            ),
            scratch_shapes=[pltpu.VMEM((8, 128), F32)],
        ),
        input_output_aliases={6: 0, 7: 2} if so_far else {},
        compiler_params=pltpu.CompilerParams(vmem_limit_bytes=24 << 20),
        cost_estimate=pl.CostEstimate(
            flops=2 * total * cols * width, bytes_accessed=total * (width + cols) * 2, transcendentals=total * cols
        ),
        name="scores",
    )(place, src, *blocks, *so_far)


def source_kernel(w_ref, e_ref, tgt_ref, out):
    weights = columns_of(w_ref[...])
    total = None
    for c in range(4):
        part = dot_f32(e_ref[c], tgt_ref[c], ((1,), (0,))) * weights[:, c : c + 1]
        total = part if total is None else total + part
    out[...] = total.astype(BF)


def source_call(weights, e_all, tgt_all):
    _, total, cols = e_all.shape
    width = tgt_all.shape[2]
    return pl.pallas_call(
        source_kernel,
        out_shape=jax.ShapeDtypeStruct((total, width), BF),
        grid=(total // PART,),
        in_specs=[
            pl.BlockSpec((8, PART), lambda i: (0, i)),
            pl.BlockSpec((4, PART, cols), lambda i: (0, i, 0)),
            pl.BlockSpec((4, cols, width), lambda i: (0, 0, 0), pipeline_mode=pl.Buffered(1)),
        ],
        out_specs=pl.BlockSpec((PART, width), lambda i: (i, 0)),
        cost_estimate=pl.CostEstimate(
            flops=8 * total * cols * width, bytes_accessed=total * (8 * cols + 2 * width), transcendentals=0
        ),
        name="source_terms",
    )(weights, e_all, tgt_all)


def target_kernel(place, w_ref, e_ref, src_ref, _, keep, give, acc, scaled, column):
    rows = acc.shape[0] // 4
    total = src_ref.shape[0]
    chunk = pl.program_id(0)

    @pl.when(chunk == 0)
    def _():
        for first in range(0, total, PART):
            here = slice(first, first + PART)
            column[here, :] = columns_of(w_ref[:, here])

    lane = lax.broadcasted_iota(jnp.int32, (PART, 128), 1)
    for first in range(0, total, PART):
        here = slice(first, first + PART)
        weight = jnp.sum(jnp.where(lane == chunk, column[here, :], 0.0), axis=1, keepdims=True)
        scaled[here, :] = (src_ref[here, :].astype(F32) * weight).astype(BF)
    acc[...] = dot_f32(e_ref[0], scaled[...], ((0,), (0,)))
    for q in range(4):
        at = place[chunk * 4 + q]

        @pl.when(at >= 0)
        def _():
            there = slice(q * rows, (q + 1) * rows)
            here = pl.ds(pl.multiple_of(at * rows, rows), rows)
            acc[there, :] = acc[there, :] + column[here, 4:5] * src_ref[here, :].astype(F32)

    keep[0] = acc[0 : 2 * rows, :]
    give[0] = acc[2 * rows : 4 * rows, :].astype(BF)


def target_call(place, weights, e_all, src, after):
    _, total, cols = e_all.shape
    width = src.shape[1]
    half = (4, cols // 2, width)
    half_spec = pl.BlockSpec((1, cols // 2, width), lambda i, p: (i, 0, 0))
    return pl.pallas_call(
        target_kernel,
        out_shape=(jax.ShapeDtypeStruct(half, F32), jax.ShapeDtypeStruct(half, BF)),
        grid_spec=pltpu.PrefetchScalarGridSpec(
            num_scalar_prefetch=1,
            grid=(4,),
            in_specs=[
                pl.BlockSpec((8, total), lambda i, p: (0, 0)),
                pl.BlockSpec((1, total, cols), lambda i, p: (i, 0, 0)),
                pl.BlockSpec((total, width), lambda i, p: (0, 0)),
                pl.BlockSpec(memory_space=pl.ANY),
            ],
            out_specs=(half_spec, half_spec),
            scratch_shapes=[
                pltpu.VMEM((cols, width), F32),
                pltpu.VMEM((total, width), BF),
                pltpu.VMEM((total, 128), F32),
            ],
        ),
        cost_estimate=pl.CostEstimate(
            flops=8 * total * cols * width, bytes_accessed=total * (width + 4 * cols) * 2 + cols * width * 12, transcendentals=0
        ),
        name="target_terms",
    )(place, weights, e_all, src, after)


def code_kernel(parts, hard, tgt, col, _, out, high):
    total = hard[...] * col[:, 0:1] + tgt[...].astype(F32) * col[:, 1:2]
    for g in range(parts.shape[0]):
        total = total + parts[g].astype(F32) * col[:, 3 + g : 4 + g]
    scaled = jnp.clip(total * col[:, 2:3], -32767.0, 32767.0)
    coded = jnp.round(scaled).astype(jnp.int32).astype(jnp.int16)
    out[...] = coded
    high[...] = coded


def line_kernel(keep, got, m1, m2, m3, mine, other):
    rows = mine.shape[0]
    total = keep[0] + got[0].astype(F32)
    for part in (m1, m2, m3):
        total = total + part[...].astype(F32)
    mine[...] = total[:rows, :]
    other[...] = total[rows:, :].astype(BF)


def decode_kernel(order, scale, own, side, far1, far2, far3, pairs1, pairs2, pairs3, far_side, out):
    step = pl.program_id(0)
    half = own.shape[0] // 2
    far, pairs = (None, far1, far2, far3), (None, pairs1, pairs2, pairs3)
    for dx in range(4):
        for dy in range(2):

            @pl.when(step == dx * 2 + dy)
            def _():
                if dx == 0:
                    whole = (own if dy == 0 else side)[...]
                    out[...] = whole.astype(jnp.int32).astype(F32) * scale[...]
                else:
                    low = pairs[dx][dy]
                    high = far[dx][...] if dy == 0 else far_side[dx - 1]
                    out[0:half, :] = low.astype(jnp.int32).astype(F32) * scale[0:half, :]
                    out[half:, :] = high.astype(jnp.int32).astype(F32) * scale[half:, :]


def decode_call(order, scale, pieces):
    rows, width = pieces[0].shape
    total = scale.shape[0]
    return pl.pallas_call(
        decode_kernel,
        out_shape=jax.ShapeDtypeStruct((total, width), F32),
        grid_spec=pltpu.PrefetchScalarGridSpec(
            num_scalar_prefetch=1,
            grid=(total // rows,),
            in_specs=[pl.BlockSpec((rows, 1), lambda i, p: (p[i], 0))]
            + [pl.BlockSpec(x.shape, lambda i, p, n=x.ndim: (0,) * n) for x in pieces],
            out_specs=pl.BlockSpec((rows, width), lambda i, p: (p[i], 0)),
        ),
        cost_estimate=pl.CostEstimate(flops=total * width, bytes_accessed=total * width * 6, transcendentals=0),
        name="decode",
    )(order, scale, *pieces)


def shards(source_emb, target_emb, hard_pool, hard_index, language, margin):
    total, width = source_emb.shape
    rows = target_emb.shape[0]
    blk, grp = lax.axis_index("blk"), lax.axis_index("grp")
    owners = 128
    cap = max(2, (2 * rows + owners - 1) // owners)
    slots = owners * cap
    z, y, c = blk // 4, (blk // 2) % 2, blk % 2

    start = grp * rows
    own_index = lax.dynamic_slice_in_dim(hard_index, start, rows, 0)
    own_source = lax.dynamic_slice_in_dim(source_emb, start, rows, 0)
    owner, pool_row = own_index // rows, own_index % rows
    position = jnp.arange(rows, dtype=jnp.int32)
    same = (owner[:, None] == owner[None, :]) & (position[None, :] < position[:, None])
    slot = owner * cap + jnp.sum(same.astype(jnp.int32), axis=1)
    at_slot = slot[:, None] == jnp.arange(slots, dtype=jnp.int32)[None, :]
    requests = jnp.sum(jnp.where(at_slot, pool_row[:, None] + 1, 0), axis=0) - 1
    wanted = lax.all_to_all(requests.reshape(owners, cap), ("grp", "blk"), 0, 0, tiled=True)
    lang_match = language[:, None] == jnp.arange(margin.shape[0], dtype=jnp.int32)[None, :]
    margin_row = jnp.sum(jnp.where(lang_match, margin[None, :], 0.0), axis=1)

    have = {(0, 0, 0): target_emb}
    have[0, 1, 0] = hop_blk(target_emb, 0, 1, 0)
    for dz in (1, 3, 2):
        have[dz, 0, 0] = hop_blk(target_emb, -dz, 0, 0)
    for dz in (1, 3, 2):
        have[dz, 1, 0] = hop_blk(have[0, 1, 0], -dz, 0, 0)
    for dz, dy in [pair for chunk in CHUNKS for pair in chunk]:
        have[dz, dy, 1] = hop_blk(have[dz, dy, 0], 0, 0, 1)

    holds = grp == blk // 2
    place = {}
    for dz in range(4):
        for dy in range(2):
            for dc in range(2):
                zz = (z + dz) % 4
                k = (zz % 2) * 4 + (y ^ dy) * 2 + (c ^ dc)
                place[dz, dy, dc] = jnp.where(holds & (zz // 2 == c), k, -1)
    order = [[(dz, dy, dc) for dc in (0, 1) for dz, dy in chunk] for chunk in CHUNKS]
    places = [jnp.stack([place[key] for key in chunk]) for chunk in order]
    flat = jnp.concatenate(places)

    stats, so_far = [], ()

    def add_chunk(n):
        nonlocal so_far
        e, stat, tgt = score_call(places[n], source_emb, [have[key] for key in order[n]], n, so_far)
        so_far = (e, tgt)
        stats.append(stat)

    add_chunk(0)
    wanted, stats[0] = lax.optimization_barrier((wanted, stats[0]))
    serve = (wanted.reshape(slots)[:, None] == position[None, :]).astype(BF)
    served = dot_f32(serve, hard_pool, ((1,), (0,))).astype(BF).reshape(owners, cap, width)
    served, places[1] = lax.optimization_barrier((served, places[1]))
    fetched = lax.all_to_all(served, ("grp", "blk"), 0, 0, tiled=True).reshape(slots, width)
    add_chunk(1)
    early_target, stats[1] = lax.optimization_barrier((target_emb, stats[1]))
    own_target = lax.ppermute(
        early_target, ("grp", "blk"), [(16 * i + j, (j % 8) * 16 + 2 * i + j // 8) for i in range(8) for j in range(16)]
    )
    add_chunk(2)
    fetched, stats[2] = lax.optimization_barrier((fetched, stats[2]))
    pick = at_slot.astype(BF)
    hard_rows = dot_f32(pick, fetched, ((1,), (0,)))
    hard_score = jnp.sum(own_source.astype(F32) * hard_rows, axis=1)
    add_chunk(3)

    tops = jnp.stack([stat[0] for stat in stats])
    sums = jnp.stack([stat[1] for stat in stats])
    reach = jnp.maximum(jnp.max(jnp.stack([stat[2] for stat in stats]), axis=0), jnp.max(jnp.abs(hard_rows)))
    own_margin = lax.dynamic_slice_in_dim(margin_row, start, rows, 0)
    own_pos = jnp.sum(own_source.astype(F32) * own_target.astype(F32), axis=1) - own_margin
    pos = lax.dynamic_update_slice_in_dim(jnp.zeros((total,), F32), own_pos, start, 0)
    hard_all = lax.dynamic_update_slice_in_dim(jnp.full((total,), LOW, F32), hard_score, start, 0)
    soft_top = jnp.max(tops, axis=0)
    soft = jnp.sum(sums * jnp.exp(tops - soft_top), axis=0)
    mine = jnp.stack([soft_top, soft, pos, hard_all, reach] + [jnp.zeros((total,), F32)] * 3)
    everyone = lax.all_to_all(jnp.broadcast_to(mine[None], (8, 8, total)), "grp", 0, 0, tiled=True)
    source_part = source_call(jnp.concatenate([jnp.exp(tops - soft_top), jnp.zeros((4, total), F32)]), *so_far)
    everyone, source_part = lax.optimization_barrier((everyone, source_part))
    source_parts = lax.all_to_all(source_part.reshape(8, rows, width), "grp", 0, 0, tiled=True)
    token = hop_blk(source_part[:16, :128], 0, 0, 1)
    pos = jnp.sum(everyone[:, 2], axis=0)
    hard_all = jnp.max(everyone[:, 3], axis=0)
    reach = jnp.max(everyone[:, 4], axis=0)
    top = jnp.maximum(jnp.max(everyone[:, 0], axis=0), jnp.maximum(pos, hard_all))
    off = jnp.sum(everyone[:, 1] * jnp.exp(everyone[:, 0] - top), axis=0) + jnp.exp(hard_all - top)
    log_total = top + jnp.log(off + jnp.exp(pos - top))
    row_loss = log_total - pos
    less = jnp.exp(pos - log_total) - 1.0
    diag_weight = jnp.where(holds, less, 0.0)

    x_at, y_at = grp // 2, grp % 2
    mass = jnp.abs(less) + off * jnp.exp(top - log_total)
    bound = jnp.maximum(1.01 * reach * mass, 1e-30)
    col = jnp.concatenate(
        [jnp.stack([jnp.exp(hard_all - log_total), less, 32767.0 / bound]), jnp.exp(everyone[:, 0] - log_total[None])]
    )
    col = lax.dynamic_slice_in_dim(col, start, rows, 1)
    hard_prob = col[0]
    col = jnp.transpose(col)
    half = rows // 2

    weights = jnp.concatenate([jnp.exp(tops - log_total), diag_weight[None], jnp.zeros((3, total), F32)])
    keep, give = target_call(flat, weights, so_far[0], source_emb, token)
    got = hop_blk(give, 0, 0, 1)
    where_at = {pair: (n, j) for n, chunk in enumerate(CHUNKS) for j, pair in enumerate(chunk)}

    def both(dz, dy):
        n, j = where_at[dz, dy]
        here = slice(j * rows, (j + 1) * rows)
        return (keep[n, here] + got[n, here].astype(F32)).astype(BF)

    moved = [hop_blk(jnp.concatenate([both(dz, 0), both(dz, 1)]), dz, 0, 0) for dz in (1, 3, 2)]
    whole = [pl.BlockSpec((1, 2 * rows, width), lambda i: (0, 0, 0))] * 2
    whole += [pl.BlockSpec((2 * rows, width), lambda i: (0, 0))] * 3
    mine, other = pl.pallas_call(
        line_kernel,
        out_shape=(jax.ShapeDtypeStruct((rows, width), F32), jax.ShapeDtypeStruct((rows, width), BF)),
        grid=(1,),
        in_specs=whole,
        out_specs=[pl.BlockSpec((rows, width), lambda i: (0, 0))] * 2,
        cost_estimate=pl.CostEstimate(flops=10 * rows * width, bytes_accessed=30 * rows * width, transcendentals=0),
        name="lines",
    )(keep, got, *moved)
    target_grad = mine + hop_blk(other, 0, 1, 0).astype(F32)

    coded, coded_high = pl.pallas_call(
        code_kernel,
        out_shape=(jax.ShapeDtypeStruct((rows, width), jnp.int16), jax.ShapeDtypeStruct((half, width), jnp.int16)),
        grid=(2,),
        in_specs=[
            pl.BlockSpec((8, half, width), lambda i: (0, i, 0)),
            pl.BlockSpec((half, width), lambda i: (i, 0)),
            pl.BlockSpec((half, width), lambda i: (i, 0)),
            pl.BlockSpec((half, col.shape[1]), lambda i: (i, 0)),
            pl.BlockSpec(memory_space=pl.ANY),
        ],
        out_specs=(pl.BlockSpec((half, width), lambda i: (i, 0)), pl.BlockSpec((half, width), lambda i: (0, 0))),
        cost_estimate=pl.CostEstimate(flops=10 * rows * width, bytes_accessed=22 * rows * width, transcendentals=0),
        name="code",
    )(source_parts, hard_rows, own_target, col, other)
    hard_gate = hard_prob + 0.0 * coded[0, 0].astype(F32)
    side = hop_grp(coded, 0, 1)
    far = [hop_grp(coded_high, -dx, 0) for dx in (1, 2, 3)]
    low = jnp.stack([coded[:half], side[:half]])
    pairs = [hop_grp(low, -dx, 0) for dx in (1, 2, 3)]
    far_side = hop_grp(jnp.stack(far), 0, 1)
    blocks = jnp.stack([((x_at + dx) % 4) * 2 + (y_at ^ dy) for dx in range(4) for dy in range(2)])
    source_grad = decode_call(
        blocks, (bound * (1.0 / 32767.0))[:, None], [coded, side, *far, *pairs, far_side]
    )

    contribution = (hard_gate[:, None] * own_source.astype(F32)).astype(BF)
    outgoing = dot_f32(pick, contribution, ((0,), (0,))).astype(BF).reshape(owners, cap, width)
    incoming = lax.all_to_all(outgoing, ("grp", "blk"), 0, 0, tiled=True).reshape(slots, width)
    pool_grad = dot_f32(serve, incoming, ((0,), (0,)))
    return (row_loss, source_grad, target_grad, pool_grad)


def solution(mesh):
    in_specs = (P("blk", None), P(("grp", "blk"), None), P(("grp", "blk"), None), P("blk"), P("blk"), P())
    out_specs = (P("blk"), P("blk", None), P(("grp", "blk"), None), P(("grp", "blk"), None))
    return jax.shard_map(shards, mesh=mesh, in_specs=in_specs, out_specs=out_specs, check_vma=False)
```

```python
import jax
import jax.numpy as jnp
from jax import lax
from jax.experimental import pallas as pl
from jax.experimental.pallas import tpu as pltpu
from jax.sharding import PartitionSpec as P

BF, F32 = jnp.bfloat16, jnp.float32
NEG = -1e30
LOW = -3e38
TILE = 768
PART = 384
CHUNKS = (((0, 0), (0, 1)), ((1, 0), (3, 0)), ((2, 0), (1, 1)), ((3, 1), (2, 1)))


def hop_blk(value, dz, dy, dc):
    route = []
    for i in range(16):
        z, y, c = i // 4, (i // 2) % 2, i % 2
        route.append((i, ((z + dz) % 4) * 4 + (y ^ dy) * 2 + (c ^ dc)))
    return lax.ppermute(value, "blk", route)


def hop_grp(value, dx, dy):
    return lax.ppermute(value, "grp", [(i, ((i // 2 + dx) % 4) * 2 + ((i % 2) ^ dy)) for i in range(8)])


def dot_f32(a, b, dims):
    return lax.dot_general(a, b, (dims, ((), ())), preferred_element_type=F32)


def columns_of(rows):
    pad = jnp.zeros((120, rows.shape[1]), F32)
    return jnp.transpose(jnp.concatenate([rows, pad], axis=0))


def score_kernel(place, src, t0, t1, t2, t3, *refs):
    e_out, stat_out, tgt_ref, a_ref = refs[-4:]
    rows = t0.shape[0]
    half = 2 * rows
    step = pl.program_id(0)

    @pl.when(step == 0)
    def _():
        top = jnp.zeros((1, 1), F32)
        for q, t in enumerate((t0, t1, t2, t3)):
            block = t[...]
            tgt_ref[q * rows : (q + 1) * rows, :] = block
            top = jnp.maximum(top, jnp.max(jnp.abs(block).astype(F32), keepdims=True))
        a_ref[...] = jnp.broadcast_to(top, a_ref.shape)

    tgt = tgt_ref[...]
    lane = lax.broadcasted_iota(jnp.int32, (PART, 128), 1)
    column = lax.broadcasted_iota(jnp.int32, (PART, 2 * half), 1)
    line = lax.broadcasted_iota(jnp.int32, (PART, 1), 0)
    parts = []
    for first in range(0, src.shape[0], PART):
        ats = []
        for sub in range(2):
            k = step * (src.shape[0] // rows) + first // rows + sub
            at = jnp.int32(-(1 << 20))
            for q in range(4):
                at = jnp.where(place[q] == k, (q - sub) * rows, at)
            ats.append(at)
        hole = line + jnp.where(line < rows, ats[0], ats[1])
        here = pl.ds(first, PART)
        s = dot_f32(src[here, :], tgt, ((1,), (1,)))
        s = jnp.where(column == hole, NEG, s)
        top = jnp.max(s, axis=1, keepdims=True)
        e = jnp.exp(s - top)
        total = jnp.sum(e, axis=1, keepdims=True)
        e_out[0, here, :] = e.astype(BF)
        parts.append(jnp.where(lane == 0, top, jnp.where(lane == 1, total, a_ref[0:1, :])))
    stat_out[...] = jnp.transpose(jnp.concatenate(parts, axis=0))[0:8, :]


def score_call(place, src, blocks, n, so_far):
    rows, width = blocks[0].shape
    total = src.shape[0]
    cols = 4 * rows
    so_far = list(so_far)
    whole = pl.BlockSpec((rows, width), lambda i, p: (0, 0))
    return pl.pallas_call(
        score_kernel,
        out_shape=(
            pltpu.HBM((4, total, cols), BF),
            jax.ShapeDtypeStruct((8, total), F32),
        ),
        grid_spec=pltpu.PrefetchScalarGridSpec(
            num_scalar_prefetch=1,
            grid=(total // TILE,),
            in_specs=[pl.BlockSpec((TILE, width), lambda i, p: (i, 0))]
            + [whole] * 4
            + [pl.BlockSpec(memory_space=pl.ANY)] * len(so_far),
            out_specs=(
                pl.BlockSpec((1, TILE, cols), lambda i, p: (n, i, 0)),
                pl.BlockSpec((8, TILE), lambda i, p: (0, i)),
            ),
            scratch_shapes=[pltpu.VMEM((cols, width), BF), pltpu.VMEM((8, 128), F32)],
        ),
        input_output_aliases={6: 0} if so_far else {},
        compiler_params=pltpu.CompilerParams(vmem_limit_bytes=24 << 20),
        cost_estimate=pl.CostEstimate(
            flops=2 * total * cols * width, bytes_accessed=total * (width + cols) * 2, transcendentals=total * cols
        ),
        name="scores",
    )(place, src, *blocks, *so_far)


def source_kernel(w_ref, e_ref, *refs):
    blocks, out, tgt = refs[:-2], refs[-2], refs[-1]
    rows = blocks[0].shape[0]

    @pl.when(pl.program_id(0) == 0)
    def _():
        for n, block in enumerate(blocks):
            tgt[n // 4, n % 4 * rows : (n % 4 + 1) * rows, :] = block[...]

    weights = columns_of(w_ref[...])
    total = None
    for c in range(4):
        part = dot_f32(e_ref[c], tgt[c], ((1,), (0,))) * weights[:, c : c + 1]
        total = part if total is None else total + part
    out[...] = total.astype(BF)


def source_call(weights, e_all, blocks):
    _, total, cols = e_all.shape
    rows, width = blocks[0].shape
    whole = pl.BlockSpec((rows, width), lambda i: (0, 0), pipeline_mode=pl.Buffered(1))
    return pl.pallas_call(
        source_kernel,
        out_shape=jax.ShapeDtypeStruct((total, width), BF),
        grid=(total // PART,),
        in_specs=[
            pl.BlockSpec((8, PART), lambda i: (0, i)),
            pl.BlockSpec((4, PART, cols), lambda i: (0, i, 0)),
        ]
        + [whole] * len(blocks),
        out_specs=pl.BlockSpec((PART, width), lambda i: (i, 0)),
        scratch_shapes=[pltpu.VMEM((4, cols, width), BF)],
        cost_estimate=pl.CostEstimate(
            flops=8 * total * cols * width, bytes_accessed=total * (8 * cols + 2 * width), transcendentals=0
        ),
        name="source_terms",
    )(weights, e_all, *blocks)


def target_kernel(place, w_ref, e_ref, src_ref, _, keep, give, acc, scaled, column):
    rows = acc.shape[0] // 4
    total = src_ref.shape[0]
    chunk = pl.program_id(0)

    @pl.when(chunk == 0)
    def _():
        for first in range(0, total, PART):
            here = slice(first, first + PART)
            column[here, :] = columns_of(w_ref[:, here])

    lane = lax.broadcasted_iota(jnp.int32, (PART, 128), 1)
    for first in range(0, total, PART):
        here = slice(first, first + PART)
        weight = jnp.sum(jnp.where(lane == chunk, column[here, :], 0.0), axis=1, keepdims=True)
        scaled[here, :] = (src_ref[here, :].astype(F32) * weight).astype(BF)
    acc[...] = dot_f32(e_ref[0], scaled[...], ((0,), (0,)))
    for q in range(4):
        at = place[chunk * 4 + q]

        @pl.when(at >= 0)
        def _():
            there = slice(q * rows, (q + 1) * rows)
            here = pl.ds(pl.multiple_of(at * rows, rows), rows)
            acc[there, :] = acc[there, :] + column[here, 4:5] * src_ref[here, :].astype(F32)

    keep[0] = acc[0 : 2 * rows, :]
    give[0] = acc[2 * rows : 4 * rows, :].astype(BF)


def target_call(place, weights, e_all, src, after):
    _, total, cols = e_all.shape
    width = src.shape[1]
    half = (4, cols // 2, width)
    half_spec = pl.BlockSpec((1, cols // 2, width), lambda i, p: (i, 0, 0))
    return pl.pallas_call(
        target_kernel,
        out_shape=(jax.ShapeDtypeStruct(half, F32), jax.ShapeDtypeStruct(half, BF)),
        grid_spec=pltpu.PrefetchScalarGridSpec(
            num_scalar_prefetch=1,
            grid=(4,),
            in_specs=[
                pl.BlockSpec((8, total), lambda i, p: (0, 0)),
                pl.BlockSpec((1, total, cols), lambda i, p: (i, 0, 0)),
                pl.BlockSpec((total, width), lambda i, p: (0, 0)),
                pl.BlockSpec(memory_space=pl.ANY),
            ],
            out_specs=(half_spec, half_spec),
            scratch_shapes=[
                pltpu.VMEM((cols, width), F32),
                pltpu.VMEM((total, width), BF),
                pltpu.VMEM((total, 128), F32),
            ],
        ),
        cost_estimate=pl.CostEstimate(
            flops=8 * total * cols * width, bytes_accessed=total * (width + 4 * cols) * 2 + cols * width * 12, transcendentals=0
        ),
        name="target_terms",
    )(place, weights, e_all, src, after)


def code_kernel(parts, hard, tgt, col, _, out, high):
    total = hard[...] * col[:, 0:1] + tgt[...].astype(F32) * col[:, 1:2]
    for g in range(parts.shape[0]):
        total = total + parts[g].astype(F32) * col[:, 3 + g : 4 + g]
    scaled = jnp.clip(total * col[:, 2:3], -32767.0, 32767.0)
    coded = jnp.round(scaled).astype(jnp.int32).astype(jnp.int16)
    out[...] = coded
    high[...] = coded


def line_kernel(keep, got, m1, m2, m3, mine, other):
    rows = mine.shape[0]
    total = keep[0] + got[0].astype(F32)
    for part in (m1, m2, m3):
        total = total + part[...].astype(F32)
    mine[...] = total[:rows, :]
    other[...] = total[rows:, :].astype(BF)


def decode_kernel(order, scale, own, side, far1, far2, far3, pairs1, pairs2, pairs3, far_side, out):
    step = pl.program_id(0)
    half = own.shape[0] // 2
    far, pairs = (None, far1, far2, far3), (None, pairs1, pairs2, pairs3)
    for dx in range(4):
        for dy in range(2):

            @pl.when(step == dx * 2 + dy)
            def _():
                if dx == 0:
                    whole = (own if dy == 0 else side)[...]
                    out[...] = whole.astype(jnp.int32).astype(F32) * scale[...]
                else:
                    low = pairs[dx][dy]
                    high = far[dx][...] if dy == 0 else far_side[dx - 1]
                    out[0:half, :] = low.astype(jnp.int32).astype(F32) * scale[0:half, :]
                    out[half:, :] = high.astype(jnp.int32).astype(F32) * scale[half:, :]


def decode_call(order, scale, pieces):
    rows, width = pieces[0].shape
    total = scale.shape[0]
    return pl.pallas_call(
        decode_kernel,
        out_shape=jax.ShapeDtypeStruct((total, width), F32),
        grid_spec=pltpu.PrefetchScalarGridSpec(
            num_scalar_prefetch=1,
            grid=(total // rows,),
            in_specs=[pl.BlockSpec((rows, 1), lambda i, p: (p[i], 0))]
            + [pl.BlockSpec(x.shape, lambda i, p, n=x.ndim: (0,) * n) for x in pieces],
            out_specs=pl.BlockSpec((rows, width), lambda i, p: (p[i], 0)),
        ),
        compiler_params=pltpu.CompilerParams(vmem_limit_bytes=24 << 20),
        cost_estimate=pl.CostEstimate(flops=total * width, bytes_accessed=total * width * 6, transcendentals=0),
        name="decode",
    )(order, scale, *pieces)


def shards(source_emb, target_emb, hard_pool, hard_index, language, margin):
    total, width = source_emb.shape
    rows = target_emb.shape[0]
    blk, grp = lax.axis_index("blk"), lax.axis_index("grp")
    owners = 128
    cap = max(2, (2 * rows + owners - 1) // owners)
    slots = owners * cap
    z, y, c = blk // 4, (blk // 2) % 2, blk % 2

    start = grp * rows
    own_index = lax.dynamic_slice_in_dim(hard_index, start, rows, 0)
    own_source = lax.dynamic_slice_in_dim(source_emb, start, rows, 0)
    owner, pool_row = own_index // rows, own_index % rows
    position = jnp.arange(rows, dtype=jnp.int32)
    same = (owner[:, None] == owner[None, :]) & (position[None, :] < position[:, None])
    slot = owner * cap + jnp.sum(same.astype(jnp.int32), axis=1)
    at_slot = slot[:, None] == jnp.arange(slots, dtype=jnp.int32)[None, :]
    requests = jnp.sum(jnp.where(at_slot, pool_row[:, None] + 1, 0), axis=0) - 1
    wanted = lax.all_to_all(requests.reshape(owners, cap), ("grp", "blk"), 0, 0, tiled=True)
    lang_match = language[:, None] == jnp.arange(margin.shape[0], dtype=jnp.int32)[None, :]
    margin_row = jnp.sum(jnp.where(lang_match, margin[None, :], 0.0), axis=1)

    have = {(0, 0, 0): target_emb}
    have[0, 1, 0] = hop_blk(target_emb, 0, 1, 0)
    for dz in (1, 3, 2):
        have[dz, 0, 0] = hop_blk(target_emb, -dz, 0, 0)
    for dz in (1, 3, 2):
        have[dz, 1, 0] = hop_blk(have[0, 1, 0], -dz, 0, 0)
    for dz, dy in [pair for chunk in CHUNKS for pair in chunk]:
        have[dz, dy, 1] = hop_blk(have[dz, dy, 0], 0, 0, 1)

    holds = grp == blk // 2
    place = {}
    for dz in range(4):
        for dy in range(2):
            for dc in range(2):
                zz = (z + dz) % 4
                k = (zz % 2) * 4 + (y ^ dy) * 2 + (c ^ dc)
                place[dz, dy, dc] = jnp.where(holds & (zz // 2 == c), k, -1)
    order = [[(dz, dy, dc) for dc in (0, 1) for dz, dy in chunk] for chunk in CHUNKS]
    places = [jnp.stack([place[key] for key in chunk]) for chunk in order]
    flat = jnp.concatenate(places)

    stats, so_far = [], ()

    def add_chunk(n):
        nonlocal so_far
        e, stat = score_call(places[n], source_emb, [have[key] for key in order[n]], n, so_far)
        so_far = (e,)
        stats.append(stat)

    add_chunk(0)
    wanted, stats[0] = lax.optimization_barrier((wanted, stats[0]))
    serve = (wanted.reshape(slots)[:, None] == position[None, :]).astype(BF)
    served = dot_f32(serve, hard_pool, ((1,), (0,))).astype(BF).reshape(owners, cap, width)
    served, places[1] = lax.optimization_barrier((served, places[1]))
    fetched = lax.all_to_all(served, ("grp", "blk"), 0, 0, tiled=True).reshape(slots, width)
    add_chunk(1)
    early_target, stats[1] = lax.optimization_barrier((target_emb, stats[1]))
    own_target = lax.ppermute(
        early_target, ("grp", "blk"), [(16 * i + j, (j % 8) * 16 + 2 * i + j // 8) for i in range(8) for j in range(16)]
    )
    add_chunk(2)
    fetched, stats[2] = lax.optimization_barrier((fetched, stats[2]))
    pick = at_slot.astype(BF)
    hard_rows = dot_f32(pick, fetched, ((1,), (0,)))
    hard_score = jnp.sum(own_source.astype(F32) * hard_rows, axis=1)
    add_chunk(3)

    tops = jnp.stack([stat[0] for stat in stats])
    sums = jnp.stack([stat[1] for stat in stats])
    reach = jnp.maximum(jnp.max(jnp.stack([stat[2] for stat in stats]), axis=0), jnp.max(jnp.abs(hard_rows)))
    own_margin = lax.dynamic_slice_in_dim(margin_row, start, rows, 0)
    own_pos = jnp.sum(own_source.astype(F32) * own_target.astype(F32), axis=1) - own_margin
    pos = lax.dynamic_update_slice_in_dim(jnp.zeros((total,), F32), own_pos, start, 0)
    hard_all = lax.dynamic_update_slice_in_dim(jnp.full((total,), LOW, F32), hard_score, start, 0)
    soft_top = jnp.max(tops, axis=0)
    soft = jnp.sum(sums * jnp.exp(tops - soft_top), axis=0)
    mine = jnp.stack([soft_top, soft, pos, hard_all, reach] + [jnp.zeros((total,), F32)] * 3)
    everyone = lax.all_to_all(jnp.broadcast_to(mine[None], (8, 8, total)), "grp", 0, 0, tiled=True)
    source_part = source_call(jnp.concatenate([jnp.exp(tops - soft_top), jnp.zeros((4, total), F32)]), so_far[0],
        [have[key] for chunk in order for key in chunk])
    everyone, source_part = lax.optimization_barrier((everyone, source_part))
    source_parts = lax.all_to_all(source_part.reshape(8, rows, width), "grp", 0, 0, tiled=True)
    token = hop_blk(source_part[:16, :128], 0, 0, 1)
    pos = jnp.sum(everyone[:, 2], axis=0)
    hard_all = jnp.max(everyone[:, 3], axis=0)
    reach = jnp.max(everyone[:, 4], axis=0)
    top = jnp.maximum(jnp.max(everyone[:, 0], axis=0), jnp.maximum(pos, hard_all))
    off = jnp.sum(everyone[:, 1] * jnp.exp(everyone[:, 0] - top), axis=0) + jnp.exp(hard_all - top)
    log_total = top + jnp.log(off + jnp.exp(pos - top))
    row_loss = log_total - pos
    less = jnp.exp(pos - log_total) - 1.0
    diag_weight = jnp.where(holds, less, 0.0)

    x_at, y_at = grp // 2, grp % 2
    mass = jnp.abs(less) + off * jnp.exp(top - log_total)
    bound = jnp.maximum(1.01 * reach * mass, 1e-30)
    col = jnp.concatenate(
        [jnp.stack([jnp.exp(hard_all - log_total), less, 32767.0 / bound]), jnp.exp(everyone[:, 0] - log_total[None])]
    )
    col = lax.dynamic_slice_in_dim(col, start, rows, 1)
    hard_prob = col[0]
    col = jnp.transpose(col)
    half = rows // 2

    weights = jnp.concatenate([jnp.exp(tops - log_total), diag_weight[None], jnp.zeros((3, total), F32)])
    keep, give = target_call(flat, weights, so_far[0], source_emb, token)
    got = hop_blk(give, 0, 0, 1)
    where_at = {pair: (n, j) for n, chunk in enumerate(CHUNKS) for j, pair in enumerate(chunk)}

    def both(dz, dy):
        n, j = where_at[dz, dy]
        here = slice(j * rows, (j + 1) * rows)
        return (keep[n, here] + got[n, here].astype(F32)).astype(BF)

    moved = [hop_blk(jnp.concatenate([both(dz, 0), both(dz, 1)]), dz, 0, 0) for dz in (1, 3, 2)]
    whole = [pl.BlockSpec((1, 2 * rows, width), lambda i: (0, 0, 0))] * 2
    whole += [pl.BlockSpec((2 * rows, width), lambda i: (0, 0))] * 3
    mine, other = pl.pallas_call(
        line_kernel,
        out_shape=(jax.ShapeDtypeStruct((rows, width), F32), jax.ShapeDtypeStruct((rows, width), BF)),
        grid=(1,),
        in_specs=whole,
        out_specs=[pl.BlockSpec((rows, width), lambda i: (0, 0))] * 2,
        cost_estimate=pl.CostEstimate(flops=10 * rows * width, bytes_accessed=30 * rows * width, transcendentals=0),
        name="lines",
    )(keep, got, *moved)
    target_grad = mine + hop_blk(other, 0, 1, 0).astype(F32)

    coded, coded_high = pl.pallas_call(
        code_kernel,
        out_shape=(jax.ShapeDtypeStruct((rows, width), jnp.int16), jax.ShapeDtypeStruct((half, width), jnp.int16)),
        grid=(2,),
        in_specs=[
            pl.BlockSpec((8, half, width), lambda i: (0, i, 0)),
            pl.BlockSpec((half, width), lambda i: (i, 0)),
            pl.BlockSpec((half, width), lambda i: (i, 0)),
            pl.BlockSpec((half, col.shape[1]), lambda i: (i, 0)),
            pl.BlockSpec(memory_space=pl.ANY),
        ],
        out_specs=(pl.BlockSpec((half, width), lambda i: (i, 0)), pl.BlockSpec((half, width), lambda i: (0, 0))),
        cost_estimate=pl.CostEstimate(flops=10 * rows * width, bytes_accessed=22 * rows * width, transcendentals=0),
        name="code",
    )(source_parts, hard_rows, own_target, col, other)
    hard_gate = hard_prob + 0.0 * coded[0, 0].astype(F32)
    side = hop_grp(coded, 0, 1)
    far = [hop_grp(coded_high, -dx, 0) for dx in (1, 2, 3)]
    low = jnp.stack([coded[:half], side[:half]])
    pairs = [hop_grp(low, -dx, 0) for dx in (1, 2, 3)]
    far_side = hop_grp(jnp.stack(far), 0, 1)
    blocks = jnp.stack([((x_at + dx) % 4) * 2 + (y_at ^ dy) for dx in range(4) for dy in range(2)])
    source_grad = decode_call(
        blocks, (bound * (1.0 / 32767.0))[:, None], [coded, side, *far, *pairs, far_side]
    )

    contribution = (hard_gate[:, None] * own_source.astype(F32)).astype(BF)
    outgoing = dot_f32(pick, contribution, ((0,), (0,))).astype(BF).reshape(owners, cap, width)
    incoming = lax.all_to_all(outgoing, ("grp", "blk"), 0, 0, tiled=True).reshape(slots, width)
    pool_grad = dot_f32(serve, incoming, ((0,), (0,)))
    return (row_loss, source_grad, target_grad, pool_grad)


def solution(mesh):
    in_specs = (P("blk", None), P(("grp", "blk"), None), P(("grp", "blk"), None), P("blk"), P("blk"), P())
    out_specs = (P("blk"), P("blk", None), P(("grp", "blk"), None), P(("grp", "blk"), None))
    return jax.shard_map(shards, mesh=mesh, in_specs=in_specs, out_specs=out_specs, check_vma=False)
```

```python
import jax
import jax.numpy as jnp
from jax import lax
from jax.experimental import pallas as pl
from jax.experimental.pallas import tpu as pltpu
from jax.sharding import PartitionSpec as P

BF, F32 = jnp.bfloat16, jnp.float32
NEG = -1e30
LOW = -3e38
TILE = 768
PART = 384
CHUNKS = (((0, 0), (0, 1)), ((1, 0), (3, 0)), ((2, 0), (1, 1)), ((3, 1), (2, 1)))


def hop_blk(value, dz, dy, dc):
    route = []
    for i in range(16):
        z, y, c = i // 4, (i // 2) % 2, i % 2
        route.append((i, ((z + dz) % 4) * 4 + (y ^ dy) * 2 + (c ^ dc)))
    return lax.ppermute(value, "blk", route)


def hop_grp(value, dx, dy):
    return lax.ppermute(value, "grp", [(i, ((i // 2 + dx) % 4) * 2 + ((i % 2) ^ dy)) for i in range(8)])


def dot_f32(a, b, dims):
    return lax.dot_general(a, b, (dims, ((), ())), preferred_element_type=F32)


def columns_of(rows):
    pad = jnp.zeros((120, rows.shape[1]), F32)
    return jnp.transpose(jnp.concatenate([rows, pad], axis=0))


def score_kernel(place, src, t0, t1, t2, t3, *refs):
    e_out, stat_out, tgt_ref, a_ref = refs[-4:]
    rows = t0.shape[0]
    half = 2 * rows
    step = pl.program_id(0)
    count = e_out.shape[1]

    @pl.when(step == 0)
    def _():
        top = jnp.zeros((1, 1), F32)
        for q, t in enumerate((t0, t1, t2, t3)):
            block = t[...]
            tgt_ref[q * rows : (q + 1) * rows, :] = block
            top = jnp.maximum(top, jnp.max(jnp.abs(block).astype(F32), keepdims=True))
        a_ref[...] = jnp.broadcast_to(top, a_ref.shape)

    tgt = tgt_ref[...]
    lane = lax.broadcasted_iota(jnp.int32, (PART, 128), 1)
    column = lax.broadcasted_iota(jnp.int32, (PART, 2 * half), 1)
    line = lax.broadcasted_iota(jnp.int32, (PART, 1), 0)
    parts = []
    for first in range(0, count, PART):
        ats = []
        for sub in range(2):
            k = step * (count // rows) + first // rows + sub
            at = jnp.int32(-(1 << 20))
            for q in range(4):
                at = jnp.where(place[q] == k, (q - sub) * rows, at)
            ats.append(at)
        hole = line + jnp.where(line < rows, ats[0], ats[1])
        here = pl.ds(first, PART)
        s = dot_f32(src[pl.ds(pl.multiple_of(step * count + first, PART), PART), :], tgt, ((1,), (1,)))
        s = jnp.where(column == hole, NEG, s)
        top = jnp.max(s, axis=1, keepdims=True)
        e = jnp.exp(s - top)
        total = jnp.sum(e, axis=1, keepdims=True)
        e_out[0, here, :] = e.astype(BF)
        parts.append(jnp.where(lane == 0, top, jnp.where(lane == 1, total, a_ref[0:1, :])))
    stat_out[...] = jnp.transpose(jnp.concatenate(parts, axis=0))[0:8, :]


def score_call(place, src, blocks, n, so_far):
    rows, width = blocks[0].shape
    total = src.shape[0]
    cols = 4 * rows
    so_far = list(so_far)
    return pl.pallas_call(
        score_kernel,
        out_shape=(
            pltpu.HBM((4, total, cols), BF),
            jax.ShapeDtypeStruct((8, total), F32),
        ),
        grid_spec=pltpu.PrefetchScalarGridSpec(
            num_scalar_prefetch=1,
            grid=(total // TILE,),
            in_specs=[pl.BlockSpec(memory_space=pltpu.VMEM)] * 5
            + [pl.BlockSpec(memory_space=pl.ANY)] * len(so_far),
            out_specs=(
                pl.BlockSpec((1, TILE, cols), lambda i, p: (n, i, 0)),
                pl.BlockSpec((8, TILE), lambda i, p: (0, i)),
            ),
            scratch_shapes=[pltpu.VMEM((cols, width), BF), pltpu.VMEM((8, 128), F32)],
        ),
        input_output_aliases={6: 0} if so_far else {},
        compiler_params=pltpu.CompilerParams(vmem_limit_bytes=24 << 20),
        cost_estimate=pl.CostEstimate(
            flops=2 * total * cols * width, bytes_accessed=total * (width + cols) * 2, transcendentals=total * cols
        ),
        name="scores",
    )(place, src, *blocks, *so_far)


def source_kernel(w_ref, e_ref, *refs):
    blocks, out, tgt = refs[:-2], refs[-2], refs[-1]
    rows = blocks[0].shape[0]

    @pl.when(pl.program_id(0) == 0)
    def _():
        for n, block in enumerate(blocks):
            tgt[n // 4, n % 4 * rows : (n % 4 + 1) * rows, :] = block[...]

    weights = columns_of(w_ref[...])
    total = None
    for c in range(4):
        part = dot_f32(e_ref[c], tgt[c], ((1,), (0,))) * weights[:, c : c + 1]
        total = part if total is None else total + part
    out[...] = total.astype(BF)


def source_call(weights, e_all, blocks):
    _, total, cols = e_all.shape
    rows, width = blocks[0].shape
    whole = pl.BlockSpec((rows, width), lambda i: (0, 0), pipeline_mode=pl.Buffered(1))
    return pl.pallas_call(
        source_kernel,
        out_shape=jax.ShapeDtypeStruct((total, width), BF),
        grid=(total // PART,),
        in_specs=[
            pl.BlockSpec((8, PART), lambda i: (0, i)),
            pl.BlockSpec((4, PART, cols), lambda i: (0, i, 0)),
        ]
        + [whole] * len(blocks),
        out_specs=pl.BlockSpec((PART, width), lambda i: (i, 0)),
        scratch_shapes=[pltpu.VMEM((4, cols, width), BF)],
        cost_estimate=pl.CostEstimate(
            flops=8 * total * cols * width, bytes_accessed=total * (8 * cols + 2 * width), transcendentals=0
        ),
        name="source_terms",
    )(weights, e_all, *blocks)


def target_kernel(place, w_ref, e_ref, src_ref, _, keep, give, acc, scaled, column):
    rows = acc.shape[0] // 4
    total = src_ref.shape[0]
    chunk = pl.program_id(0)

    @pl.when(chunk == 0)
    def _():
        for first in range(0, total, PART):
            here = slice(first, first + PART)
            column[here, :] = columns_of(w_ref[:, here])

    lane = lax.broadcasted_iota(jnp.int32, (PART, 128), 1)
    for first in range(0, total, PART):
        here = slice(first, first + PART)
        weight = jnp.sum(jnp.where(lane == chunk, column[here, :], 0.0), axis=1, keepdims=True)
        scaled[here, :] = (src_ref[here, :].astype(F32) * weight).astype(BF)
    acc[...] = dot_f32(e_ref[0], scaled[...], ((0,), (0,)))
    for q in range(4):
        at = place[chunk * 4 + q]

        @pl.when(at >= 0)
        def _():
            there = slice(q * rows, (q + 1) * rows)
            here = pl.ds(pl.multiple_of(at * rows, rows), rows)
            acc[there, :] = acc[there, :] + column[here, 4:5] * src_ref[here, :].astype(F32)

    keep[0] = acc[0 : 2 * rows, :]
    give[0] = acc[2 * rows : 4 * rows, :].astype(BF)


def target_call(place, weights, e_all, src, after):
    _, total, cols = e_all.shape
    width = src.shape[1]
    half = (4, cols // 2, width)
    half_spec = pl.BlockSpec((1, cols // 2, width), lambda i, p: (i, 0, 0))
    return pl.pallas_call(
        target_kernel,
        out_shape=(jax.ShapeDtypeStruct(half, F32), jax.ShapeDtypeStruct(half, BF)),
        grid_spec=pltpu.PrefetchScalarGridSpec(
            num_scalar_prefetch=1,
            grid=(4,),
            in_specs=[
                pl.BlockSpec((8, total), lambda i, p: (0, 0)),
                pl.BlockSpec((1, total, cols), lambda i, p: (i, 0, 0)),
                pl.BlockSpec((total, width), lambda i, p: (0, 0)),
                pl.BlockSpec(memory_space=pl.ANY),
            ],
            out_specs=(half_spec, half_spec),
            scratch_shapes=[
                pltpu.VMEM((cols, width), F32),
                pltpu.VMEM((total, width), BF),
                pltpu.VMEM((total, 128), F32),
            ],
        ),
        cost_estimate=pl.CostEstimate(
            flops=8 * total * cols * width, bytes_accessed=total * (width + 4 * cols) * 2 + cols * width * 12, transcendentals=0
        ),
        name="target_terms",
    )(place, weights, e_all, src, after)


def code_kernel(parts, hard, tgt, col, _a, _b, _c, out, high):
    total = hard[...] * col[:, 0:1] + tgt[...].astype(F32) * col[:, 1:2]
    for g in range(parts.shape[0]):
        total = total + parts[g].astype(F32) * col[:, 3 + g : 4 + g]
    scaled = jnp.clip(total * col[:, 2:3], -32767.0, 32767.0)
    coded = jnp.round(scaled).astype(jnp.int32).astype(jnp.int16)
    out[...] = coded
    high[...] = coded


def line_kernel(keep, got, m1, m2, m3, mine, other):
    rows = mine.shape[0]
    total = keep[0] + got[0].astype(F32)
    for part in (m1, m2, m3):
        total = total + part[...].astype(F32)
    mine[...] = total[:rows, :]
    other[...] = total[rows:, :].astype(BF)


def decode_kernel(order, scale, own, side, far1, far2, far3, pairs1, pairs2, pairs3, far_side, out):
    step = pl.program_id(0)
    half = own.shape[0] // 2
    far, pairs = (None, far1, far2, far3), (None, pairs1, pairs2, pairs3)
    for dx in range(4):
        for dy in range(2):

            @pl.when(step == dx * 2 + dy)
            def _():
                if dx == 0:
                    whole = (own if dy == 0 else side)[...]
                    out[...] = whole.astype(jnp.int32).astype(F32) * scale[...]
                else:
                    low = pairs[dx][dy]
                    high = far[dx][...] if dy == 0 else far_side[dx - 1]
                    out[0:half, :] = low.astype(jnp.int32).astype(F32) * scale[0:half, :]
                    out[half:, :] = high.astype(jnp.int32).astype(F32) * scale[half:, :]


def decode_call(order, scale, pieces):
    rows, width = pieces[0].shape
    total = scale.shape[0]
    return pl.pallas_call(
        decode_kernel,
        out_shape=jax.ShapeDtypeStruct((total, width), F32),
        grid_spec=pltpu.PrefetchScalarGridSpec(
            num_scalar_prefetch=1,
            grid=(total // rows,),
            in_specs=[pl.BlockSpec((rows, 1), lambda i, p: (p[i], 0))]
            + [pl.BlockSpec(x.shape, lambda i, p, n=x.ndim: (0,) * n) for x in pieces],
            out_specs=pl.BlockSpec((rows, width), lambda i, p: (p[i], 0)),
        ),
        compiler_params=pltpu.CompilerParams(vmem_limit_bytes=24 << 20),
        cost_estimate=pl.CostEstimate(flops=total * width, bytes_accessed=total * width * 6, transcendentals=0),
        name="decode",
    )(order, scale, *pieces)


def shards(source_emb, target_emb, hard_pool, hard_index, language, margin):
    total, width = source_emb.shape
    rows = target_emb.shape[0]
    blk, grp = lax.axis_index("blk"), lax.axis_index("grp")
    owners = 128
    cap = max(2, (2 * rows + owners - 1) // owners)
    slots = owners * cap
    z, y, c = blk // 4, (blk // 2) % 2, blk % 2

    start = grp * rows
    own_index = lax.dynamic_slice_in_dim(hard_index, start, rows, 0)
    own_source = lax.dynamic_slice_in_dim(source_emb, start, rows, 0)
    owner, pool_row = own_index // rows, own_index % rows
    position = jnp.arange(rows, dtype=jnp.int32)
    same = (owner[:, None] == owner[None, :]) & (position[None, :] < position[:, None])
    slot = owner * cap + jnp.sum(same.astype(jnp.int32), axis=1)
    at_slot = slot[:, None] == jnp.arange(slots, dtype=jnp.int32)[None, :]
    requests = jnp.sum(jnp.where(at_slot, pool_row[:, None] + 1, 0), axis=0) - 1
    wanted = lax.all_to_all(requests.reshape(owners, cap), ("grp", "blk"), 0, 0, tiled=True)
    lang_match = language[:, None] == jnp.arange(margin.shape[0], dtype=jnp.int32)[None, :]
    margin_row = jnp.sum(jnp.where(lang_match, margin[None, :], 0.0), axis=1)

    have = {(0, 0, 0): target_emb}
    have[0, 1, 0] = hop_blk(target_emb, 0, 1, 0)
    for dz in (1, 3, 2):
        have[dz, 0, 0] = hop_blk(target_emb, -dz, 0, 0)
    for dz in (1, 3, 2):
        have[dz, 1, 0] = hop_blk(have[0, 1, 0], -dz, 0, 0)
    for dz, dy in [pair for chunk in CHUNKS for pair in chunk]:
        have[dz, dy, 1] = hop_blk(have[dz, dy, 0], 0, 0, 1)

    holds = grp == blk // 2
    place = {}
    for dz in range(4):
        for dy in range(2):
            for dc in range(2):
                zz = (z + dz) % 4
                k = (zz % 2) * 4 + (y ^ dy) * 2 + (c ^ dc)
                place[dz, dy, dc] = jnp.where(holds & (zz // 2 == c), k, -1)
    order = [[(dz, dy, dc) for dc in (0, 1) for dz, dy in chunk] for chunk in CHUNKS]
    places = [jnp.stack([place[key] for key in chunk]) for chunk in order]
    flat = jnp.concatenate(places)

    stats, so_far = [], ()

    def add_chunk(n):
        nonlocal so_far
        e, stat = score_call(places[n], source_emb, [have[key] for key in order[n]], n, so_far)
        so_far = (e,)
        stats.append(stat)

    add_chunk(0)
    wanted, stats[0] = lax.optimization_barrier((wanted, stats[0]))
    serve = (wanted.reshape(slots)[:, None] == position[None, :]).astype(BF)
    served = dot_f32(serve, hard_pool, ((1,), (0,))).astype(BF).reshape(owners, cap, width)
    served, places[1] = lax.optimization_barrier((served, places[1]))
    fetched = lax.all_to_all(served, ("grp", "blk"), 0, 0, tiled=True).reshape(slots, width)
    add_chunk(1)
    early_target, stats[1] = lax.optimization_barrier((target_emb, stats[1]))
    own_target = lax.ppermute(
        early_target, ("grp", "blk"), [(16 * i + j, (j % 8) * 16 + 2 * i + j // 8) for i in range(8) for j in range(16)]
    )
    add_chunk(2)
    fetched, stats[2] = lax.optimization_barrier((fetched, stats[2]))
    pick = at_slot.astype(BF)
    hard_rows = dot_f32(pick, fetched, ((1,), (0,)))
    hard_score = jnp.sum(own_source.astype(F32) * hard_rows, axis=1)
    add_chunk(3)

    tops = jnp.stack([stat[0] for stat in stats])
    sums = jnp.stack([stat[1] for stat in stats])
    reach = jnp.maximum(jnp.max(jnp.stack([stat[2] for stat in stats]), axis=0), jnp.max(jnp.abs(hard_rows)))
    own_margin = lax.dynamic_slice_in_dim(margin_row, start, rows, 0)
    own_pos = jnp.sum(own_source.astype(F32) * own_target.astype(F32), axis=1) - own_margin
    pos = lax.dynamic_update_slice_in_dim(jnp.zeros((total,), F32), own_pos, start, 0)
    hard_all = lax.dynamic_update_slice_in_dim(jnp.full((total,), LOW, F32), hard_score, start, 0)
    soft_top = jnp.max(tops, axis=0)
    soft = jnp.sum(sums * jnp.exp(tops - soft_top), axis=0)
    mine = jnp.stack([soft_top, soft, pos, hard_all, reach] + [jnp.zeros((total,), F32)] * 3)
    everyone = lax.all_to_all(jnp.broadcast_to(mine[None], (8, 8, total)), "grp", 0, 0, tiled=True)
    source_part = source_call(jnp.concatenate([jnp.exp(tops - soft_top), jnp.zeros((4, total), F32)]), so_far[0],
        [have[key] for chunk in order for key in chunk])
    everyone, source_part = lax.optimization_barrier((everyone, source_part))
    source_parts = lax.all_to_all(source_part.reshape(8, rows, width), "grp", 0, 0, tiled=True)
    token = hop_blk(source_part[:16, :128], 0, 0, 1)
    pos = jnp.sum(everyone[:, 2], axis=0)
    hard_all = jnp.max(everyone[:, 3], axis=0)
    reach = jnp.max(everyone[:, 4], axis=0)
    top = jnp.maximum(jnp.max(everyone[:, 0], axis=0), jnp.maximum(pos, hard_all))
    off = jnp.sum(everyone[:, 1] * jnp.exp(everyone[:, 0] - top), axis=0) + jnp.exp(hard_all - top)
    log_total = top + jnp.log(off + jnp.exp(pos - top))
    row_loss = log_total - pos
    less = jnp.exp(pos - log_total) - 1.0
    diag_weight = jnp.where(holds, less, 0.0)

    x_at, y_at = grp // 2, grp % 2
    mass = jnp.abs(less) + off * jnp.exp(top - log_total)
    bound = jnp.maximum(1.01 * reach * mass, 1e-30)
    col = jnp.concatenate(
        [jnp.stack([jnp.exp(hard_all - log_total), less, 32767.0 / bound]), jnp.exp(everyone[:, 0] - log_total[None])]
    )
    col = lax.dynamic_slice_in_dim(col, start, rows, 1)
    hard_prob = col[0]
    col = jnp.transpose(col)
    half = rows // 2

    weights = jnp.concatenate([jnp.exp(tops - log_total), diag_weight[None], jnp.zeros((3, total), F32)])
    keep, give = target_call(flat, weights, so_far[0], source_emb, token)
    got = hop_blk(give, 0, 0, 1)
    where_at = {pair: (n, j) for n, chunk in enumerate(CHUNKS) for j, pair in enumerate(chunk)}

    def both(dz, dy):
        n, j = where_at[dz, dy]
        here = slice(j * rows, (j + 1) * rows)
        return (keep[n, here] + got[n, here].astype(F32)).astype(BF)

    leave = [jnp.concatenate([both(dz, 0), both(dz, 1)]) for dz in (1, 3, 2)]
    moved = [hop_blk(part, dz, 0, 0) for part, dz in zip(leave, (1, 3, 2))]
    whole = [pl.BlockSpec((1, 2 * rows, width), lambda i: (0, 0, 0))] * 2
    whole += [pl.BlockSpec((2 * rows, width), lambda i: (0, 0))] * 3
    mine, other = pl.pallas_call(
        line_kernel,
        out_shape=(jax.ShapeDtypeStruct((rows, width), F32), jax.ShapeDtypeStruct((rows, width), BF)),
        grid=(1,),
        in_specs=whole,
        out_specs=[pl.BlockSpec((rows, width), lambda i: (0, 0))] * 2,
        cost_estimate=pl.CostEstimate(flops=10 * rows * width, bytes_accessed=30 * rows * width, transcendentals=0),
        name="lines",
    )(keep, got, *moved)

    coded, coded_high = pl.pallas_call(
        code_kernel,
        out_shape=(jax.ShapeDtypeStruct((rows, width), jnp.int16), jax.ShapeDtypeStruct((half, width), jnp.int16)),
        grid=(2,),
        in_specs=[
            pl.BlockSpec((8, half, width), lambda i: (0, i, 0)),
            pl.BlockSpec((half, width), lambda i: (i, 0)),
            pl.BlockSpec((half, width), lambda i: (i, 0)),
            pl.BlockSpec((half, col.shape[1]), lambda i: (i, 0)),
        ]
        + [pl.BlockSpec(memory_space=pl.ANY)] * 3,
        out_specs=(pl.BlockSpec((half, width), lambda i: (i, 0)), pl.BlockSpec((half, width), lambda i: (0, 0))),
        cost_estimate=pl.CostEstimate(flops=10 * rows * width, bytes_accessed=22 * rows * width, transcendentals=0),
        name="code",
    )(source_parts, hard_rows, own_target, col, *leave)
    side = hop_grp(coded, 0, 1)
    far = [hop_grp(coded_high, -dx, 0) for dx in (1, 2, 3)]
    other, side, far = lax.optimization_barrier((other, side, far))
    hard_gate = hard_prob + 0.0 * side[0, 0].astype(F32)
    target_grad = mine + hop_blk(other, 0, 1, 0).astype(F32)
    low = jnp.stack([coded[:half], side[:half]])
    pairs = [hop_grp(low, -dx, 0) for dx in (1, 2, 3)]
    far_side = hop_grp(jnp.stack(far), 0, 1)
    blocks = jnp.stack([((x_at + dx) % 4) * 2 + (y_at ^ dy) for dx in range(4) for dy in range(2)])
    source_grad = decode_call(
        blocks, (bound * (1.0 / 32767.0))[:, None], [coded, side, *far, *pairs, far_side]
    )

    contribution = (hard_gate[:, None] * own_source.astype(F32)).astype(BF)
    outgoing = dot_f32(pick, contribution, ((0,), (0,))).astype(BF).reshape(owners, cap, width)
    incoming = lax.all_to_all(outgoing, ("grp", "blk"), 0, 0, tiled=True).reshape(slots, width)
    pool_grad = dot_f32(serve, incoming, ((0,), (0,)))
    return (row_loss, source_grad, target_grad, pool_grad)


def solution(mesh):
    in_specs = (P("blk", None), P(("grp", "blk"), None), P(("grp", "blk"), None), P("blk"), P("blk"), P())
    out_specs = (P("blk"), P("blk", None), P(("grp", "blk"), None), P(("grp", "blk"), None))
    return jax.shard_map(shards, mesh=mesh, in_specs=in_specs, out_specs=out_specs, check_vma=False)
```

```python
import jax
import jax.numpy as jnp
from jax import lax
from jax.experimental import pallas as pl
from jax.experimental.pallas import tpu as pltpu
from jax.sharding import PartitionSpec as P

BF, F32 = jnp.bfloat16, jnp.float32
NEG = -1e30
LOW = -3e38
TILE = 768
PART = 384
CHUNKS = (((0, 0), (0, 1)), ((1, 0), (3, 0)), ((2, 0), (1, 1)), ((3, 1), (2, 1)))


def hop_blk(value, dz, dy, dc):
    route = []
    for i in range(16):
        z, y, c = i // 4, (i // 2) % 2, i % 2
        route.append((i, ((z + dz) % 4) * 4 + (y ^ dy) * 2 + (c ^ dc)))
    return lax.ppermute(value, "blk", route)


def hop_grp(value, dx, dy):
    return lax.ppermute(value, "grp", [(i, ((i // 2 + dx) % 4) * 2 + ((i % 2) ^ dy)) for i in range(8)])


def dot_f32(a, b, dims):
    return lax.dot_general(a, b, (dims, ((), ())), preferred_element_type=F32)


def columns_of(rows):
    pad = jnp.zeros((120, rows.shape[1]), F32)
    return jnp.transpose(jnp.concatenate([rows, pad], axis=0))


def score_kernel(place, src, t0, t1, t2, t3, *refs):
    e_out, stat_out, tgt_ref, a_ref = refs[-4:]
    rows = t0.shape[0]
    half = 2 * rows
    step = pl.program_id(0)
    count = e_out.shape[1]

    @pl.when(step == 0)
    def _():
        top = jnp.zeros((1, 1), F32)
        for q, t in enumerate((t0, t1, t2, t3)):
            block = t[...]
            tgt_ref[q * rows : (q + 1) * rows, :] = block
            top = jnp.maximum(top, jnp.max(jnp.abs(block).astype(F32), keepdims=True))
        a_ref[...] = jnp.broadcast_to(top, a_ref.shape)

    tgt = tgt_ref[...]
    lane = lax.broadcasted_iota(jnp.int32, (PART, 128), 1)
    column = lax.broadcasted_iota(jnp.int32, (PART, 2 * half), 1)
    line = lax.broadcasted_iota(jnp.int32, (PART, 1), 0)
    parts = []
    for first in range(0, count, PART):
        ats = []
        for sub in range(2):
            k = step * (count // rows) + first // rows + sub
            at = jnp.int32(-(1 << 20))
            for q in range(4):
                at = jnp.where(place[q] == k, (q - sub) * rows, at)
            ats.append(at)
        hole = line + jnp.where(line < rows, ats[0], ats[1])
        here = pl.ds(first, PART)
        s = dot_f32(src[pl.ds(pl.multiple_of(step * count + first, PART), PART), :], tgt, ((1,), (1,)))
        s = jnp.where(column == hole, NEG, s)
        top = jnp.max(s, axis=1, keepdims=True)
        e = jnp.exp(s - top)
        total = jnp.sum(e, axis=1, keepdims=True)
        e_out[0, here, :] = e.astype(BF)
        parts.append(jnp.where(lane == 0, top, jnp.where(lane == 1, total, a_ref[0:1, :])))
    stat_out[...] = jnp.transpose(jnp.concatenate(parts, axis=0))[0:8, :]


def score_call(place, src, blocks, n, so_far):
    rows, width = blocks[0].shape
    total = src.shape[0]
    cols = 4 * rows
    so_far = list(so_far)
    return pl.pallas_call(
        score_kernel,
        out_shape=(
            pltpu.HBM((4, total, cols), BF),
            jax.ShapeDtypeStruct((8, total), F32),
        ),
        grid_spec=pltpu.PrefetchScalarGridSpec(
            num_scalar_prefetch=1,
            grid=(total // TILE,),
            in_specs=[pl.BlockSpec(memory_space=pltpu.VMEM)] * 5
            + [pl.BlockSpec(memory_space=pl.ANY)] * len(so_far),
            out_specs=(
                pl.BlockSpec((1, TILE, cols), lambda i, p: (n, i, 0)),
                pl.BlockSpec((8, TILE), lambda i, p: (0, i)),
            ),
            scratch_shapes=[pltpu.VMEM((cols, width), BF), pltpu.VMEM((8, 128), F32)],
        ),
        input_output_aliases={6: 0} if so_far else {},
        compiler_params=pltpu.CompilerParams(vmem_limit_bytes=24 << 20),
        cost_estimate=pl.CostEstimate(
            flops=2 * total * cols * width, bytes_accessed=total * (width + cols) * 2, transcendentals=total * cols
        ),
        name="scores",
    )(place, src, *blocks, *so_far)


def source_kernel(w_ref, e_ref, *refs):
    blocks, out, tgt = refs[:-2], refs[-2], refs[-1]
    rows = blocks[0].shape[0]

    @pl.when(pl.program_id(0) == 0)
    def _():
        for n, block in enumerate(blocks):
            tgt[n // 4, n % 4 * rows : (n % 4 + 1) * rows, :] = block[...]

    weights = columns_of(w_ref[...])
    total = None
    for c in range(4):
        part = dot_f32(e_ref[c], tgt[c], ((1,), (0,))) * weights[:, c : c + 1]
        total = part if total is None else total + part
    out[...] = total.astype(BF)


def source_call(weights, e_all, blocks):
    _, total, cols = e_all.shape
    rows, width = blocks[0].shape
    whole = pl.BlockSpec((rows, width), lambda i: (0, 0), pipeline_mode=pl.Buffered(1))
    return pl.pallas_call(
        source_kernel,
        out_shape=jax.ShapeDtypeStruct((total, width), BF),
        grid=(total // PART,),
        in_specs=[
            pl.BlockSpec((8, PART), lambda i: (0, i)),
            pl.BlockSpec((4, PART, cols), lambda i: (0, i, 0)),
        ]
        + [whole] * len(blocks),
        out_specs=pl.BlockSpec((PART, width), lambda i: (i, 0)),
        scratch_shapes=[pltpu.VMEM((4, cols, width), BF)],
        cost_estimate=pl.CostEstimate(
            flops=8 * total * cols * width, bytes_accessed=total * (8 * cols + 2 * width), transcendentals=0
        ),
        name="source_terms",
    )(weights, e_all, *blocks)


def target_kernel(place, w_ref, e_ref, src_ref, _, keep, give, acc, scaled, column):
    rows = acc.shape[0] // 4
    total = src_ref.shape[0]
    chunk = pl.program_id(0)

    @pl.when(chunk == 0)
    def _():
        for first in range(0, total, PART):
            here = slice(first, first + PART)
            column[here, :] = columns_of(w_ref[:, here])

    lane = lax.broadcasted_iota(jnp.int32, (PART, 128), 1)
    for first in range(0, total, PART):
        here = slice(first, first + PART)
        weight = jnp.sum(jnp.where(lane == chunk, column[here, :], 0.0), axis=1, keepdims=True)
        scaled[here, :] = (src_ref[here, :].astype(F32) * weight).astype(BF)
    acc[...] = dot_f32(e_ref[0], scaled[...], ((0,), (0,)))
    for q in range(4):
        at = place[chunk * 4 + q]

        @pl.when(at >= 0)
        def _():
            there = slice(q * rows, (q + 1) * rows)
            here = pl.ds(pl.multiple_of(at * rows, rows), rows)
            acc[there, :] = acc[there, :] + column[here, 4:5] * src_ref[here, :].astype(F32)

    keep[0] = acc[0 : 2 * rows, :]
    give[0] = acc[2 * rows : 4 * rows, :].astype(BF)


def target_call(place, weights, e_all, src, after):
    _, total, cols = e_all.shape
    width = src.shape[1]
    half = (4, cols // 2, width)
    half_spec = pl.BlockSpec((1, cols // 2, width), lambda i, p: (i, 0, 0))
    return pl.pallas_call(
        target_kernel,
        out_shape=(jax.ShapeDtypeStruct(half, F32), jax.ShapeDtypeStruct(half, BF)),
        grid_spec=pltpu.PrefetchScalarGridSpec(
            num_scalar_prefetch=1,
            grid=(4,),
            in_specs=[
                pl.BlockSpec((8, total), lambda i, p: (0, 0)),
                pl.BlockSpec((1, total, cols), lambda i, p: (i, 0, 0)),
                pl.BlockSpec((total, width), lambda i, p: (0, 0)),
                pl.BlockSpec(memory_space=pl.ANY),
            ],
            out_specs=(half_spec, half_spec),
            scratch_shapes=[
                pltpu.VMEM((cols, width), F32),
                pltpu.VMEM((total, width), BF),
                pltpu.VMEM((total, 128), F32),
            ],
        ),
        cost_estimate=pl.CostEstimate(
            flops=8 * total * cols * width, bytes_accessed=total * (width + 4 * cols) * 2 + cols * width * 12, transcendentals=0
        ),
        name="target_terms",
    )(place, weights, e_all, src, after)


def code_kernel(parts, hard, tgt, col, *refs):
    out, high = refs[-2:]
    total = hard[...] * col[:, 0:1] + tgt[...].astype(F32) * col[:, 1:2]
    for g in range(parts.shape[0]):
        total = total + parts[g].astype(F32) * col[:, 3 + g : 4 + g]
    scaled = jnp.clip(total * col[:, 2:3], -32767.0, 32767.0)
    coded = jnp.round(scaled).astype(jnp.int32).astype(jnp.int16)
    out[...] = coded
    high[...] = coded


def line_kernel(keep, got, m1, m2, m3, mine, other):
    rows = mine.shape[0]
    total = keep[0] + got[0].astype(F32)
    for part in (m1, m2, m3):
        total = total + part[...].astype(F32)
    mine[...] = total[:rows, :]
    other[...] = total[rows:, :].astype(BF)


def decode_kernel(order, scale, own, side, far1, far2, far3, pairs1, pairs2, pairs3, far_side, out):
    step = pl.program_id(0)
    half = own.shape[0] // 2
    far, pairs = (None, far1, far2, far3), (None, pairs1, pairs2, pairs3)
    for dx in range(4):
        for dy in range(2):

            @pl.when(step == dx * 2 + dy)
            def _():
                if dx == 0:
                    whole = (own if dy == 0 else side)[...]
                    out[...] = whole.astype(jnp.int32).astype(F32) * scale[...]
                else:
                    low = pairs[dx][dy]
                    high = far[dx][...] if dy == 0 else far_side[dx - 1]
                    out[0:half, :] = low.astype(jnp.int32).astype(F32) * scale[0:half, :]
                    out[half:, :] = high.astype(jnp.int32).astype(F32) * scale[half:, :]


def decode_call(order, scale, pieces):
    rows, width = pieces[0].shape
    total = scale.shape[0]
    return pl.pallas_call(
        decode_kernel,
        out_shape=jax.ShapeDtypeStruct((total, width), F32),
        grid_spec=pltpu.PrefetchScalarGridSpec(
            num_scalar_prefetch=1,
            grid=(total // rows,),
            in_specs=[pl.BlockSpec((rows, 1), lambda i, p: (p[i], 0))]
            + [pl.BlockSpec(x.shape, lambda i, p, n=x.ndim: (0,) * n) for x in pieces],
            out_specs=pl.BlockSpec((rows, width), lambda i, p: (p[i], 0)),
        ),
        compiler_params=pltpu.CompilerParams(vmem_limit_bytes=24 << 20),
        cost_estimate=pl.CostEstimate(flops=total * width, bytes_accessed=total * width * 6, transcendentals=0),
        name="decode",
    )(order, scale, *pieces)


def shards(source_emb, target_emb, hard_pool, hard_index, language, margin):
    total, width = source_emb.shape
    rows = target_emb.shape[0]
    blk, grp = lax.axis_index("blk"), lax.axis_index("grp")
    owners = 128
    cap = max(2, (2 * rows + owners - 1) // owners)
    slots = owners * cap
    z, y, c = blk // 4, (blk // 2) % 2, blk % 2

    start = grp * rows
    own_index = lax.dynamic_slice_in_dim(hard_index, start, rows, 0)
    own_source = lax.dynamic_slice_in_dim(source_emb, start, rows, 0)
    owner, pool_row = own_index // rows, own_index % rows
    position = jnp.arange(rows, dtype=jnp.int32)
    same = (owner[:, None] == owner[None, :]) & (position[None, :] < position[:, None])
    slot = owner * cap + jnp.sum(same.astype(jnp.int32), axis=1)
    pick = (slot[:, None] == jnp.arange(slots, dtype=jnp.int32)[None, :]).astype(BF)
    lane = jnp.arange(128, dtype=jnp.int32)[None, :]
    note = jnp.where(lane == 0, pool_row[:, None] + 1, jnp.where(lane == 1, position[:, None], 0)).astype(BF)
    sent = dot_f32(pick, jnp.concatenate([own_source, note], axis=1), ((0,), (0,))).astype(BF)
    sent = sent.reshape(owners, cap, width + 128)
    asked = lax.all_to_all(sent, ("grp", "blk"), 0, 0, tiled=True)

    lang_match = language[:, None] == jnp.arange(margin.shape[0], dtype=jnp.int32)[None, :]
    margin_row = jnp.sum(jnp.where(lang_match, margin[None, :], 0.0), axis=1)

    have = {(0, 0, 0): target_emb}
    have[0, 1, 0] = hop_blk(target_emb, 0, 1, 0)
    for dz in (1, 3, 2):
        have[dz, 0, 0] = hop_blk(target_emb, -dz, 0, 0)
    for dz in (1, 3, 2):
        have[dz, 1, 0] = hop_blk(have[0, 1, 0], -dz, 0, 0)
    for dz, dy in [pair for chunk in CHUNKS for pair in chunk]:
        have[dz, dy, 1] = hop_blk(have[dz, dy, 0], 0, 0, 1)

    holds = grp == blk // 2
    place = {}
    for dz in range(4):
        for dy in range(2):
            for dc in range(2):
                zz = (z + dz) % 4
                k = (zz % 2) * 4 + (y ^ dy) * 2 + (c ^ dc)
                place[dz, dy, dc] = jnp.where(holds & (zz // 2 == c), k, -1)
    order = [[(dz, dy, dc) for dc in (0, 1) for dz, dy in chunk] for chunk in CHUNKS]
    places = [jnp.stack([place[key] for key in chunk]) for chunk in order]
    flat = jnp.concatenate(places)

    stats, so_far = [], ()

    def add_chunk(n):
        nonlocal so_far
        e, stat = score_call(places[n], source_emb, [have[key] for key in order[n]], n, so_far)
        so_far = (e,)
        stats.append(stat)

    add_chunk(0)
    add_chunk(1)
    asked, stats[1] = lax.optimization_barrier((asked, stats[1]))
    asked = asked.reshape(slots, width + 128)
    asker_rows = asked[:, :width]
    pool_at = asked[:, width].astype(jnp.int32) - 1
    asker_at = asked[:, width + 1].astype(jnp.int32)
    serve = (pool_at[:, None] == position[None, :]).astype(BF)
    served = dot_f32(serve, hard_pool, ((1,), (0,))).astype(BF)
    served, places[2] = lax.optimization_barrier((served, places[2]))
    fetched = lax.all_to_all(served.reshape(owners, cap, width), ("grp", "blk"), 0, 0, tiled=True)
    early_target, stats[1] = lax.optimization_barrier((target_emb, stats[1]))
    own_target = lax.ppermute(
        early_target, ("grp", "blk"), [(16 * i + j, (j % 8) * 16 + 2 * i + j // 8) for i in range(8) for j in range(16)]
    )
    add_chunk(2)
    add_chunk(3)
    fetched, stats[3] = lax.optimization_barrier((fetched, stats[3]))
    hard_rows = dot_f32(pick, fetched.reshape(slots, width), ((1,), (0,)))
    hard_score = jnp.sum(own_source.astype(F32) * hard_rows, axis=1)

    tops = jnp.stack([stat[0] for stat in stats])
    sums = jnp.stack([stat[1] for stat in stats])
    reach = jnp.maximum(jnp.max(jnp.stack([stat[2] for stat in stats]), axis=0), jnp.max(jnp.abs(hard_rows)))
    own_margin = lax.dynamic_slice_in_dim(margin_row, start, rows, 0)
    own_pos = jnp.sum(own_source.astype(F32) * own_target.astype(F32), axis=1) - own_margin
    pos = lax.dynamic_update_slice_in_dim(jnp.zeros((total,), F32), own_pos, start, 0)
    hard_all = lax.dynamic_update_slice_in_dim(jnp.full((total,), LOW, F32), hard_score, start, 0)
    soft_top = jnp.max(tops, axis=0)
    soft = jnp.sum(sums * jnp.exp(tops - soft_top), axis=0)
    mine = jnp.stack([soft_top, soft, pos, hard_all, reach] + [jnp.zeros((total,), F32)] * 3)
    everyone = lax.all_to_all(jnp.broadcast_to(mine[None], (8, 8, total)), "grp", 0, 0, tiled=True)
    source_part = source_call(jnp.concatenate([jnp.exp(tops - soft_top), jnp.zeros((4, total), F32)]), so_far[0],
        [have[key] for chunk in order for key in chunk])
    everyone, source_part = lax.optimization_barrier((everyone, source_part))
    source_parts = lax.all_to_all(source_part.reshape(8, rows, width), "grp", 0, 0, tiled=True)
    token = hop_blk(source_part[:16, :128], 0, 0, 1)
    pos = jnp.sum(everyone[:, 2], axis=0)
    hard_all = jnp.max(everyone[:, 3], axis=0)
    reach = jnp.max(everyone[:, 4], axis=0)
    top = jnp.maximum(jnp.max(everyone[:, 0], axis=0), jnp.maximum(pos, hard_all))
    off = jnp.sum(everyone[:, 1] * jnp.exp(everyone[:, 0] - top), axis=0) + jnp.exp(hard_all - top)
    log_total = top + jnp.log(off + jnp.exp(pos - top))
    row_loss = log_total - pos
    less = jnp.exp(pos - log_total) - 1.0
    diag_weight = jnp.where(holds, less, 0.0)

    x_at, y_at = grp // 2, grp % 2
    mass = jnp.abs(less) + off * jnp.exp(top - log_total)
    bound = jnp.maximum(1.01 * reach * mass, 1e-30)
    col = jnp.concatenate(
        [jnp.stack([jnp.exp(hard_all - log_total), less, 32767.0 / bound]), jnp.exp(everyone[:, 0] - log_total[None])]
    )
    col = lax.dynamic_slice_in_dim(col, start, rows, 1)
    col = jnp.transpose(col)
    half = rows // 2

    weights = jnp.concatenate([jnp.exp(tops - log_total), diag_weight[None], jnp.zeros((3, total), F32)])
    keep, give = target_call(flat, weights, so_far[0], source_emb, token)
    got = hop_blk(give, 0, 0, 1)
    where_at = {pair: (n, j) for n, chunk in enumerate(CHUNKS) for j, pair in enumerate(chunk)}

    def both(dz, dy):
        n, j = where_at[dz, dy]
        here = slice(j * rows, (j + 1) * rows)
        return (keep[n, here] + got[n, here].astype(F32)).astype(BF)

    leave = [jnp.concatenate([both(dz, 0), both(dz, 1)]) for dz in (1, 3, 2)]
    moved = [hop_blk(part, dz, 0, 0) for part, dz in zip(leave, (1, 3, 2))]
    whole = [pl.BlockSpec((1, 2 * rows, width), lambda i: (0, 0, 0))] * 2
    whole += [pl.BlockSpec((2 * rows, width), lambda i: (0, 0))] * 3
    mine, other = pl.pallas_call(
        line_kernel,
        out_shape=(jax.ShapeDtypeStruct((rows, width), F32), jax.ShapeDtypeStruct((rows, width), BF)),
        grid=(1,),
        in_specs=whole,
        out_specs=[pl.BlockSpec((rows, width), lambda i: (0, 0))] * 2,
        cost_estimate=pl.CostEstimate(flops=10 * rows * width, bytes_accessed=30 * rows * width, transcendentals=0),
        name="lines",
    )(keep, got, *moved)

    coded, coded_high = pl.pallas_call(
        code_kernel,
        out_shape=(jax.ShapeDtypeStruct((rows, width), jnp.int16), jax.ShapeDtypeStruct((half, width), jnp.int16)),
        grid=(2,),
        in_specs=[
            pl.BlockSpec((8, half, width), lambda i: (0, i, 0)),
            pl.BlockSpec((half, width), lambda i: (i, 0)),
            pl.BlockSpec((half, width), lambda i: (i, 0)),
            pl.BlockSpec((half, col.shape[1]), lambda i: (i, 0)),
        ]
        + [pl.BlockSpec(memory_space=pl.ANY)] * 3,
        out_specs=(pl.BlockSpec((half, width), lambda i: (i, 0)), pl.BlockSpec((half, width), lambda i: (0, 0))),
        cost_estimate=pl.CostEstimate(flops=10 * rows * width, bytes_accessed=22 * rows * width, transcendentals=0),
        name="code",
    )(source_parts, hard_rows, own_target, col, *leave)
    side = hop_grp(coded, 0, 1)
    far = [hop_grp(coded_high, -dx, 0) for dx in (1, 2, 3)]
    other, side, far, late_logs = lax.optimization_barrier((other, side, far, log_total))
    target_grad = mine + hop_blk(other, 0, 1, 0).astype(F32)
    low = jnp.stack([coded[:half], side[:half]])
    pairs = [hop_grp(low, -dx, 0) for dx in (1, 2, 3)]
    far_side = hop_grp(jnp.stack(far), 0, 1)
    blocks = jnp.stack([((x_at + dx) % 4) * 2 + (y_at ^ dy) for dx in range(4) for dy in range(2)])
    source_grad = decode_call(
        blocks, (bound * (1.0 / 32767.0))[:, None], [coded, side, *far, *pairs, far_side]
    )

    all_logs = lax.all_to_all(jnp.broadcast_to(late_logs[None], (16, total)), "blk", 0, 0, tiled=True)
    at_group = jnp.arange(8, dtype=jnp.int32)[:, None, None, None] * rows
    at_row = at_group + asker_at.reshape(8, 16, cap, 1)
    match = at_row == jnp.arange(total, dtype=jnp.int32)[None, None, None, :]
    asked_log = jnp.sum(jnp.where(match, all_logs[None, :, None, :], 0.0), axis=3).reshape(slots)
    asked_score = jnp.sum(asker_rows.astype(F32) * served.astype(F32), axis=1)
    asked_prob = jnp.where(pool_at >= 0, jnp.exp(jnp.where(pool_at >= 0, asked_score - asked_log, LOW)), 0.0)
    pool_terms = (asked_prob[:, None] * asker_rows.astype(F32)).astype(BF)
    pool_grad = dot_f32(serve, pool_terms, ((0,), (0,)))
    return (row_loss, source_grad, target_grad, pool_grad)


def solution(mesh):
    in_specs = (P("blk", None), P(("grp", "blk"), None), P(("grp", "blk"), None), P("blk"), P("blk"), P())
    out_specs = (P("blk"), P("blk", None), P(("grp", "blk"), None), P(("grp", "blk"), None))
    return jax.shard_map(shards, mesh=mesh, in_specs=in_specs, out_specs=out_specs, check_vma=False)
```

```python
import jax
import jax.numpy as jnp
from jax import lax
from jax.experimental import pallas as pl
from jax.experimental.pallas import tpu as pltpu
from jax.sharding import PartitionSpec as P

BF, F32 = jnp.bfloat16, jnp.float32
NEG = -1e30
LOW = -3e38
TILE = 768
PART = 384
CHUNKS = (((0, 0), (0, 1)), ((1, 0), (3, 0)), ((2, 0), (1, 1)), ((3, 1), (2, 1)))


def hop_blk(value, dz, dy, dc):
    route = []
    for i in range(16):
        z, y, c = i // 4, (i // 2) % 2, i % 2
        route.append((i, ((z + dz) % 4) * 4 + (y ^ dy) * 2 + (c ^ dc)))
    return lax.ppermute(value, "blk", route)


def hop_grp(value, dx, dy):
    return lax.ppermute(value, "grp", [(i, ((i // 2 + dx) % 4) * 2 + ((i % 2) ^ dy)) for i in range(8)])


def dot_f32(a, b, dims):
    return lax.dot_general(a, b, (dims, ((), ())), preferred_element_type=F32)


def columns_of(rows):
    pad = jnp.zeros((120, rows.shape[1]), F32)
    return jnp.transpose(jnp.concatenate([rows, pad], axis=0))


def score_kernel(place, src, t0, t1, t2, t3, *refs):
    e_out, stat_out, tgt_ref, a_ref = refs[-4:]
    rows = t0.shape[0]
    half = 2 * rows
    step = pl.program_id(0)
    count = e_out.shape[1]

    @pl.when(step == 0)
    def _():
        top = jnp.zeros((1, 1), F32)
        for q, t in enumerate((t0, t1, t2, t3)):
            block = t[...]
            tgt_ref[q * rows : (q + 1) * rows, :] = block
            top = jnp.maximum(top, jnp.max(jnp.abs(block).astype(F32), keepdims=True))
        a_ref[...] = jnp.broadcast_to(top, a_ref.shape)

    tgt = tgt_ref[...]
    lane = lax.broadcasted_iota(jnp.int32, (PART, 128), 1)
    column = lax.broadcasted_iota(jnp.int32, (PART, 2 * half), 1)
    line = lax.broadcasted_iota(jnp.int32, (PART, 1), 0)
    parts = []
    for first in range(0, count, PART):
        ats = []
        for sub in range(2):
            k = step * (count // rows) + first // rows + sub
            at = jnp.int32(-(1 << 20))
            for q in range(4):
                at = jnp.where(place[q] == k, (q - sub) * rows, at)
            ats.append(at)
        hole = line + jnp.where(line < rows, ats[0], ats[1])
        here = pl.ds(first, PART)
        s = dot_f32(src[pl.ds(pl.multiple_of(step * count + first, PART), PART), :], tgt, ((1,), (1,)))
        s = jnp.where(column == hole, NEG, s)
        top = jnp.max(s, axis=1, keepdims=True)
        e = jnp.exp(s - top)
        total = jnp.sum(e, axis=1, keepdims=True)
        e_out[0, here, :] = e.astype(BF)
        parts.append(jnp.where(lane == 0, top, jnp.where(lane == 1, total, a_ref[0:1, :])))
    stat_out[...] = jnp.transpose(jnp.concatenate(parts, axis=0))[0:8, :]


def score_call(place, src, blocks, n, so_far):
    rows, width = blocks[0].shape
    total = src.shape[0]
    cols = 4 * rows
    so_far = list(so_far)
    return pl.pallas_call(
        score_kernel,
        out_shape=(
            pltpu.HBM((4, total, cols), BF),
            jax.ShapeDtypeStruct((8, total), F32),
        ),
        grid_spec=pltpu.PrefetchScalarGridSpec(
            num_scalar_prefetch=1,
            grid=(total // TILE,),
            in_specs=[pl.BlockSpec(memory_space=pltpu.VMEM)] * 5
            + [pl.BlockSpec(memory_space=pl.ANY)] * len(so_far),
            out_specs=(
                pl.BlockSpec((1, TILE, cols), lambda i, p: (n, i, 0)),
                pl.BlockSpec((8, TILE), lambda i, p: (0, i)),
            ),
            scratch_shapes=[pltpu.VMEM((cols, width), BF), pltpu.VMEM((8, 128), F32)],
        ),
        input_output_aliases={6: 0} if so_far else {},
        compiler_params=pltpu.CompilerParams(vmem_limit_bytes=24 << 20),
        cost_estimate=pl.CostEstimate(
            flops=2 * total * cols * width, bytes_accessed=total * (width + cols) * 2, transcendentals=total * cols
        ),
        name="scores",
    )(place, src, *blocks, *so_far)


def source_kernel(w_ref, e_ref, *refs):
    blocks, out, tgt = refs[:-2], refs[-2], refs[-1]
    rows = blocks[0].shape[0]

    @pl.when(pl.program_id(0) == 0)
    def _():
        for n, block in enumerate(blocks):
            tgt[n // 4, n % 4 * rows : (n % 4 + 1) * rows, :] = block[...]

    weights = columns_of(w_ref[...])
    total = None
    for c in range(4):
        part = dot_f32(e_ref[c], tgt[c], ((1,), (0,))) * weights[:, c : c + 1]
        total = part if total is None else total + part
    out[...] = total.astype(BF)


def source_call(weights, e_all, blocks):
    _, total, cols = e_all.shape
    rows, width = blocks[0].shape
    whole = pl.BlockSpec((rows, width), lambda i: (0, 0), pipeline_mode=pl.Buffered(1))
    return pl.pallas_call(
        source_kernel,
        out_shape=jax.ShapeDtypeStruct((total, width), BF),
        grid=(total // PART,),
        in_specs=[
            pl.BlockSpec((8, PART), lambda i: (0, i)),
            pl.BlockSpec((4, PART, cols), lambda i: (0, i, 0)),
        ]
        + [whole] * len(blocks),
        out_specs=pl.BlockSpec((PART, width), lambda i: (i, 0)),
        scratch_shapes=[pltpu.VMEM((4, cols, width), BF)],
        cost_estimate=pl.CostEstimate(
            flops=8 * total * cols * width, bytes_accessed=total * (8 * cols + 2 * width), transcendentals=0
        ),
        name="source_terms",
    )(weights, e_all, *blocks)


def target_kernel(place, w_ref, e_ref, src_ref, _, keep, give, acc, scaled, column):
    rows = acc.shape[0] // 4
    total = src_ref.shape[0]
    chunk = pl.program_id(0)

    @pl.when(chunk == 0)
    def _():
        for first in range(0, total, PART):
            here = slice(first, first + PART)
            column[here, :] = columns_of(w_ref[:, here])

    lane = lax.broadcasted_iota(jnp.int32, (PART, 128), 1)
    for first in range(0, total, PART):
        here = slice(first, first + PART)
        weight = jnp.sum(jnp.where(lane == chunk, column[here, :], 0.0), axis=1, keepdims=True)
        scaled[here, :] = (src_ref[here, :].astype(F32) * weight).astype(BF)
    acc[...] = dot_f32(e_ref[0], scaled[...], ((0,), (0,)))
    for q in range(4):
        at = place[chunk * 4 + q]

        @pl.when(at >= 0)
        def _():
            there = slice(q * rows, (q + 1) * rows)
            here = pl.ds(pl.multiple_of(at * rows, rows), rows)
            acc[there, :] = acc[there, :] + column[here, 4:5] * src_ref[here, :].astype(F32)

    keep[0] = acc[0 : 2 * rows, :]
    give[0] = acc[2 * rows : 4 * rows, :].astype(BF)


def target_call(place, weights, e_all, src, after):
    _, total, cols = e_all.shape
    width = src.shape[1]
    half = (4, cols // 2, width)
    half_spec = pl.BlockSpec((1, cols // 2, width), lambda i, p: (i, 0, 0))
    return pl.pallas_call(
        target_kernel,
        out_shape=(jax.ShapeDtypeStruct(half, F32), jax.ShapeDtypeStruct(half, BF)),
        grid_spec=pltpu.PrefetchScalarGridSpec(
            num_scalar_prefetch=1,
            grid=(4,),
            in_specs=[
                pl.BlockSpec((8, total), lambda i, p: (0, 0)),
                pl.BlockSpec((1, total, cols), lambda i, p: (i, 0, 0)),
                pl.BlockSpec((total, width), lambda i, p: (0, 0)),
                pl.BlockSpec(memory_space=pl.ANY),
            ],
            out_specs=(half_spec, half_spec),
            scratch_shapes=[
                pltpu.VMEM((cols, width), F32),
                pltpu.VMEM((total, width), BF),
                pltpu.VMEM((total, 128), F32),
            ],
        ),
        cost_estimate=pl.CostEstimate(
            flops=8 * total * cols * width, bytes_accessed=total * (width + 4 * cols) * 2 + cols * width * 12, transcendentals=0
        ),
        name="target_terms",
    )(place, weights, e_all, src, after)


def code_kernel(parts, hard, tgt, col, _a, _b, _c, out, high):
    total = hard[...] * col[:, 0:1] + tgt[...].astype(F32) * col[:, 1:2]
    for g in range(parts.shape[0]):
        total = total + parts[g].astype(F32) * col[:, 3 + g : 4 + g]
    scaled = jnp.clip(total * col[:, 2:3], -32767.0, 32767.0)
    coded = jnp.round(scaled).astype(jnp.int32).astype(jnp.int16)
    out[...] = coded
    high[...] = coded


def line_kernel(keep, got, m1, m2, m3, mine, other):
    rows = mine.shape[0]
    total = keep[0] + got[0].astype(F32)
    for part in (m1, m2, m3):
        total = total + part[...].astype(F32)
    mine[...] = total[:rows, :]
    other[...] = total[rows:, :].astype(BF)


def decode_kernel(order, scale, own, side, far1, far2, far3, pairs1, pairs2, pairs3, far_side, out):
    step = pl.program_id(0)
    half = own.shape[0] // 2
    far, pairs = (None, far1, far2, far3), (None, pairs1, pairs2, pairs3)
    for dx in range(4):
        for dy in range(2):

            @pl.when(step == dx * 2 + dy)
            def _():
                if dx == 0:
                    whole = (own if dy == 0 else side)[...]
                    out[...] = whole.astype(jnp.int32).astype(F32) * scale[...]
                else:
                    low = pairs[dx][dy]
                    high = far[dx][...] if dy == 0 else far_side[dx - 1]
                    out[0:half, :] = low.astype(jnp.int32).astype(F32) * scale[0:half, :]
                    out[half:, :] = high.astype(jnp.int32).astype(F32) * scale[half:, :]


def decode_call(order, scale, pieces):
    rows, width = pieces[0].shape
    total = scale.shape[0]
    return pl.pallas_call(
        decode_kernel,
        out_shape=jax.ShapeDtypeStruct((total, width), F32),
        grid_spec=pltpu.PrefetchScalarGridSpec(
            num_scalar_prefetch=1,
            grid=(total // rows,),
            in_specs=[pl.BlockSpec((rows, 1), lambda i, p: (p[i], 0))]
            + [pl.BlockSpec(x.shape, lambda i, p, n=x.ndim: (0,) * n) for x in pieces],
            out_specs=pl.BlockSpec((rows, width), lambda i, p: (p[i], 0)),
        ),
        compiler_params=pltpu.CompilerParams(vmem_limit_bytes=24 << 20),
        cost_estimate=pl.CostEstimate(flops=total * width, bytes_accessed=total * width * 6, transcendentals=0),
        name="decode",
    )(order, scale, *pieces)


def shards(source_emb, target_emb, hard_pool, hard_index, language, margin):
    total, width = source_emb.shape
    rows = target_emb.shape[0]
    blk, grp = lax.axis_index("blk"), lax.axis_index("grp")
    owners = 128
    cap = max(2, (2 * rows + owners - 1) // owners)
    slots = owners * cap
    z, y, c = blk // 4, (blk // 2) % 2, blk % 2

    start = grp * rows
    own_index = lax.dynamic_slice_in_dim(hard_index, start, rows, 0)
    own_source = lax.dynamic_slice_in_dim(source_emb, start, rows, 0)
    owner, pool_row = own_index // rows, own_index % rows
    position = jnp.arange(rows, dtype=jnp.int32)
    same = (owner[:, None] == owner[None, :]) & (position[None, :] < position[:, None])
    slot = owner * cap + jnp.sum(same.astype(jnp.int32), axis=1)
    at_slot = slot[:, None] == jnp.arange(slots, dtype=jnp.int32)[None, :]
    requests = jnp.sum(jnp.where(at_slot, pool_row[:, None] + 1, 0), axis=0) - 1
    wanted = lax.all_to_all(requests.reshape(owners, cap), ("grp", "blk"), 0, 0, tiled=True)
    lang_match = language[:, None] == jnp.arange(margin.shape[0], dtype=jnp.int32)[None, :]
    margin_row = jnp.sum(jnp.where(lang_match, margin[None, :], 0.0), axis=1)

    have = {(0, 0, 0): target_emb}
    have[0, 1, 0] = hop_blk(target_emb, 0, 1, 0)
    for dz in (1, 3, 2):
        have[dz, 0, 0] = hop_blk(target_emb, -dz, 0, 0)
    for dz in (1, 3, 2):
        have[dz, 1, 0] = hop_blk(have[0, 1, 0], -dz, 0, 0)
    for dz, dy in [pair for chunk in CHUNKS for pair in chunk]:
        have[dz, dy, 1] = hop_blk(have[dz, dy, 0], 0, 0, 1)

    holds = grp == blk // 2
    place = {}
    for dz in range(4):
        for dy in range(2):
            for dc in range(2):
                zz = (z + dz) % 4
                k = (zz % 2) * 4 + (y ^ dy) * 2 + (c ^ dc)
                place[dz, dy, dc] = jnp.where(holds & (zz // 2 == c), k, -1)
    order = [[(dz, dy, dc) for dc in (0, 1) for dz, dy in chunk] for chunk in CHUNKS]
    places = [jnp.stack([place[key] for key in chunk]) for chunk in order]
    flat = jnp.concatenate(places)

    stats, so_far = [], ()

    def add_chunk(n):
        nonlocal so_far
        e, stat = score_call(places[n], source_emb, [have[key] for key in order[n]], n, so_far)
        so_far = (e,)
        stats.append(stat)

    add_chunk(0)
    wanted, stats[0] = lax.optimization_barrier((wanted, stats[0]))
    serve = (wanted.reshape(slots)[:, None] == position[None, :]).astype(BF)
    served = dot_f32(serve, hard_pool, ((1,), (0,))).astype(BF).reshape(owners, cap, width)
    served, places[1] = lax.optimization_barrier((served, places[1]))
    fetched = lax.all_to_all(served, ("grp", "blk"), 0, 0, tiled=True).reshape(slots, width)
    add_chunk(1)
    early_target, stats[1] = lax.optimization_barrier((target_emb, stats[1]))
    own_target = lax.ppermute(
        early_target, ("grp", "blk"), [(16 * i + j, (j % 8) * 16 + 2 * i + j // 8) for i in range(8) for j in range(16)]
    )
    add_chunk(2)
    fetched, stats[2] = lax.optimization_barrier((fetched, stats[2]))
    pick = at_slot.astype(BF)
    hard_rows = dot_f32(pick, fetched, ((1,), (0,)))
    hard_score = jnp.sum(own_source.astype(F32) * hard_rows, axis=1)
    add_chunk(3)

    tops = jnp.stack([stat[0] for stat in stats])
    sums = jnp.stack([stat[1] for stat in stats])
    reach = jnp.maximum(jnp.max(jnp.stack([stat[2] for stat in stats]), axis=0), jnp.max(jnp.abs(hard_rows)))
    own_margin = lax.dynamic_slice_in_dim(margin_row, start, rows, 0)
    own_pos = jnp.sum(own_source.astype(F32) * own_target.astype(F32), axis=1) - own_margin
    pos = lax.dynamic_update_slice_in_dim(jnp.zeros((total,), F32), own_pos, start, 0)
    hard_all = lax.dynamic_update_slice_in_dim(jnp.full((total,), LOW, F32), hard_score, start, 0)
    soft_top = jnp.max(tops, axis=0)
    soft = jnp.sum(sums * jnp.exp(tops - soft_top), axis=0)
    mine = jnp.stack([soft_top, soft, pos, hard_all, reach] + [jnp.zeros((total,), F32)] * 3)
    everyone = lax.all_to_all(jnp.broadcast_to(mine[None], (8, 8, total)), "grp", 0, 0, tiled=True)
    source_part = source_call(jnp.concatenate([jnp.exp(tops - soft_top), jnp.zeros((4, total), F32)]), so_far[0],
        [have[key] for chunk in order for key in chunk])
    everyone, source_part = lax.optimization_barrier((everyone, source_part))
    source_parts = lax.all_to_all(source_part.reshape(8, rows, width), "grp", 0, 0, tiled=True)
    token = hop_blk(source_part[:16, :128], 0, 0, 1)
    pos = jnp.sum(everyone[:, 2], axis=0)
    hard_all = jnp.max(everyone[:, 3], axis=0)
    reach = jnp.max(everyone[:, 4], axis=0)
    top = jnp.maximum(jnp.max(everyone[:, 0], axis=0), jnp.maximum(pos, hard_all))
    off = jnp.sum(everyone[:, 1] * jnp.exp(everyone[:, 0] - top), axis=0) + jnp.exp(hard_all - top)
    log_total = top + jnp.log(off + jnp.exp(pos - top))
    row_loss = log_total - pos
    less = jnp.exp(pos - log_total) - 1.0
    diag_weight = jnp.where(holds, less, 0.0)

    x_at, y_at = grp // 2, grp % 2
    mass = jnp.abs(less) + off * jnp.exp(top - log_total)
    bound = jnp.maximum(1.01 * reach * mass, 1e-30)
    col = jnp.concatenate(
        [jnp.stack([jnp.exp(hard_all - log_total), less, 32767.0 / bound]), jnp.exp(everyone[:, 0] - log_total[None])]
    )
    col = lax.dynamic_slice_in_dim(col, start, rows, 1)
    hard_prob = col[0]
    col = jnp.transpose(col)
    half = rows // 2

    weights = jnp.concatenate([jnp.exp(tops - log_total), diag_weight[None], jnp.zeros((3, total), F32)])
    keep, give = target_call(flat, weights, so_far[0], source_emb, token)
    got = hop_blk(give, 0, 0, 1)
    where_at = {pair: (n, j) for n, chunk in enumerate(CHUNKS) for j, pair in enumerate(chunk)}

    def both(dz, dy):
        n, j = where_at[dz, dy]
        here = slice(j * rows, (j + 1) * rows)
        return (keep[n, here] + got[n, here].astype(F32)).astype(BF)

    leave = [jnp.concatenate([both(dz, 0), both(dz, 1)]) for dz in (1, 3, 2)]
    moved = [hop_blk(part, dz, 0, 0) for part, dz in zip(leave, (1, 3, 2))]
    whole = [pl.BlockSpec((1, 2 * rows, width), lambda i: (0, 0, 0))] * 2
    whole += [pl.BlockSpec((2 * rows, width), lambda i: (0, 0))] * 3
    mine, other = pl.pallas_call(
        line_kernel,
        out_shape=(jax.ShapeDtypeStruct((rows, width), F32), jax.ShapeDtypeStruct((rows, width), BF)),
        grid=(1,),
        in_specs=whole,
        out_specs=[pl.BlockSpec((rows, width), lambda i: (0, 0))] * 2,
        cost_estimate=pl.CostEstimate(flops=10 * rows * width, bytes_accessed=30 * rows * width, transcendentals=0),
        name="lines",
    )(keep, got, *moved)

    coded, coded_high = pl.pallas_call(
        code_kernel,
        out_shape=(jax.ShapeDtypeStruct((rows, width), jnp.int16), jax.ShapeDtypeStruct((half, width), jnp.int16)),
        grid=(2,),
        in_specs=[
            pl.BlockSpec((8, half, width), lambda i: (0, i, 0)),
            pl.BlockSpec((half, width), lambda i: (i, 0)),
            pl.BlockSpec((half, width), lambda i: (i, 0)),
            pl.BlockSpec((half, col.shape[1]), lambda i: (i, 0)),
        ]
        + [pl.BlockSpec(memory_space=pl.ANY)] * 3,
        out_specs=(pl.BlockSpec((half, width), lambda i: (i, 0)), pl.BlockSpec((half, width), lambda i: (0, 0))),
        cost_estimate=pl.CostEstimate(flops=10 * rows * width, bytes_accessed=22 * rows * width, transcendentals=0),
        name="code",
    )(source_parts, hard_rows, own_target, col, *leave)
    side = hop_grp(coded, 0, 1)
    far = [hop_grp(coded_high, -dx, 0) for dx in (1, 2, 3)]
    contribution = (hard_prob[:, None] * own_source.astype(F32)).astype(BF)
    outgoing = dot_f32(pick, contribution, ((0,), (0,))).astype(BF).reshape(owners, cap, width)
    other, side, far, outgoing = lax.optimization_barrier((other, side, far, outgoing))
    target_grad = mine + hop_blk(other, 0, 1, 0).astype(F32)
    low = jnp.stack([coded[:half], side[:half]])
    pairs = [hop_grp(low, -dx, 0) for dx in (1, 2, 3)]
    far_side = hop_grp(jnp.stack(far), 0, 1)
    blocks = jnp.stack([((x_at + dx) % 4) * 2 + (y_at ^ dy) for dx in range(4) for dy in range(2)])
    source_grad = decode_call(
        blocks, (bound * (1.0 / 32767.0))[:, None], [coded, side, *far, *pairs, far_side]
    )

    incoming = lax.all_to_all(outgoing, ("grp", "blk"), 0, 0, tiled=True).reshape(slots, width)
    pool_grad = dot_f32(serve, incoming, ((0,), (0,)))
    return (row_loss, source_grad, target_grad, pool_grad)


def solution(mesh):
    in_specs = (P("blk", None), P(("grp", "blk"), None), P(("grp", "blk"), None), P("blk"), P("blk"), P())
    out_specs = (P("blk"), P("blk", None), P(("grp", "blk"), None), P(("grp", "blk"), None))
    return jax.shard_map(shards, mesh=mesh, in_specs=in_specs, out_specs=out_specs, check_vma=False)
```

```python
import jax
import jax.numpy as jnp
from jax import lax
from jax.experimental import pallas as pl
from jax.experimental.pallas import tpu as pltpu
from jax.sharding import PartitionSpec as P

BF, F32 = jnp.bfloat16, jnp.float32
NEG = -1e30
LOW = -3e38
TILE = 768
PART = 384
CHUNKS = (((0, 0), (0, 1)), ((1, 0), (3, 0)), ((2, 0), (1, 1)), ((3, 1), (2, 1)))


def hop_blk(value, dz, dy, dc):
    route = []
    for i in range(16):
        z, y, c = i // 4, (i // 2) % 2, i % 2
        route.append((i, ((z + dz) % 4) * 4 + (y ^ dy) * 2 + (c ^ dc)))
    return lax.ppermute(value, "blk", route)


def hop_grp(value, dx, dy):
    return lax.ppermute(value, "grp", [(i, ((i // 2 + dx) % 4) * 2 + ((i % 2) ^ dy)) for i in range(8)])


def dot_f32(a, b, dims):
    return lax.dot_general(a, b, (dims, ((), ())), preferred_element_type=F32)


def columns_of(rows):
    pad = jnp.zeros((120, rows.shape[1]), F32)
    return jnp.transpose(jnp.concatenate([rows, pad], axis=0))


def score_kernel(place, src, t0, t1, t2, t3, *refs):
    e_out, stat_out, tgt_ref, a_ref = refs[-4:]
    rows = t0.shape[0]
    half = 2 * rows
    step = pl.program_id(0)
    count = e_out.shape[1]

    @pl.when(step == 0)
    def _():
        top = jnp.zeros((1, 1), F32)
        for q, t in enumerate((t0, t1, t2, t3)):
            block = t[...]
            tgt_ref[q * rows : (q + 1) * rows, :] = block
            top = jnp.maximum(top, jnp.max(jnp.abs(block).astype(F32), keepdims=True))
        a_ref[...] = jnp.broadcast_to(top, a_ref.shape)

    tgt = tgt_ref[...]
    lane = lax.broadcasted_iota(jnp.int32, (PART, 128), 1)
    column = lax.broadcasted_iota(jnp.int32, (PART, 2 * half), 1)
    line = lax.broadcasted_iota(jnp.int32, (PART, 1), 0)
    parts = []
    for first in range(0, count, PART):
        ats = []
        for sub in range(2):
            k = step * (count // rows) + first // rows + sub
            at = jnp.int32(-(1 << 20))
            for q in range(4):
                at = jnp.where(place[q] == k, (q - sub) * rows, at)
            ats.append(at)
        hole = line + jnp.where(line < rows, ats[0], ats[1])
        here = pl.ds(first, PART)
        s = dot_f32(src[pl.ds(pl.multiple_of(step * count + first, PART), PART), :], tgt, ((1,), (1,)))
        s = jnp.where(column == hole, NEG, s)
        top = jnp.max(s, axis=1, keepdims=True)
        e = jnp.exp(s - top)
        total = jnp.sum(e, axis=1, keepdims=True)
        e_out[0, here, :] = e.astype(BF)
        parts.append(jnp.where(lane == 0, top, jnp.where(lane == 1, total, a_ref[0:1, :])))
    stat_out[...] = jnp.transpose(jnp.concatenate(parts, axis=0))[0:8, :]


def score_call(place, src, blocks, n, so_far):
    rows, width = blocks[0].shape
    total = src.shape[0]
    cols = 4 * rows
    so_far = list(so_far)
    return pl.pallas_call(
        score_kernel,
        out_shape=(
            pltpu.HBM((4, total, cols), BF),
            jax.ShapeDtypeStruct((8, total), F32),
        ),
        grid_spec=pltpu.PrefetchScalarGridSpec(
            num_scalar_prefetch=1,
            grid=(total // TILE,),
            in_specs=[pl.BlockSpec(memory_space=pltpu.VMEM)] * 5
            + [pl.BlockSpec(memory_space=pl.ANY)] * len(so_far),
            out_specs=(
                pl.BlockSpec((1, TILE, cols), lambda i, p: (n, i, 0)),
                pl.BlockSpec((8, TILE), lambda i, p: (0, i)),
            ),
            scratch_shapes=[pltpu.VMEM((cols, width), BF), pltpu.VMEM((8, 128), F32)],
        ),
        input_output_aliases={6: 0} if so_far else {},
        compiler_params=pltpu.CompilerParams(vmem_limit_bytes=24 << 20),
        cost_estimate=pl.CostEstimate(
            flops=2 * total * cols * width, bytes_accessed=total * (width + cols) * 2, transcendentals=total * cols
        ),
        name="scores",
    )(place, src, *blocks, *so_far)


def source_kernel(w_ref, e_ref, *refs):
    blocks, out, tgt = refs[:-2], refs[-2], refs[-1]
    rows = blocks[0].shape[0]

    @pl.when(pl.program_id(0) == 0)
    def _():
        for n, block in enumerate(blocks):
            tgt[n // 4, n % 4 * rows : (n % 4 + 1) * rows, :] = block[...]

    weights = columns_of(w_ref[...])
    total = None
    for c in range(4):
        part = dot_f32(e_ref[c], tgt[c], ((1,), (0,))) * weights[:, c : c + 1]
        total = part if total is None else total + part
    out[...] = total.astype(BF)


def source_call(weights, e_all, blocks):
    _, total, cols = e_all.shape
    rows, width = blocks[0].shape
    whole = pl.BlockSpec((rows, width), lambda i: (0, 0), pipeline_mode=pl.Buffered(1))
    return pl.pallas_call(
        source_kernel,
        out_shape=jax.ShapeDtypeStruct((total, width), BF),
        grid=(total // PART,),
        in_specs=[
            pl.BlockSpec((8, PART), lambda i: (0, i)),
            pl.BlockSpec((4, PART, cols), lambda i: (0, i, 0)),
        ]
        + [whole] * len(blocks),
        out_specs=pl.BlockSpec((PART, width), lambda i: (i, 0)),
        scratch_shapes=[pltpu.VMEM((4, cols, width), BF)],
        cost_estimate=pl.CostEstimate(
            flops=8 * total * cols * width, bytes_accessed=total * (8 * cols + 2 * width), transcendentals=0
        ),
        name="source_terms",
    )(weights, e_all, *blocks)


def target_kernel(place, w_ref, e_ref, src_ref, _, keep, give, acc, scaled, column):
    rows = acc.shape[0] // 4
    total = src_ref.shape[0]
    chunk = pl.program_id(0)

    @pl.when(chunk == 0)
    def _():
        for first in range(0, total, PART):
            here = slice(first, first + PART)
            column[here, :] = columns_of(w_ref[:, here])

    lane = lax.broadcasted_iota(jnp.int32, (PART, 128), 1)
    for first in range(0, total, PART):
        here = slice(first, first + PART)
        weight = jnp.sum(jnp.where(lane == chunk, column[here, :], 0.0), axis=1, keepdims=True)
        scaled[here, :] = (src_ref[here, :].astype(F32) * weight).astype(BF)
    acc[...] = dot_f32(e_ref[0], scaled[...], ((0,), (0,)))
    for q in range(4):
        at = place[chunk * 4 + q]

        @pl.when(at >= 0)
        def _():
            there = slice(q * rows, (q + 1) * rows)
            here = pl.ds(pl.multiple_of(at * rows, rows), rows)
            acc[there, :] = acc[there, :] + column[here, 4:5] * src_ref[here, :].astype(F32)

    keep[0] = acc[0 : 2 * rows, :]
    give[0] = acc[2 * rows : 4 * rows, :].astype(BF)


def target_call(place, weights, e_all, src, after):
    _, total, cols = e_all.shape
    width = src.shape[1]
    half = (4, cols // 2, width)
    half_spec = pl.BlockSpec((1, cols // 2, width), lambda i, p: (i, 0, 0))
    return pl.pallas_call(
        target_kernel,
        out_shape=(jax.ShapeDtypeStruct(half, F32), jax.ShapeDtypeStruct(half, BF)),
        grid_spec=pltpu.PrefetchScalarGridSpec(
            num_scalar_prefetch=1,
            grid=(4,),
            in_specs=[
                pl.BlockSpec((8, total), lambda i, p: (0, 0)),
                pl.BlockSpec((1, total, cols), lambda i, p: (i, 0, 0)),
                pl.BlockSpec((total, width), lambda i, p: (0, 0)),
                pl.BlockSpec(memory_space=pl.ANY),
            ],
            out_specs=(half_spec, half_spec),
            scratch_shapes=[
                pltpu.VMEM((cols, width), F32),
                pltpu.VMEM((total, width), BF),
                pltpu.VMEM((total, 128), F32),
            ],
        ),
        cost_estimate=pl.CostEstimate(
            flops=8 * total * cols * width, bytes_accessed=total * (width + 4 * cols) * 2 + cols * width * 12, transcendentals=0
        ),
        name="target_terms",
    )(place, weights, e_all, src, after)


def code_kernel(parts, hard, tgt, col, _a, _b, _c, out, high):
    total = hard[...] * col[:, 0:1] + tgt[...].astype(F32) * col[:, 1:2]
    for g in range(parts.shape[0]):
        total = total + parts[g].astype(F32) * col[:, 3 + g : 4 + g]
    scaled = jnp.clip(total * col[:, 2:3], -32767.0, 32767.0)
    coded = jnp.round(scaled).astype(jnp.int32).astype(jnp.int16)
    out[...] = coded
    high[...] = coded


def line_kernel(keep, got, m1, m2, m3, mine, other):
    rows = mine.shape[0]
    total = keep[0] + got[0].astype(F32)
    for part in (m1, m2, m3):
        total = total + part[...].astype(F32)
    mine[...] = total[:rows, :]
    other[...] = total[rows:, :].astype(BF)


def decode_kernel(order, scale, own, side, far1, far2, far3, pairs1, pairs2, pairs3, far_side, out):
    step = pl.program_id(0)
    half = own.shape[0] // 2
    far, pairs = (None, far1, far2, far3), (None, pairs1, pairs2, pairs3)
    for dx in range(4):
        for dy in range(2):

            @pl.when(step == dx * 2 + dy)
            def _():
                if dx == 0:
                    whole = (own if dy == 0 else side)[...]
                    out[...] = whole.astype(jnp.int32).astype(F32) * scale[...]
                else:
                    low = pairs[dx][dy]
                    high = far[dx][...] if dy == 0 else far_side[dx - 1]
                    out[0:half, :] = low.astype(jnp.int32).astype(F32) * scale[0:half, :]
                    out[half:, :] = high.astype(jnp.int32).astype(F32) * scale[half:, :]


def decode_call(order, scale, pieces):
    rows, width = pieces[0].shape
    total = scale.shape[0]
    return pl.pallas_call(
        decode_kernel,
        out_shape=jax.ShapeDtypeStruct((total, width), F32),
        grid_spec=pltpu.PrefetchScalarGridSpec(
            num_scalar_prefetch=1,
            grid=(total // rows,),
            in_specs=[pl.BlockSpec((rows, 1), lambda i, p: (p[i], 0))]
            + [pl.BlockSpec(x.shape, lambda i, p, n=x.ndim: (0,) * n) for x in pieces],
            out_specs=pl.BlockSpec((rows, width), lambda i, p: (p[i], 0)),
        ),
        compiler_params=pltpu.CompilerParams(vmem_limit_bytes=24 << 20),
        cost_estimate=pl.CostEstimate(flops=total * width, bytes_accessed=total * width * 6, transcendentals=0),
        name="decode",
    )(order, scale, *pieces)


def shards(source_emb, target_emb, hard_pool, hard_index, language, margin):
    total, width = source_emb.shape
    rows = target_emb.shape[0]
    blk, grp = lax.axis_index("blk"), lax.axis_index("grp")
    owners = 128
    cap = max(2, (2 * rows + owners - 1) // owners)
    slots = owners * cap
    z, y, c = blk // 4, (blk // 2) % 2, blk % 2

    start = grp * rows
    own_index = lax.dynamic_slice_in_dim(hard_index, start, rows, 0)
    own_source = lax.dynamic_slice_in_dim(source_emb, start, rows, 0)
    owner, pool_row = own_index // rows, own_index % rows
    position = jnp.arange(rows, dtype=jnp.int32)
    same = (owner[:, None] == owner[None, :]) & (position[None, :] < position[:, None])
    slot = owner * cap + jnp.sum(same.astype(jnp.int32), axis=1)
    at_slot = slot[:, None] == jnp.arange(slots, dtype=jnp.int32)[None, :]
    requests = jnp.sum(jnp.where(at_slot, pool_row[:, None] + 1, 0), axis=0) - 1
    wanted = lax.all_to_all(requests.reshape(owners, cap), ("grp", "blk"), 0, 0, tiled=True)
    lang_match = language[:, None] == jnp.arange(margin.shape[0], dtype=jnp.int32)[None, :]
    margin_row = jnp.sum(jnp.where(lang_match, margin[None, :], 0.0), axis=1)

    have = {(0, 0, 0): target_emb}
    have[0, 1, 0] = hop_blk(target_emb, 0, 1, 0)
    for dz in (1, 3, 2):
        have[dz, 0, 0] = hop_blk(target_emb, -dz, 0, 0)
    for dz in (1, 3, 2):
        have[dz, 1, 0] = hop_blk(have[0, 1, 0], -dz, 0, 0)
    for dz, dy in [pair for chunk in CHUNKS for pair in chunk]:
        have[dz, dy, 1] = hop_blk(have[dz, dy, 0], 0, 0, 1)

    holds = grp == blk // 2
    place = {}
    for dz in range(4):
        for dy in range(2):
            for dc in range(2):
                zz = (z + dz) % 4
                k = (zz % 2) * 4 + (y ^ dy) * 2 + (c ^ dc)
                place[dz, dy, dc] = jnp.where(holds & (zz // 2 == c), k, -1)
    order = [[(dz, dy, dc) for dc in (0, 1) for dz, dy in chunk] for chunk in CHUNKS]
    places = [jnp.stack([place[key] for key in chunk]) for chunk in order]
    flat = jnp.concatenate(places)

    stats, so_far = [], ()

    def add_chunk(n):
        nonlocal so_far
        e, stat = score_call(places[n], source_emb, [have[key] for key in order[n]], n, so_far)
        so_far = (e,)
        stats.append(stat)

    add_chunk(0)
    wanted, stats[0] = lax.optimization_barrier((wanted, stats[0]))
    serve = (wanted.reshape(slots)[:, None] == position[None, :]).astype(BF)
    served = dot_f32(serve, hard_pool, ((1,), (0,))).astype(BF).reshape(owners, cap, width)
    served, places[1] = lax.optimization_barrier((served, places[1]))
    fetched = lax.all_to_all(served, ("grp", "blk"), 0, 0, tiled=True).reshape(slots, width)
    add_chunk(1)
    early_target, stats[1] = lax.optimization_barrier((target_emb, stats[1]))
    own_target = lax.ppermute(
        early_target, ("grp", "blk"), [(16 * i + j, (j % 8) * 16 + 2 * i + j // 8) for i in range(8) for j in range(16)]
    )
    add_chunk(2)
    fetched, stats[2] = lax.optimization_barrier((fetched, stats[2]))
    pick = at_slot.astype(BF)
    hard_rows = dot_f32(pick, fetched, ((1,), (0,)))
    hard_score = jnp.sum(own_source.astype(F32) * hard_rows, axis=1)
    add_chunk(3)

    tops = jnp.stack([stat[0] for stat in stats])
    sums = jnp.stack([stat[1] for stat in stats])
    reach = jnp.maximum(jnp.max(jnp.stack([stat[2] for stat in stats]), axis=0), jnp.max(jnp.abs(hard_rows)))
    own_margin = lax.dynamic_slice_in_dim(margin_row, start, rows, 0)
    own_pos = jnp.sum(own_source.astype(F32) * own_target.astype(F32), axis=1) - own_margin
    pos = lax.dynamic_update_slice_in_dim(jnp.zeros((total,), F32), own_pos, start, 0)
    hard_all = lax.dynamic_update_slice_in_dim(jnp.full((total,), LOW, F32), hard_score, start, 0)
    soft_top = jnp.max(tops, axis=0)
    soft = jnp.sum(sums * jnp.exp(tops - soft_top), axis=0)
    mine = jnp.stack([soft_top, soft, pos, hard_all, reach] + [jnp.zeros((total,), F32)] * 3)
    everyone = lax.all_to_all(jnp.broadcast_to(mine[None], (8, 8, total)), "grp", 0, 0, tiled=True)
    source_part = source_call(jnp.concatenate([jnp.exp(tops - soft_top), jnp.zeros((4, total), F32)]), so_far[0],
        [have[key] for chunk in order for key in chunk])
    everyone, source_part = lax.optimization_barrier((everyone, source_part))
    source_parts = lax.all_to_all(source_part.reshape(8, rows, width), "grp", 0, 0, tiled=True)
    token = hop_blk(source_part[:16, :128], 0, 0, 1)
    pos = jnp.sum(everyone[:, 2], axis=0)
    hard_all = jnp.max(everyone[:, 3], axis=0)
    reach = jnp.max(everyone[:, 4], axis=0)
    top = jnp.maximum(jnp.max(everyone[:, 0], axis=0), jnp.maximum(pos, hard_all))
    off = jnp.sum(everyone[:, 1] * jnp.exp(everyone[:, 0] - top), axis=0) + jnp.exp(hard_all - top)
    log_total = top + jnp.log(off + jnp.exp(pos - top))
    row_loss = log_total - pos
    less = jnp.exp(pos - log_total) - 1.0
    diag_weight = jnp.where(holds, less, 0.0)

    x_at, y_at = grp // 2, grp % 2
    mass = jnp.abs(less) + off * jnp.exp(top - log_total)
    bound = jnp.maximum(1.01 * reach * mass, 1e-30)
    col = jnp.concatenate(
        [jnp.stack([jnp.exp(hard_all - log_total), less, 32767.0 / bound]), jnp.exp(everyone[:, 0] - log_total[None])]
    )
    col = lax.dynamic_slice_in_dim(col, start, rows, 1)
    hard_prob = col[0]
    col = jnp.transpose(col)
    half = rows // 2

    weights = jnp.concatenate([jnp.exp(tops - log_total), diag_weight[None], jnp.zeros((3, total), F32)])
    keep, give = target_call(flat, weights, so_far[0], source_emb, token)
    got = hop_blk(give, 0, 0, 1)
    where_at = {pair: (n, j) for n, chunk in enumerate(CHUNKS) for j, pair in enumerate(chunk)}

    def both(dz, dy):
        n, j = where_at[dz, dy]
        here = slice(j * rows, (j + 1) * rows)
        return (keep[n, here] + got[n, here].astype(F32)).astype(BF)

    leave = [jnp.concatenate([both(dz, 0), both(dz, 1)]) for dz in (1, 3, 2)]
    moved = [hop_blk(part, dz, 0, 0) for part, dz in zip(leave, (1, 3, 2))]
    whole = [pl.BlockSpec((1, 2 * rows, width), lambda i: (0, 0, 0))] * 2
    whole += [pl.BlockSpec((2 * rows, width), lambda i: (0, 0))] * 3
    mine, other = pl.pallas_call(
        line_kernel,
        out_shape=(jax.ShapeDtypeStruct((rows, width), F32), jax.ShapeDtypeStruct((rows, width), BF)),
        grid=(1,),
        in_specs=whole,
        out_specs=[pl.BlockSpec((rows, width), lambda i: (0, 0))] * 2,
        cost_estimate=pl.CostEstimate(flops=10 * rows * width, bytes_accessed=30 * rows * width, transcendentals=0),
        name="lines",
    )(keep, got, *moved)

    coded, coded_high = pl.pallas_call(
        code_kernel,
        out_shape=(jax.ShapeDtypeStruct((rows, width), jnp.int16), jax.ShapeDtypeStruct((half, width), jnp.int16)),
        grid=(2,),
        in_specs=[
            pl.BlockSpec((8, half, width), lambda i: (0, i, 0)),
            pl.BlockSpec((half, width), lambda i: (i, 0)),
            pl.BlockSpec((half, width), lambda i: (i, 0)),
            pl.BlockSpec((half, col.shape[1]), lambda i: (i, 0)),
        ]
        + [pl.BlockSpec(memory_space=pl.ANY)] * 3,
        out_specs=(pl.BlockSpec((half, width), lambda i: (i, 0)), pl.BlockSpec((half, width), lambda i: (0, 0))),
        cost_estimate=pl.CostEstimate(flops=10 * rows * width, bytes_accessed=22 * rows * width, transcendentals=0),
        name="code",
    )(source_parts, hard_rows, own_target, col, *leave)
    side = hop_grp(coded, 0, 1)
    far = [hop_grp(coded_high, -dx, 0) for dx in (1, 2, 3)]
    contribution = (hard_prob[:, None] * own_source.astype(F32)).astype(BF)
    outgoing = dot_f32(pick, contribution, ((0,), (0,))).astype(BF).reshape(owners, cap, width)
    line_far = hop_blk(other, 0, 1, 0)
    mine, side, far, outgoing = lax.optimization_barrier((mine, side, far, outgoing))
    low = jnp.stack([coded[:half], side[:half]])
    pairs = [hop_grp(low, -dx, 0) for dx in (1, 2, 3)]
    far_side = hop_grp(jnp.stack(far), 0, 1)
    blocks = jnp.stack([((x_at + dx) % 4) * 2 + (y_at ^ dy) for dx in range(4) for dy in range(2)])
    source_grad = decode_call(
        blocks, (bound * (1.0 / 32767.0))[:, None], [coded, side, *far, *pairs, far_side]
    )

    line_far, source_grad = lax.optimization_barrier((line_far, source_grad))
    target_grad = mine + line_far.astype(F32)

    incoming = lax.all_to_all(outgoing, ("grp", "blk"), 0, 0, tiled=True).reshape(slots, width)
    pool_grad = dot_f32(serve, incoming, ((0,), (0,)))
    return (row_loss, source_grad, target_grad, pool_grad)


def solution(mesh):
    in_specs = (P("blk", None), P(("grp", "blk"), None), P(("grp", "blk"), None), P("blk"), P("blk"), P())
    out_specs = (P("blk"), P("blk", None), P(("grp", "blk"), None), P(("grp", "blk"), None))
    return jax.shard_map(shards, mesh=mesh, in_specs=in_specs, out_specs=out_specs, check_vma=False)
```

```python
import jax
import jax.numpy as jnp
from jax import lax
from jax.experimental import pallas as pl
from jax.experimental.pallas import tpu as pltpu
from jax.sharding import PartitionSpec as P

BF, F32 = jnp.bfloat16, jnp.float32
NEG = -1e30
LOW = -3e38
TILE = 768
PART = 384
CHUNKS = (((0, 0), (0, 1)), ((1, 0), (3, 0)), ((2, 0), (1, 1)), ((3, 1), (2, 1)))


def hop_blk(value, dz, dy, dc):
    route = []
    for i in range(16):
        z, y, c = i // 4, (i // 2) % 2, i % 2
        route.append((i, ((z + dz) % 4) * 4 + (y ^ dy) * 2 + (c ^ dc)))
    return lax.ppermute(value, "blk", route)


def hop_grp(value, dx, dy):
    return lax.ppermute(value, "grp", [(i, ((i // 2 + dx) % 4) * 2 + ((i % 2) ^ dy)) for i in range(8)])


def dot_f32(a, b, dims):
    return lax.dot_general(a, b, (dims, ((), ())), preferred_element_type=F32)


def columns_of(rows):
    pad = jnp.zeros((120, rows.shape[1]), F32)
    return jnp.transpose(jnp.concatenate([rows, pad], axis=0))


def score_kernel(place, src, t0, t1, t2, t3, *refs):
    e_out, stat_out, tgt_ref, a_ref = refs[-4:]
    rows = t0.shape[0]
    half = 2 * rows
    step = pl.program_id(0)

    @pl.when(step == 0)
    def _():
        top = jnp.zeros((1, 1), F32)
        for q, t in enumerate((t0, t1, t2, t3)):
            block = t[...]
            tgt_ref[q * rows : (q + 1) * rows, :] = block
            top = jnp.maximum(top, jnp.max(jnp.abs(block).astype(F32), keepdims=True))
        a_ref[...] = jnp.broadcast_to(top, a_ref.shape)

    tgt = tgt_ref[...]
    lane = lax.broadcasted_iota(jnp.int32, (PART, 128), 1)
    column = lax.broadcasted_iota(jnp.int32, (PART, 2 * half), 1)
    line = lax.broadcasted_iota(jnp.int32, (PART, 1), 0)
    parts = []
    for first in range(0, src.shape[0], PART):
        ats = []
        for sub in range(2):
            k = step * (src.shape[0] // rows) + first // rows + sub
            at = jnp.int32(-(1 << 20))
            for q in range(4):
                at = jnp.where(place[q] == k, (q - sub) * rows, at)
            ats.append(at)
        hole = line + jnp.where(line < rows, ats[0], ats[1])
        here = pl.ds(first, PART)
        s = dot_f32(src[here, :], tgt, ((1,), (1,)))
        s = jnp.where(column == hole, NEG, s)
        top = jnp.max(s, axis=1, keepdims=True)
        e = jnp.exp(s - top)
        total = jnp.sum(e, axis=1, keepdims=True)
        e_out[0, here, :] = e.astype(BF)
        parts.append(jnp.where(lane == 0, top, jnp.where(lane == 1, total, a_ref[0:1, :])))
    stat_out[...] = jnp.transpose(jnp.concatenate(parts, axis=0))[0:8, :]


def score_call(place, src, blocks, n, so_far):
    rows, width = blocks[0].shape
    total = src.shape[0]
    cols = 4 * rows
    so_far = list(so_far)
    whole = pl.BlockSpec((rows, width), lambda i, p: (0, 0))
    return pl.pallas_call(
        score_kernel,
        out_shape=(
            pltpu.HBM((4, total, cols), BF),
            jax.ShapeDtypeStruct((8, total), F32),
        ),
        grid_spec=pltpu.PrefetchScalarGridSpec(
            num_scalar_prefetch=1,
            grid=(total // TILE,),
            in_specs=[pl.BlockSpec((TILE, width), lambda i, p: (i, 0))]
            + [whole] * 4
            + [pl.BlockSpec(memory_space=pl.ANY)] * len(so_far),
            out_specs=(
                pl.BlockSpec((1, TILE, cols), lambda i, p: (n, i, 0)),
                pl.BlockSpec((8, TILE), lambda i, p: (0, i)),
            ),
            scratch_shapes=[pltpu.VMEM((cols, width), BF), pltpu.VMEM((8, 128), F32)],
        ),
        input_output_aliases={6: 0} if so_far else {},
        compiler_params=pltpu.CompilerParams(vmem_limit_bytes=24 << 20),
        cost_estimate=pl.CostEstimate(
            flops=2 * total * cols * width, bytes_accessed=total * (width + cols) * 2, transcendentals=total * cols
        ),
        name="scores",
    )(place, src, *blocks, *so_far)


def source_kernel(w_ref, e_ref, *refs):
    blocks, out, tgt = refs[:-2], refs[-2], refs[-1]
    rows = blocks[0].shape[0]

    @pl.when(pl.program_id(0) == 0)
    def _():
        for n, block in enumerate(blocks):
            tgt[n // 4, n % 4 * rows : (n % 4 + 1) * rows, :] = block[...]

    weights = columns_of(w_ref[...])
    total = None
    for c in range(4):
        part = dot_f32(e_ref[c], tgt[c], ((1,), (0,))) * weights[:, c : c + 1]
        total = part if total is None else total + part
    out[...] = total.astype(BF)


def source_call(weights, e_all, blocks):
    _, total, cols = e_all.shape
    rows, width = blocks[0].shape
    whole = pl.BlockSpec((rows, width), lambda i: (0, 0), pipeline_mode=pl.Buffered(1))
    return pl.pallas_call(
        source_kernel,
        out_shape=jax.ShapeDtypeStruct((total, width), BF),
        grid=(total // PART,),
        in_specs=[
            pl.BlockSpec((8, PART), lambda i: (0, i)),
            pl.BlockSpec((4, PART, cols), lambda i: (0, i, 0)),
        ]
        + [whole] * len(blocks),
        out_specs=pl.BlockSpec((PART, width), lambda i: (i, 0)),
        scratch_shapes=[pltpu.VMEM((4, cols, width), BF)],
        cost_estimate=pl.CostEstimate(
            flops=8 * total * cols * width, bytes_accessed=total * (8 * cols + 2 * width), transcendentals=0
        ),
        name="source_terms",
    )(weights, e_all, *blocks)


def target_kernel(place, w_ref, e_ref, src_ref, _, keep, give, acc, scaled, column):
    rows = acc.shape[0] // 4
    total = src_ref.shape[0]
    chunk = pl.program_id(0)

    @pl.when(chunk == 0)
    def _():
        for first in range(0, total, PART):
            here = slice(first, first + PART)
            column[here, :] = columns_of(w_ref[:, here])

    lane = lax.broadcasted_iota(jnp.int32, (PART, 128), 1)
    for first in range(0, total, PART):
        here = slice(first, first + PART)
        weight = jnp.sum(jnp.where(lane == chunk, column[here, :], 0.0), axis=1, keepdims=True)
        scaled[here, :] = (src_ref[here, :].astype(F32) * weight).astype(BF)
    acc[...] = dot_f32(e_ref[0], scaled[...], ((0,), (0,)))
    for q in range(4):
        at = place[chunk * 4 + q]

        @pl.when(at >= 0)
        def _():
            there = slice(q * rows, (q + 1) * rows)
            here = pl.ds(pl.multiple_of(at * rows, rows), rows)
            acc[there, :] = acc[there, :] + column[here, 4:5] * src_ref[here, :].astype(F32)

    keep[0] = acc[0 : 2 * rows, :]
    give[0] = acc[2 * rows : 4 * rows, :].astype(BF)


def target_call(place, weights, e_all, src, after):
    _, total, cols = e_all.shape
    width = src.shape[1]
    half = (4, cols // 2, width)
    half_spec = pl.BlockSpec((1, cols // 2, width), lambda i, p: (i, 0, 0))
    return pl.pallas_call(
        target_kernel,
        out_shape=(jax.ShapeDtypeStruct(half, F32), jax.ShapeDtypeStruct(half, BF)),
        grid_spec=pltpu.PrefetchScalarGridSpec(
            num_scalar_prefetch=1,
            grid=(4,),
            in_specs=[
                pl.BlockSpec((8, total), lambda i, p: (0, 0)),
                pl.BlockSpec((1, total, cols), lambda i, p: (i, 0, 0)),
                pl.BlockSpec((total, width), lambda i, p: (0, 0)),
                pl.BlockSpec(memory_space=pl.ANY),
            ],
            out_specs=(half_spec, half_spec),
            scratch_shapes=[
                pltpu.VMEM((cols, width), F32),
                pltpu.VMEM((total, width), BF),
                pltpu.VMEM((total, 128), F32),
            ],
        ),
        cost_estimate=pl.CostEstimate(
            flops=8 * total * cols * width, bytes_accessed=total * (width + 4 * cols) * 2 + cols * width * 12, transcendentals=0
        ),
        name="target_terms",
    )(place, weights, e_all, src, after)


def code_kernel(parts, hard, tgt, col, _, out, high):
    total = hard[...] * col[:, 0:1] + tgt[...].astype(F32) * col[:, 1:2]
    for g in range(parts.shape[0]):
        total = total + parts[g].astype(F32) * col[:, 3 + g : 4 + g]
    scaled = jnp.clip(total * col[:, 2:3], -32767.0, 32767.0)
    coded = jnp.round(scaled).astype(jnp.int32).astype(jnp.int16)
    out[...] = coded
    high[...] = coded


def line_kernel(keep, got, m1, m2, m3, mine, other):
    rows = mine.shape[0]
    total = keep[0] + got[0].astype(F32)
    for part in (m1, m2, m3):
        total = total + part[...].astype(F32)
    mine[...] = total[:rows, :]
    other[...] = total[rows:, :].astype(BF)


def decode_kernel(order, scale, own, side, far1, far2, far3, pairs1, pairs2, pairs3, far_side, out):
    step = pl.program_id(0)
    half = own.shape[0] // 2
    far, pairs = (None, far1, far2, far3), (None, pairs1, pairs2, pairs3)
    for dx in range(4):
        for dy in range(2):

            @pl.when(step == dx * 2 + dy)
            def _():
                if dx == 0:
                    whole = (own if dy == 0 else side)[...]
                    out[...] = whole.astype(jnp.int32).astype(F32) * scale[...]
                else:
                    low = pairs[dx][dy]
                    high = far[dx][...] if dy == 0 else far_side[dx - 1]
                    out[0:half, :] = low.astype(jnp.int32).astype(F32) * scale[0:half, :]
                    out[half:, :] = high.astype(jnp.int32).astype(F32) * scale[half:, :]


def decode_call(order, scale, pieces):
    rows, width = pieces[0].shape
    total = scale.shape[0]
    return pl.pallas_call(
        decode_kernel,
        out_shape=jax.ShapeDtypeStruct((total, width), F32),
        grid_spec=pltpu.PrefetchScalarGridSpec(
            num_scalar_prefetch=1,
            grid=(total // rows,),
            in_specs=[pl.BlockSpec((rows, 1), lambda i, p: (p[i], 0))]
            + [pl.BlockSpec(x.shape, lambda i, p, n=x.ndim: (0,) * n) for x in pieces],
            out_specs=pl.BlockSpec((rows, width), lambda i, p: (p[i], 0)),
        ),
        compiler_params=pltpu.CompilerParams(vmem_limit_bytes=24 << 20),
        cost_estimate=pl.CostEstimate(flops=total * width, bytes_accessed=total * width * 6, transcendentals=0),
        name="decode",
    )(order, scale, *pieces)


def shards(source_emb, target_emb, hard_pool, hard_index, language, margin):
    total, width = source_emb.shape
    rows = target_emb.shape[0]
    blk, grp = lax.axis_index("blk"), lax.axis_index("grp")
    owners = 128
    cap = max(2, (2 * rows + owners - 1) // owners)
    slots = owners * cap
    z, y, c = blk // 4, (blk // 2) % 2, blk % 2

    start = grp * rows
    own_index = lax.dynamic_slice_in_dim(hard_index, start, rows, 0)
    own_source = lax.dynamic_slice_in_dim(source_emb, start, rows, 0)
    owner, pool_row = own_index // rows, own_index % rows
    position = jnp.arange(rows, dtype=jnp.int32)
    same = (owner[:, None] == owner[None, :]) & (position[None, :] < position[:, None])
    slot = owner * cap + jnp.sum(same.astype(jnp.int32), axis=1)
    at_slot = slot[:, None] == jnp.arange(slots, dtype=jnp.int32)[None, :]
    requests = jnp.sum(jnp.where(at_slot, pool_row[:, None] + 1, 0), axis=0) - 1
    wanted = lax.all_to_all(requests.reshape(owners, cap), ("grp", "blk"), 0, 0, tiled=True)
    lang_match = language[:, None] == jnp.arange(margin.shape[0], dtype=jnp.int32)[None, :]
    margin_row = jnp.sum(jnp.where(lang_match, margin[None, :], 0.0), axis=1)

    have = {(0, 0, 0): target_emb}
    have[0, 1, 0] = hop_blk(target_emb, 0, 1, 0)
    for dz in (1, 3, 2):
        have[dz, 0, 0] = hop_blk(target_emb, -dz, 0, 0)
    for dz in (1, 3, 2):
        have[dz, 1, 0] = hop_blk(have[0, 1, 0], -dz, 0, 0)
    for dz, dy in [pair for chunk in CHUNKS for pair in chunk]:
        have[dz, dy, 1] = hop_blk(have[dz, dy, 0], 0, 0, 1)

    holds = grp == blk // 2
    place = {}
    for dz in range(4):
        for dy in range(2):
            for dc in range(2):
                zz = (z + dz) % 4
                k = (zz % 2) * 4 + (y ^ dy) * 2 + (c ^ dc)
                place[dz, dy, dc] = jnp.where(holds & (zz // 2 == c), k, -1)
    order = [[(dz, dy, dc) for dc in (0, 1) for dz, dy in chunk] for chunk in CHUNKS]
    places = [jnp.stack([place[key] for key in chunk]) for chunk in order]
    flat = jnp.concatenate(places)

    stats, so_far = [], ()

    def add_chunk(n):
        nonlocal so_far
        e, stat = score_call(places[n], source_emb, [have[key] for key in order[n]], n, so_far)
        so_far = (e,)
        stats.append(stat)

    add_chunk(0)
    wanted, stats[0] = lax.optimization_barrier((wanted, stats[0]))
    serve = (wanted.reshape(slots)[:, None] == position[None, :]).astype(BF)
    served = dot_f32(serve, hard_pool, ((1,), (0,))).astype(BF).reshape(owners, cap, width)
    served, places[1] = lax.optimization_barrier((served, places[1]))
    fetched = lax.all_to_all(served, ("grp", "blk"), 0, 0, tiled=True).reshape(slots, width)
    add_chunk(1)
    early_target, stats[1] = lax.optimization_barrier((target_emb, stats[1]))
    own_target = lax.ppermute(
        early_target, ("grp", "blk"), [(16 * i + j, (j % 8) * 16 + 2 * i + j // 8) for i in range(8) for j in range(16)]
    )
    add_chunk(2)
    fetched, stats[2] = lax.optimization_barrier((fetched, stats[2]))
    pick = at_slot.astype(BF)
    hard_rows = dot_f32(pick, fetched, ((1,), (0,)))
    hard_score = jnp.sum(own_source.astype(F32) * hard_rows, axis=1)
    add_chunk(3)

    tops = jnp.stack([stat[0] for stat in stats])
    sums = jnp.stack([stat[1] for stat in stats])
    reach = jnp.maximum(jnp.max(jnp.stack([stat[2] for stat in stats]), axis=0), jnp.max(jnp.abs(hard_rows)))
    own_margin = lax.dynamic_slice_in_dim(margin_row, start, rows, 0)
    own_pos = jnp.sum(own_source.astype(F32) * own_target.astype(F32), axis=1) - own_margin
    pos = lax.dynamic_update_slice_in_dim(jnp.zeros((total,), F32), own_pos, start, 0)
    hard_all = lax.dynamic_update_slice_in_dim(jnp.full((total,), LOW, F32), hard_score, start, 0)
    soft_top = jnp.max(tops, axis=0)
    soft = jnp.sum(sums * jnp.exp(tops - soft_top), axis=0)
    mine = jnp.stack([soft_top, soft, pos, hard_all, reach] + [jnp.zeros((total,), F32)] * 3)
    everyone = lax.all_to_all(jnp.broadcast_to(mine[None], (8, 8, total)), "grp", 0, 0, tiled=True)
    source_part = source_call(jnp.concatenate([jnp.exp(tops - soft_top), jnp.zeros((4, total), F32)]), so_far[0],
        [have[key] for chunk in order for key in chunk])
    everyone, source_part = lax.optimization_barrier((everyone, source_part))
    source_parts = lax.all_to_all(source_part.reshape(8, rows, width), "grp", 0, 0, tiled=True)
    token = hop_blk(source_part[:16, :128], 0, 0, 1)
    pos = jnp.sum(everyone[:, 2], axis=0)
    hard_all = jnp.max(everyone[:, 3], axis=0)
    reach = jnp.max(everyone[:, 4], axis=0)
    top = jnp.maximum(jnp.max(everyone[:, 0], axis=0), jnp.maximum(pos, hard_all))
    off = jnp.sum(everyone[:, 1] * jnp.exp(everyone[:, 0] - top), axis=0) + jnp.exp(hard_all - top)
    log_total = top + jnp.log(off + jnp.exp(pos - top))
    row_loss = log_total - pos
    less = jnp.exp(pos - log_total) - 1.0
    diag_weight = jnp.where(holds, less, 0.0)

    x_at, y_at = grp // 2, grp % 2
    mass = jnp.abs(less) + off * jnp.exp(top - log_total)
    bound = jnp.maximum(1.01 * reach * mass, 1e-30)
    col = jnp.concatenate(
        [jnp.stack([jnp.exp(hard_all - log_total), less, 32767.0 / bound]), jnp.exp(everyone[:, 0] - log_total[None])]
    )
    col = lax.dynamic_slice_in_dim(col, start, rows, 1)
    hard_prob = col[0]
    col = jnp.transpose(col)
    half = rows // 2

    weights = jnp.concatenate([jnp.exp(tops - log_total), diag_weight[None], jnp.zeros((3, total), F32)])
    keep, give = target_call(flat, weights, so_far[0], source_emb, token)
    got = hop_blk(give, 0, 0, 1)
    where_at = {pair: (n, j) for n, chunk in enumerate(CHUNKS) for j, pair in enumerate(chunk)}

    def both(dz, dy):
        n, j = where_at[dz, dy]
        here = slice(j * rows, (j + 1) * rows)
        return (keep[n, here] + got[n, here].astype(F32)).astype(BF)

    moved = [hop_blk(jnp.concatenate([both(dz, 0), both(dz, 1)]), dz, 0, 0) for dz in (1, 3, 2)]
    whole = [pl.BlockSpec((1, 2 * rows, width), lambda i: (0, 0, 0))] * 2
    whole += [pl.BlockSpec((2 * rows, width), lambda i: (0, 0))] * 3
    mine, other = pl.pallas_call(
        line_kernel,
        out_shape=(jax.ShapeDtypeStruct((rows, width), F32), jax.ShapeDtypeStruct((rows, width), BF)),
        grid=(1,),
        in_specs=whole,
        out_specs=[pl.BlockSpec((rows, width), lambda i: (0, 0))] * 2,
        cost_estimate=pl.CostEstimate(flops=10 * rows * width, bytes_accessed=30 * rows * width, transcendentals=0),
        name="lines",
    )(keep, got, *moved)
    target_grad = mine + hop_blk(other, 0, 1, 0).astype(F32)

    coded, coded_high = pl.pallas_call(
        code_kernel,
        out_shape=(jax.ShapeDtypeStruct((rows, width), jnp.int16), jax.ShapeDtypeStruct((half, width), jnp.int16)),
        grid=(2,),
        in_specs=[
            pl.BlockSpec((8, half, width), lambda i: (0, i, 0)),
            pl.BlockSpec((half, width), lambda i: (i, 0)),
            pl.BlockSpec((half, width), lambda i: (i, 0)),
            pl.BlockSpec((half, col.shape[1]), lambda i: (i, 0)),
            pl.BlockSpec(memory_space=pl.ANY),
        ],
        out_specs=(pl.BlockSpec((half, width), lambda i: (i, 0)), pl.BlockSpec((half, width), lambda i: (0, 0))),
        cost_estimate=pl.CostEstimate(flops=10 * rows * width, bytes_accessed=22 * rows * width, transcendentals=0),
        name="code",
    )(source_parts, hard_rows, own_target, col, other)
    contribution = (hard_prob[:, None] * own_source.astype(F32)).astype(BF)
    outgoing = dot_f32(pick, contribution, ((0,), (0,))).astype(BF).reshape(owners, cap, width)
    outgoing, coded, coded_high = lax.optimization_barrier((outgoing, coded, coded_high))
    side = hop_grp(coded, 0, 1)
    far = [hop_grp(coded_high, -dx, 0) for dx in (1, 2, 3)]
    low = jnp.stack([coded[:half], side[:half]])
    pairs = [hop_grp(low, -dx, 0) for dx in (1, 2, 3)]
    far_side = hop_grp(jnp.stack(far), 0, 1)
    blocks = jnp.stack([((x_at + dx) % 4) * 2 + (y_at ^ dy) for dx in range(4) for dy in range(2)])
    source_grad = decode_call(
        blocks, (bound * (1.0 / 32767.0))[:, None], [coded, side, *far, *pairs, far_side]
    )

    incoming = lax.all_to_all(outgoing, ("grp", "blk"), 0, 0, tiled=True).reshape(slots, width)
    pool_grad = dot_f32(serve, incoming, ((0,), (0,)))
    return (row_loss, source_grad, target_grad, pool_grad)


def solution(mesh):
    in_specs = (P("blk", None), P(("grp", "blk"), None), P(("grp", "blk"), None), P("blk"), P("blk"), P())
    out_specs = (P("blk"), P("blk", None), P(("grp", "blk"), None), P(("grp", "blk"), None))
    return jax.shard_map(shards, mesh=mesh, in_specs=in_specs, out_specs=out_specs, check_vma=False)
```

```python
import jax
import jax.numpy as jnp
from jax import lax
from jax.experimental import pallas as pl
from jax.experimental.pallas import tpu as pltpu
from jax.sharding import PartitionSpec as P

BF, F32 = jnp.bfloat16, jnp.float32
NEG = -1e30
LOW = -3e38
TILE = 768
PART = 384
CHUNKS = (((0, 0), (0, 1)), ((1, 0), (3, 0)), ((2, 0), (1, 1)), ((3, 1), (2, 1)))


def hop_blk(value, dz, dy, dc):
    route = []
    for i in range(16):
        z, y, c = i // 4, (i // 2) % 2, i % 2
        route.append((i, ((z + dz) % 4) * 4 + (y ^ dy) * 2 + (c ^ dc)))
    return lax.ppermute(value, "blk", route)


def hop_grp(value, dx, dy):
    return lax.ppermute(value, "grp", [(i, ((i // 2 + dx) % 4) * 2 + ((i % 2) ^ dy)) for i in range(8)])


def dot_f32(a, b, dims):
    return lax.dot_general(a, b, (dims, ((), ())), preferred_element_type=F32)


def columns_of(rows):
    pad = jnp.zeros((120, rows.shape[1]), F32)
    return jnp.transpose(jnp.concatenate([rows, pad], axis=0))


def score_kernel(place, src, t0, t1, t2, t3, *refs):
    e_out, stat_out, tgt_ref, a_ref = refs[-4:]
    rows = t0.shape[0]
    half = 2 * rows
    step = pl.program_id(0)

    @pl.when(step == 0)
    def _():
        top = jnp.zeros((1, 1), F32)
        for q, t in enumerate((t0, t1, t2, t3)):
            block = t[...]
            tgt_ref[q * rows : (q + 1) * rows, :] = block
            top = jnp.maximum(top, jnp.max(jnp.abs(block).astype(F32), keepdims=True))
        a_ref[...] = jnp.broadcast_to(top, a_ref.shape)

    tgt = tgt_ref[...]
    lane = lax.broadcasted_iota(jnp.int32, (PART, 128), 1)
    column = lax.broadcasted_iota(jnp.int32, (PART, 2 * half), 1)
    line = lax.broadcasted_iota(jnp.int32, (PART, 1), 0)
    parts = []
    for first in range(0, src.shape[0], PART):
        ats = []
        for sub in range(2):
            k = step * (src.shape[0] // rows) + first // rows + sub
            at = jnp.int32(-(1 << 20))
            for q in range(4):
                at = jnp.where(place[q] == k, (q - sub) * rows, at)
            ats.append(at)
        hole = line + jnp.where(line < rows, ats[0], ats[1])
        here = pl.ds(first, PART)
        s = dot_f32(src[here, :], tgt, ((1,), (1,)))
        s = jnp.where(column == hole, NEG, s)
        top = jnp.max(s, axis=1, keepdims=True)
        e = jnp.exp(s - top)
        total = jnp.sum(e, axis=1, keepdims=True)
        e_out[0, here, :] = e.astype(BF)
        parts.append(jnp.where(lane == 0, top, jnp.where(lane == 1, total, a_ref[0:1, :])))
    stat_out[...] = jnp.transpose(jnp.concatenate(parts, axis=0))[0:8, :]


def score_call(place, src, blocks, n, so_far):
    rows, width = blocks[0].shape
    total = src.shape[0]
    cols = 4 * rows
    so_far = list(so_far)
    whole = pl.BlockSpec((rows, width), lambda i, p: (0, 0))
    return pl.pallas_call(
        score_kernel,
        out_shape=(
            pltpu.HBM((4, total, cols), BF),
            jax.ShapeDtypeStruct((8, total), F32),
        ),
        grid_spec=pltpu.PrefetchScalarGridSpec(
            num_scalar_prefetch=1,
            grid=(total // TILE,),
            in_specs=[pl.BlockSpec((TILE, width), lambda i, p: (i, 0))]
            + [whole] * 4
            + [pl.BlockSpec(memory_space=pl.ANY)] * len(so_far),
            out_specs=(
                pl.BlockSpec((1, TILE, cols), lambda i, p: (n, i, 0)),
                pl.BlockSpec((8, TILE), lambda i, p: (0, i)),
            ),
            scratch_shapes=[pltpu.VMEM((cols, width), BF), pltpu.VMEM((8, 128), F32)],
        ),
        input_output_aliases={6: 0} if so_far else {},
        compiler_params=pltpu.CompilerParams(vmem_limit_bytes=24 << 20),
        cost_estimate=pl.CostEstimate(
            flops=2 * total * cols * width, bytes_accessed=total * (width + cols) * 2, transcendentals=total * cols
        ),
        name="scores",
    )(place, src, *blocks, *so_far)


def source_kernel(w_ref, e_ref, *refs):
    blocks, out, tgt = refs[:-2], refs[-2], refs[-1]
    rows = blocks[0].shape[0]

    @pl.when(pl.program_id(0) == 0)
    def _():
        for n, block in enumerate(blocks):
            tgt[n // 4, n % 4 * rows : (n % 4 + 1) * rows, :] = block[...]

    weights = columns_of(w_ref[...])
    total = None
    for c in range(4):
        part = dot_f32(e_ref[c], tgt[c], ((1,), (0,))) * weights[:, c : c + 1]
        total = part if total is None else total + part
    out[...] = total.astype(BF)


def source_call(weights, e_all, blocks):
    _, total, cols = e_all.shape
    rows, width = blocks[0].shape
    whole = pl.BlockSpec((rows, width), lambda i: (0, 0), pipeline_mode=pl.Buffered(1))
    return pl.pallas_call(
        source_kernel,
        out_shape=jax.ShapeDtypeStruct((total, width), BF),
        grid=(total // PART,),
        in_specs=[
            pl.BlockSpec((8, PART), lambda i: (0, i)),
            pl.BlockSpec((4, PART, cols), lambda i: (0, i, 0)),
        ]
        + [whole] * len(blocks),
        out_specs=pl.BlockSpec((PART, width), lambda i: (i, 0)),
        scratch_shapes=[pltpu.VMEM((4, cols, width), BF)],
        cost_estimate=pl.CostEstimate(
            flops=8 * total * cols * width, bytes_accessed=total * (8 * cols + 2 * width), transcendentals=0
        ),
        name="source_terms",
    )(weights, e_all, *blocks)


def target_kernel(place, w_ref, e_ref, src_ref, _, keep, give, acc, scaled, column):
    rows = acc.shape[0] // 4
    total = src_ref.shape[0]
    chunk = pl.program_id(0)

    @pl.when(chunk == 0)
    def _():
        for first in range(0, total, PART):
            here = slice(first, first + PART)
            column[here, :] = columns_of(w_ref[:, here])

    lane = lax.broadcasted_iota(jnp.int32, (PART, 128), 1)
    for first in range(0, total, PART):
        here = slice(first, first + PART)
        weight = jnp.sum(jnp.where(lane == chunk, column[here, :], 0.0), axis=1, keepdims=True)
        scaled[here, :] = (src_ref[here, :].astype(F32) * weight).astype(BF)
    acc[...] = dot_f32(e_ref[0], scaled[...], ((0,), (0,)))
    for q in range(4):
        at = place[chunk * 4 + q]

        @pl.when(at >= 0)
        def _():
            there = slice(q * rows, (q + 1) * rows)
            here = pl.ds(pl.multiple_of(at * rows, rows), rows)
            acc[there, :] = acc[there, :] + column[here, 4:5] * src_ref[here, :].astype(F32)

    keep[0] = acc[0 : 2 * rows, :]
    give[0] = acc[2 * rows : 4 * rows, :].astype(BF)


def target_call(place, weights, e_all, src, after):
    _, total, cols = e_all.shape
    width = src.shape[1]
    half = (4, cols // 2, width)
    half_spec = pl.BlockSpec((1, cols // 2, width), lambda i, p: (i, 0, 0))
    return pl.pallas_call(
        target_kernel,
        out_shape=(jax.ShapeDtypeStruct(half, F32), jax.ShapeDtypeStruct(half, BF)),
        grid_spec=pltpu.PrefetchScalarGridSpec(
            num_scalar_prefetch=1,
            grid=(4,),
            in_specs=[
                pl.BlockSpec((8, total), lambda i, p: (0, 0)),
                pl.BlockSpec((1, total, cols), lambda i, p: (i, 0, 0)),
                pl.BlockSpec((total, width), lambda i, p: (0, 0)),
                pl.BlockSpec(memory_space=pl.ANY),
            ],
            out_specs=(half_spec, half_spec),
            scratch_shapes=[
                pltpu.VMEM((cols, width), F32),
                pltpu.VMEM((total, width), BF),
                pltpu.VMEM((total, 128), F32),
            ],
        ),
        cost_estimate=pl.CostEstimate(
            flops=8 * total * cols * width, bytes_accessed=total * (width + 4 * cols) * 2 + cols * width * 12, transcendentals=0
        ),
        name="target_terms",
    )(place, weights, e_all, src, after)


def code_kernel(parts, hard, tgt, col, _, out, high):
    total = hard[...] * col[:, 0:1] + tgt[...].astype(F32) * col[:, 1:2]
    for g in range(parts.shape[0]):
        total = total + parts[g].astype(F32) * col[:, 3 + g : 4 + g]
    scaled = jnp.clip(total * col[:, 2:3], -32767.0, 32767.0)
    coded = jnp.round(scaled).astype(jnp.int32).astype(jnp.int16)
    out[...] = coded
    high[...] = coded


def line_kernel(keep, got, m1, m2, m3, mine, other):
    rows = mine.shape[0]
    total = keep[0] + got[0].astype(F32)
    for part in (m1, m2, m3):
        total = total + part[...].astype(F32)
    mine[...] = total[:rows, :]
    other[...] = total[rows:, :].astype(BF)


def decode_kernel(order, scale, own, side, far1, far2, far3, pairs1, pairs2, pairs3, far_side, out):
    step = pl.program_id(0)
    half = own.shape[0] // 2
    far, pairs = (None, far1, far2, far3), (None, pairs1, pairs2, pairs3)
    for dx in range(4):
        for dy in range(2):

            @pl.when(step == dx * 2 + dy)
            def _():
                if dx == 0:
                    whole = (own if dy == 0 else side)[...]
                    out[...] = whole.astype(jnp.int32).astype(F32) * scale[...]
                else:
                    low = pairs[dx][dy]
                    high = far[dx][...] if dy == 0 else far_side[dx - 1]
                    out[0:half, :] = low.astype(jnp.int32).astype(F32) * scale[0:half, :]
                    out[half:, :] = high.astype(jnp.int32).astype(F32) * scale[half:, :]


def decode_call(order, scale, pieces):
    rows, width = pieces[0].shape
    total = scale.shape[0]
    return pl.pallas_call(
        decode_kernel,
        out_shape=jax.ShapeDtypeStruct((total, width), F32),
        grid_spec=pltpu.PrefetchScalarGridSpec(
            num_scalar_prefetch=1,
            grid=(total // rows,),
            in_specs=[pl.BlockSpec((rows, 1), lambda i, p: (p[i], 0))]
            + [pl.BlockSpec(x.shape, lambda i, p, n=x.ndim: (0,) * n) for x in pieces],
            out_specs=pl.BlockSpec((rows, width), lambda i, p: (p[i], 0)),
        ),
        compiler_params=pltpu.CompilerParams(vmem_limit_bytes=24 << 20),
        cost_estimate=pl.CostEstimate(flops=total * width, bytes_accessed=total * width * 6, transcendentals=0),
        name="decode",
    )(order, scale, *pieces)


def shards(source_emb, target_emb, hard_pool, hard_index, language, margin):
    total, width = source_emb.shape
    rows = target_emb.shape[0]
    blk, grp = lax.axis_index("blk"), lax.axis_index("grp")
    owners = 128
    cap = max(2, (2 * rows + owners - 1) // owners)
    slots = owners * cap
    z, y, c = blk // 4, (blk // 2) % 2, blk % 2

    start = grp * rows
    own_index = lax.dynamic_slice_in_dim(hard_index, start, rows, 0)
    own_source = lax.dynamic_slice_in_dim(source_emb, start, rows, 0)
    owner, pool_row = own_index // rows, own_index % rows
    position = jnp.arange(rows, dtype=jnp.int32)
    same = (owner[:, None] == owner[None, :]) & (position[None, :] < position[:, None])
    slot = owner * cap + jnp.sum(same.astype(jnp.int32), axis=1)
    at_slot = slot[:, None] == jnp.arange(slots, dtype=jnp.int32)[None, :]
    requests = jnp.sum(jnp.where(at_slot, pool_row[:, None] + 1, 0), axis=0) - 1
    wanted = lax.all_to_all(requests.reshape(owners, cap), ("grp", "blk"), 0, 0, tiled=True)
    lang_match = language[:, None] == jnp.arange(margin.shape[0], dtype=jnp.int32)[None, :]
    margin_row = jnp.sum(jnp.where(lang_match, margin[None, :], 0.0), axis=1)

    have = {(0, 0, 0): target_emb}
    have[0, 1, 0] = hop_blk(target_emb, 0, 1, 0)
    for dz in (1, 3, 2):
        have[dz, 0, 0] = hop_blk(target_emb, -dz, 0, 0)
    for dz in (1, 3, 2):
        have[dz, 1, 0] = hop_blk(have[0, 1, 0], -dz, 0, 0)
    for dz, dy in [pair for chunk in CHUNKS for pair in chunk]:
        have[dz, dy, 1] = hop_blk(have[dz, dy, 0], 0, 0, 1)

    holds = grp == blk // 2
    place = {}
    for dz in range(4):
        for dy in range(2):
            for dc in range(2):
                zz = (z + dz) % 4
                k = (zz % 2) * 4 + (y ^ dy) * 2 + (c ^ dc)
                place[dz, dy, dc] = jnp.where(holds & (zz // 2 == c), k, -1)
    order = [[(dz, dy, dc) for dc in (0, 1) for dz, dy in chunk] for chunk in CHUNKS]
    places = [jnp.stack([place[key] for key in chunk]) for chunk in order]
    flat = jnp.concatenate(places)

    stats, so_far = [], ()

    def add_chunk(n):
        nonlocal so_far
        e, stat = score_call(places[n], source_emb, [have[key] for key in order[n]], n, so_far)
        so_far = (e,)
        stats.append(stat)

    add_chunk(0)
    wanted, stats[0] = lax.optimization_barrier((wanted, stats[0]))
    serve = (wanted.reshape(slots)[:, None] == position[None, :]).astype(BF)
    served = dot_f32(serve, hard_pool, ((1,), (0,))).astype(BF).reshape(owners, cap, width)
    served, places[1] = lax.optimization_barrier((served, places[1]))
    fetched = lax.all_to_all(served, ("grp", "blk"), 0, 0, tiled=True).reshape(slots, width)
    add_chunk(1)
    early_target, stats[1] = lax.optimization_barrier((target_emb, stats[1]))
    own_target = lax.ppermute(
        early_target, ("grp", "blk"), [(16 * i + j, (j % 8) * 16 + 2 * i + j // 8) for i in range(8) for j in range(16)]
    )
    add_chunk(2)
    fetched, stats[2] = lax.optimization_barrier((fetched, stats[2]))
    pick = at_slot.astype(BF)
    hard_rows = dot_f32(pick, fetched, ((1,), (0,)))
    hard_score = jnp.sum(own_source.astype(F32) * hard_rows, axis=1)
    add_chunk(3)

    tops = jnp.stack([stat[0] for stat in stats])
    sums = jnp.stack([stat[1] for stat in stats])
    reach = jnp.maximum(jnp.max(jnp.stack([stat[2] for stat in stats]), axis=0), jnp.max(jnp.abs(hard_rows)))
    own_margin = lax.dynamic_slice_in_dim(margin_row, start, rows, 0)
    own_pos = jnp.sum(own_source.astype(F32) * own_target.astype(F32), axis=1) - own_margin
    pos = lax.dynamic_update_slice_in_dim(jnp.zeros((total,), F32), own_pos, start, 0)
    hard_all = lax.dynamic_update_slice_in_dim(jnp.full((total,), LOW, F32), hard_score, start, 0)
    soft_top = jnp.max(tops, axis=0)
    soft = jnp.sum(sums * jnp.exp(tops - soft_top), axis=0)
    mine = jnp.stack([soft_top, soft, pos, hard_all, reach] + [jnp.zeros((total,), F32)] * 3)
    everyone = lax.all_to_all(jnp.broadcast_to(mine[None], (8, 8, total)), "grp", 0, 0, tiled=True)
    source_part = source_call(jnp.concatenate([jnp.exp(tops - soft_top), jnp.zeros((4, total), F32)]), so_far[0],
        [have[key] for chunk in order for key in chunk])
    everyone, source_part = lax.optimization_barrier((everyone, source_part))
    source_parts = lax.all_to_all(source_part.reshape(8, rows, width), "grp", 0, 0, tiled=True)
    token = hop_blk(source_part[:16, :128], 0, 0, 1)
    pos = jnp.sum(everyone[:, 2], axis=0)
    hard_all = jnp.max(everyone[:, 3], axis=0)
    reach = jnp.max(everyone[:, 4], axis=0)
    top = jnp.maximum(jnp.max(everyone[:, 0], axis=0), jnp.maximum(pos, hard_all))
    off = jnp.sum(everyone[:, 1] * jnp.exp(everyone[:, 0] - top), axis=0) + jnp.exp(hard_all - top)
    log_total = top + jnp.log(off + jnp.exp(pos - top))
    row_loss = log_total - pos
    less = jnp.exp(pos - log_total) - 1.0
    diag_weight = jnp.where(holds, less, 0.0)

    x_at, y_at = grp // 2, grp % 2
    mass = jnp.abs(less) + off * jnp.exp(top - log_total)
    bound = jnp.maximum(1.01 * reach * mass, 1e-30)
    col = jnp.concatenate(
        [jnp.stack([jnp.exp(hard_all - log_total), less, 32767.0 / bound]), jnp.exp(everyone[:, 0] - log_total[None])]
    )
    col = lax.dynamic_slice_in_dim(col, start, rows, 1)
    hard_prob = col[0]
    col = jnp.transpose(col)
    half = rows // 2

    weights = jnp.concatenate([jnp.exp(tops - log_total), diag_weight[None], jnp.zeros((3, total), F32)])
    keep, give = target_call(flat, weights, so_far[0], source_emb, token)
    got = hop_blk(give, 0, 0, 1)
    where_at = {pair: (n, j) for n, chunk in enumerate(CHUNKS) for j, pair in enumerate(chunk)}

    def both(dz, dy):
        n, j = where_at[dz, dy]
        here = slice(j * rows, (j + 1) * rows)
        return (keep[n, here] + got[n, here].astype(F32)).astype(BF)

    moved = [hop_blk(jnp.concatenate([both(dz, 0), both(dz, 1)]), dz, 0, 0) for dz in (1, 3, 2)]
    whole = [pl.BlockSpec((1, 2 * rows, width), lambda i: (0, 0, 0))] * 2
    whole += [pl.BlockSpec((2 * rows, width), lambda i: (0, 0))] * 3
    mine, other = pl.pallas_call(
        line_kernel,
        out_shape=(jax.ShapeDtypeStruct((rows, width), F32), jax.ShapeDtypeStruct((rows, width), BF)),
        grid=(1,),
        in_specs=whole,
        out_specs=[pl.BlockSpec((rows, width), lambda i: (0, 0))] * 2,
        cost_estimate=pl.CostEstimate(flops=10 * rows * width, bytes_accessed=30 * rows * width, transcendentals=0),
        name="lines",
    )(keep, got, *moved)
    target_grad = mine + hop_blk(other, 0, 1, 0).astype(F32)

    coded, coded_high = pl.pallas_call(
        code_kernel,
        out_shape=(jax.ShapeDtypeStruct((rows, width), jnp.int16), jax.ShapeDtypeStruct((half, width), jnp.int16)),
        grid=(2,),
        in_specs=[
            pl.BlockSpec((8, half, width), lambda i: (0, i, 0)),
            pl.BlockSpec((half, width), lambda i: (i, 0)),
            pl.BlockSpec((half, width), lambda i: (i, 0)),
            pl.BlockSpec((half, col.shape[1]), lambda i: (i, 0)),
            pl.BlockSpec(memory_space=pl.ANY),
        ],
        out_specs=(pl.BlockSpec((half, width), lambda i: (i, 0)), pl.BlockSpec((half, width), lambda i: (0, 0))),
        cost_estimate=pl.CostEstimate(flops=10 * rows * width, bytes_accessed=22 * rows * width, transcendentals=0),
        name="code",
    )(source_parts, hard_rows, own_target, col, other)
    contribution = (hard_prob[:, None] * own_source.astype(F32)).astype(BF)
    outgoing = dot_f32(pick, contribution, ((0,), (0,))).astype(BF).reshape(owners, cap, width)
    outgoing, coded, coded_high = lax.optimization_barrier((outgoing, coded, coded_high))
    side = hop_grp(coded, 0, 1)
    far = [hop_grp(coded_high, -dx, 0) for dx in (1, 2, 3)]
    low = jnp.stack([coded[:half], side[:half]])
    pairs = [hop_grp(low, -dx, 0) for dx in (1, 2, 3)]
    far_side = hop_grp(jnp.stack(far), 0, 1)
    blocks = jnp.stack([((x_at + dx) % 4) * 2 + (y_at ^ dy) for dx in range(4) for dy in range(2)])
    source_grad = decode_call(
        blocks, (bound * (1.0 / 32767.0))[:, None], [coded, side, *far, *pairs, far_side]
    )

    incoming = lax.all_to_all(outgoing, ("grp", "blk"), 0, 0, tiled=True)
    incoming, source_grad = lax.optimization_barrier((incoming, source_grad))
    pool_grad = dot_f32(serve, incoming.reshape(slots, width), ((0,), (0,)))
    return (row_loss, source_grad, target_grad, pool_grad)


def solution(mesh):
    in_specs = (P("blk", None), P(("grp", "blk"), None), P(("grp", "blk"), None), P("blk"), P("blk"), P())
    out_specs = (P("blk"), P("blk", None), P(("grp", "blk"), None), P(("grp", "blk"), None))
    return jax.shard_map(shards, mesh=mesh, in_specs=in_specs, out_specs=out_specs, check_vma=False)
```
